32 devices in a mesh: ctx: 8 (over y, x, core), fsdp: 4 (over z).
Axes of the slice: x: 2, y: 2, z: 4, core: 2. Of those that a mesh axis runs over, the one named last changes fastest.
Arguments:
- loaded: bfloat16 [8, 8, 128, 4096], P('ctx', None, None, 'fsdp'), may hold values from -6 to 6
- slot_pos: int32 [8, 8, 128], P('ctx'), may hold values from -1 to 255, as said below
- contig_lengths: int32 [16], replicated, may hold values from 1 to 1024, 2048 in all
- w_in: bfloat16 [4096, 3, 4096], P('ctx', None, 'fsdp'), may hold values from -0.09375 to 0.09375
- short_taps: float32 [3, 7, 4096], P(None, None, 'fsdp'), may hold values from -2 to 2
- long_taps: float32 [128, 4096], P(None, 'fsdp'), may hold values from -0.5 to 0.5
- grad_out: bfloat16 [2048, 4096], P('ctx', 'fsdp'), may hold values from -0.59765625 to 0.59765625
Outputs:
- gated_out: bfloat16 [2048, 4096], P('ctx', 'fsdp')
- token_grads: bfloat16 [2048, 4096], P('ctx', 'fsdp')
- weight_grads: bfloat16 [4096, 3, 4096], P('ctx', None, 'fsdp')
- short_grads: float32 [3, 7, 4096], P(None, None, 'fsdp')
- long_grads: float32 [128, 4096], P(None, 'fsdp')
The draws below stay inside these ranges and needn't reach their ends.
Inputs may be any that keep to these rules, and one draw needn't show every extreme that they name: `slot_pos`: for each destination e, the slots with a value of 0 or more name every row 0 to 255 of e's block exactly once; -1 marks an empty slot; for each destination some loader fills all 128 of its slots. `contig_lengths`: the lengths sum to 2048.
All inputs are finite; a program needn't handle non-finite values.
Results may differ from the reference program's by a relative error of at most 0.012.
Values may be sent and summed in bfloat16 or wider, within the bound.
A program may use at most 192 MiB of HBM per device.

```python
import math
import jax
import jax.numpy as jnp
import numpy as np
from jax import lax

D = 4096
HC = 4096
SHORT = 7
LONG = 128
TOK_DEV = 256
TOKENS = 2048
SLOT = 128
NCONTIG = 16
N_CTX = 8


def draw_slot_pos(key, part):
    groups = TOK_DEV // 8
    seats = SLOT // 8
    seat_total = N_CTX * seats
    dest_keys = jax.random.split(jax.random.fold_in(key, 11), N_CTX)

    def one_dest(dest_key):
        heavy_key, order_key, place_key = jax.random.split(dest_key, 3)
        heavy = jax.random.randint(heavy_key, (), 0, N_CTX)
        ranks = jax.random.permutation(order_key, seat_total).astype(jnp.int32)
        seat_ids = jnp.arange(seat_total, dtype=jnp.int32)
        owners = seat_ids // seats
        scores = jnp.where(owners == heavy, 0, seat_total) + ranks
        chosen = jnp.argsort(scores, stable=True)[:groups]
        placed = jax.random.permutation(place_key, groups).astype(jnp.int32)
        values = placed[:, None] * 8 + jnp.arange(8, dtype=jnp.int32)[None, :]
        table = jnp.full((seat_total, 8), -1, jnp.int32).at[chosen].set(values)
        return table.reshape(N_CTX, SLOT)
    return jax.vmap(one_dest)(dest_keys).astype(jnp.int32)


def steps_of(key, dims, cuts, least, high):
    loudness = 1.0
    for position, shards_of in cuts:
        heights = jax.random.uniform(jax.random.fold_in(jax.random.fold_in(key, 6), position), (shards_of,), jnp.float32, least / len(cuts), high / len(cuts))
        loudness = loudness * jnp.repeat(jnp.exp(heights), dims[position] // shards_of).reshape((-1,) + (1,) * (len(dims) - 1 - position))
    return loudness


def length_profile(count, total, bound, lean):
    weights = [(1 << 20) // math.isqrt(grade ** lean) + 1 for grade in range(2, count + 1)]
    surplus, counts = total - bound - (count - 1), [1] * (count - 1)
    while surplus > 0:
        free = [i for i in range(count - 1) if counts[i] < bound]
        mass, budget = sum([weights[i] for i in free]), surplus
        for i in free:
            extra = min(bound - counts[i], max(1, budget * weights[i] // mass), surplus)
            counts[i] = counts[i] + extra
            surplus = surplus - extra
    return np.array([bound] + counts)


def uneven(own_key, number_of, total, limit, lean):
    if number_of == 2:
        one = jax.random.randint(own_key, (), max(1, total - limit), min(limit, total - 1) + 1)
        return jnp.stack([one, total - one])
    lengths = jnp.asarray(length_profile(number_of, total, limit, lean), jnp.int32)
    pairs = (number_of - 1) // 2
    source_of, receiver = lengths[1:1 + 2 * pairs:2], lengths[2:2 + 2 * pairs:2]
    room = jnp.minimum(source_of - 1, limit - receiver)
    passed = jax.random.randint(jax.random.fold_in(own_key, 1), (pairs,), 0, 1 << 20) % (room + 1)
    lengths = lengths.at[1:1 + 2 * pairs:2].set(source_of - passed).at[2:2 + 2 * pairs:2].set(receiver + passed)
    return lengths[jax.random.permutation(jax.random.fold_in(own_key, 2), number_of)]


def normal_values(stream_key, shape, scale, limit, cuts=(), kind=jnp.bfloat16):
    level = steps_of(stream_key, shape, cuts, -0.22, 0.18) if cuts else 1.0
    result = jax.random.normal(stream_key, shape, jnp.float32) * scale * level
    return jnp.minimum(jnp.maximum(result, -limit), limit).astype(kind)


def setup_inputs(seed: int = 0) -> dict:
    keys = jax.random.split(jax.random.key(seed), 8)
    loaded = normal_values(keys[0], (N_CTX, N_CTX, SLOT, D), 1.0, 6.0, ((0, 8), (3, 4)))
    slot_pos = draw_slot_pos(jax.random.fold_in(keys[7], 71), 0)
    contig_lengths = uneven(keys[2], NCONTIG, TOKENS, 4 * TOK_DEV, 2).astype(jnp.int32)
    w_in = normal_values(keys[3], (D, 3, HC), D ** -0.5, 0.09375, ((0, 8), (2, 4)))
    short_taps = normal_values(keys[4], (3, SHORT, HC), SHORT ** -0.5, 2.0, ((2, 4),), jnp.float32)
    long_taps = normal_values(keys[5], (LONG, HC), LONG ** -0.5, 0.5, ((1, 4),), jnp.float32)
    grad_out = normal_values(keys[6], (TOKENS, HC), 0.1, 0.59765625, ((0, 8), (1, 4)))
    return {"loaded": loaded, "slot_pos": slot_pos, "contig_lengths": contig_lengths, "w_in": w_in, "short_taps": short_taps, "long_taps": long_taps, "grad_out": grad_out}


def starts_of(positions, contig_lengths):
    ends = jnp.cumsum(contig_lengths, dtype=jnp.int32)
    begins = ends - contig_lengths
    chosen = jnp.where(begins[None, :] <= positions[:, None], begins[None, :], 0)
    return jnp.max(chosen, axis=1).astype(jnp.int32)


def lead_filter(ext, taps, positions, begins_here):
    width = taps.shape[0]
    count = ext.shape[0] - width + 1
    bcast_shape = (count,) + (1,) * (ext.ndim - 1)
    total = jnp.zeros((count,) + ext.shape[1:], jnp.float32)
    for tap_index in range(width):
        keep_mask = (positions - tap_index >= begins_here).astype(jnp.float32).reshape(bcast_shape)
        first = width - 1 - tap_index
        total = total + taps[tap_index] * ext[first:first + count] * keep_mask
    return total


def trail_filter(ext, taps, positions, begins_ext):
    width = taps.shape[0]
    count = ext.shape[0] - width + 1
    bcast_shape = (count,) + (1,) * (ext.ndim - 1)
    total = jnp.zeros((count,) + ext.shape[1:], jnp.float32)
    for tap_index in range(width):
        keep_mask = (positions >= begins_ext[tap_index:tap_index + count]).astype(jnp.float32).reshape(bcast_shape)
        total = total + taps[tap_index] * ext[tap_index:tap_index + count] * keep_mask
    return total


def tap_sums(grads, ext, width, lead_count, positions, begins_here):
    count = grads.shape[0]
    bcast_shape = (count,) + (1,) * (grads.ndim - 1)
    pieces = []
    for tap_index in range(width):
        keep_mask = (positions - tap_index >= begins_here).astype(jnp.float32).reshape(bcast_shape)
        first = lead_count - tap_index
        pieces.append(jnp.sum(grads * ext[first:first + count] * keep_mask, axis=0))
    return jnp.stack(pieces, 0)


def reference(loaded, slot_pos, contig_lengths, w_in, short_taps, long_taps, grad_out):
    by_dest = jnp.transpose(loaded, (1, 0, 2, 3)).reshape(N_CTX * N_CTX * SLOT, D)
    bases = (jnp.arange(N_CTX, dtype=jnp.int32) * TOK_DEV)[:, None, None]
    targets = jnp.where(slot_pos >= 0, slot_pos + bases, TOKENS).reshape(-1).astype(jnp.int32)
    tokens = jnp.zeros((TOKENS, D), jnp.bfloat16).at[targets].set(by_dest, mode="drop")
    positions = jnp.arange(TOKENS, dtype=jnp.int32)
    begins_here = starts_of(positions, contig_lengths)
    long_begins = starts_of(jnp.arange(TOKENS + LONG - 1, dtype=jnp.int32), contig_lengths)
    short_begins = starts_of(jnp.arange(TOKENS + SHORT - 1, dtype=jnp.int32), contig_lengths)
    block_width = math.gcd(HC, 512)
    block_count = HC // block_width

    def channel_block(token_acc, block_index):
        start_col = (block_index * block_width).astype(jnp.int32)
        w_block = lax.dynamic_slice_in_dim(w_in, start_col, block_width, 2)
        flat_w = w_block.reshape(D, 3 * block_width)
        short_block = lax.dynamic_slice_in_dim(short_taps, start_col, block_width, 2)
        long_block = lax.dynamic_slice_in_dim(long_taps, start_col, block_width, 1)
        grad_block = lax.dynamic_slice_in_dim(grad_out, start_col, block_width, 1)
        streams = jnp.dot(tokens, flat_w, preferred_element_type=jnp.float32).reshape(TOKENS, 3, block_width)
        mixed_half = streams.astype(jnp.bfloat16)
        short_lags = jnp.transpose(short_block, (1, 0, 2))
        lead_mixed = jnp.concatenate([jnp.zeros((SHORT - 1, 3, block_width), jnp.bfloat16), mixed_half], 0).astype(jnp.float32)
        filtered = lead_filter(lead_mixed, short_lags, positions, begins_here)
        product = (filtered[:, 1] * filtered[:, 2]).astype(jnp.bfloat16)
        lead_product = jnp.concatenate([jnp.zeros((LONG - 1, block_width), jnp.bfloat16), product], 0).astype(jnp.float32)
        carried = lead_filter(lead_product, long_block, positions, begins_here)
        gated_block = (filtered[:, 0] * carried).astype(jnp.bfloat16)
        upstream = grad_block.astype(jnp.float32)
        back_prod = (upstream * filtered[:, 0]).astype(jnp.bfloat16)
        first_grad = upstream * carried
        trail_prod = jnp.concatenate([back_prod, jnp.zeros((LONG - 1, block_width), jnp.bfloat16)], 0).astype(jnp.float32)
        grad_product = trail_filter(trail_prod, long_block, positions, long_begins)
        grad_filtered = jnp.stack([first_grad, grad_product * filtered[:, 2], grad_product * filtered[:, 1]], 1).astype(jnp.bfloat16)
        trail_grad = jnp.concatenate([grad_filtered, jnp.zeros((SHORT - 1, 3, block_width), jnp.bfloat16)], 0).astype(jnp.float32)
        grad_mixed = trail_filter(trail_grad, short_lags, positions, short_begins).astype(jnp.bfloat16)
        flat_grad = grad_mixed.reshape(TOKENS, 3 * block_width)
        token_acc = token_acc + jnp.dot(flat_grad, flat_w.T, preferred_element_type=jnp.float32)

        def row_term(accum, row_block):
            start_row = (row_block * TOK_DEV).astype(jnp.int32)
            feature_rows = lax.dynamic_slice_in_dim(tokens, start_row, TOK_DEV, 0)
            grad_rows = lax.dynamic_slice_in_dim(flat_grad, start_row, TOK_DEV, 0)
            term = jnp.dot(feature_rows.T, grad_rows, preferred_element_type=jnp.float32).astype(jnp.bfloat16)
            return accum + lax.optimization_barrier(term).astype(jnp.float32), None

        summed, _ = lax.scan(row_term, jnp.zeros((D, 3 * block_width), jnp.float32), jnp.arange(N_CTX, dtype=jnp.int32))
        weight_block = summed.astype(jnp.bfloat16).reshape(D, 3, block_width)
        long_block_grads = tap_sums(back_prod.astype(jnp.float32), lead_product, LONG, LONG - 1, positions, begins_here)
        short_lag_grads = tap_sums(grad_filtered.astype(jnp.float32), lead_mixed, SHORT, SHORT - 1, positions, begins_here)
        short_block_grads = jnp.transpose(short_lag_grads, (1, 0, 2))
        return token_acc, (gated_block, weight_block, short_block_grads, long_block_grads)

    token_sum, outs = lax.scan(channel_block, jnp.zeros((TOKENS, D), jnp.float32), jnp.arange(block_count, dtype=jnp.int32))
    gated_blocks, weight_blocks, short_blocks, long_blocks = outs
    gated_out = jnp.transpose(gated_blocks, (1, 0, 2)).reshape(TOKENS, HC)
    weight_grads = jnp.transpose(weight_blocks, (1, 2, 0, 3)).reshape(D, 3, HC)
    short_grads = jnp.transpose(short_blocks, (1, 2, 0, 3)).reshape(3, SHORT, HC)
    long_grads = jnp.transpose(long_blocks, (1, 0, 2)).reshape(LONG, HC)
    token_grads = token_sum.astype(jnp.bfloat16)
    return gated_out, token_grads, weight_grads, short_grads, long_grads
```

```python
import jax
import jax.numpy as jnp
from jax import lax
from jax.experimental import pallas as pl
from jax.experimental.pallas import tpu as pltpu
from jax.sharding import PartitionSpec as P

LANES = 128
F32, BF16 = jnp.float32, jnp.bfloat16


def round_up(x, to):
    return -(-x // to) * to


def swapped(x, mask):
    size = lax.axis_size("ctx")
    return lax.ppermute(x, "ctx", [(i, i ^ mask) for i in range(size)])


def neighbour_rows(x, by):
    size = lax.axis_size("ctx")
    pairs = [(i, i + 2 * by) for i in range(size) if 0 <= i + 2 * by < size]
    return lax.ppermute(x, "ctx", pairs)


def chip_masks(size):
    masks, step = [], 2
    while step < size:
        masks.append(step)
        step *= 2
    return masks


def walk(masks):
    held = [0]
    for mask in masks:
        held = held + [k ^ mask for k in held]
    return held


def by_core(own, other, dim):
    core = lax.axis_index("ctx") % 2
    low = jnp.where(core == 0, own, other)
    high = jnp.where(core == 0, other, own)
    return jnp.concatenate([low, high], dim)


def half(x, dim, which):
    width = x.shape[dim] // 2
    return lax.dynamic_slice_in_dim(x, which * width, width, dim)


def remote(src, dst, send, recv, **place):
    return pltpu.make_async_remote_copy(
        src_ref=src, dst_ref=dst, send_sem=send, recv_sem=recv,
        device_id=place, device_id_type=pl.DeviceIdType.MESH,
    )


def local(src, dst, sem):
    return pltpu.make_async_copy(src, dst, sem)


def at_cols(start, size):
    return pl.ds(pl.multiple_of(start, LANES), size)


def greet(n_ctx, n_line):
    me, z = lax.axis_index("ctx"), lax.axis_index("fsdp")
    barrier = pltpu.get_barrier_semaphore()
    others = [1] + [k for k in range(2, n_ctx, 2)]
    for k in others:
        pl.semaphore_signal(
            barrier, inc=1, device_id={"ctx": me ^ k}, device_id_type=pl.DeviceIdType.MESH
        )

    @pl.when(z > 0)
    def _():
        pl.semaphore_signal(
            barrier, inc=1, device_id={"fsdp": z - 1}, device_id_type=pl.DeviceIdType.MESH
        )

    @pl.when(z < n_line - 1)
    def _():
        pl.semaphore_signal(
            barrier, inc=1, device_id={"fsdp": z + 1}, device_id_type=pl.DeviceIdType.MESH
        )

    ends = jnp.where(z > 0, 1, 0) + jnp.where(z < n_line - 1, 1, 0)
    pl.semaphore_wait(barrier, len(others) + ends)


class Spread:
    def __init__(self, buf, send, recv, masks, me):
        self.buf, self.send, self.recv, self.me = buf, send, recv, me
        self.orders = (masks, masks[::-1])
        self.keys = tuple(walk(m) for m in self.orders)
        self.count = 1 << len(masks)

    def copy(self, chain, stage, i):
        to = (1 << stage) + i
        return remote(
            self.buf.at[chain, i], self.buf.at[chain, to],
            self.send.at[chain, to], self.recv.at[chain, to],
            ctx=self.me ^ self.orders[chain][stage],
        )

    def stages(self, i):
        return range(i.bit_length(), len(self.orders[0]))

    def start(self, chain, i, stages=None):
        for stage in self.stages(i) if stages is None else stages:
            self.copy(chain, stage, i).start()

    def arrive(self, chain, i):
        stage = i.bit_length() - 1
        self.copy(chain, stage, i - (1 << stage)).wait_recv()

    def finish(self):
        for chain in (0, 1):
            for i in range(self.count):
                for stage in self.stages(i):
                    self.copy(chain, stage, i).wait_send()


def gather_kernel(
    sizes, w, slots, pos,
    proj, up12, up0, down0, down12, tokens, wall,
    wbuf, xbuf, sbuf, pbuf, part, ppart, acc,
    w_send, w_recv, s_send, s_recv, up_send, up_recv, dn_send, dn_recv,
    core_send, core_recv, misc_send, misc_recv, local_sem, out_sem, halo_send, halo_recv,
):
    n_ctx, n, far, pad = sizes
    me, z = lax.axis_index("ctx"), lax.axis_index("fsdp")
    core, chip = me % 2, me // 2
    chips = n_ctx // 2
    rows, dz = ppart.shape
    streams, feats, ch = wbuf.shape[2:]
    masks = chip_masks(n_ctx)
    greet(n_ctx, n)

    sib = me ^ 1
    own_pos = local(pos.at[0], pbuf.at[core], local_sem.at[0])
    own_pos.start()
    send_pos = remote(pos.at[0], pbuf.at[core], misc_send.at[0], misc_recv.at[0], ctx=sib)
    send_pos.start()
    own_slots = local(slots.at[pl.ds(2 * chip, 2)], sbuf.at[chip], local_sem.at[1])
    own_slots.start()
    deals = []
    for k in range(2, n_ctx, 2):
        to = me ^ k
        deals.append(remote(
            slots.at[pl.ds(to - core, 2)], sbuf.at[chip], s_send.at[k // 2], s_recv.at[k // 2], ctx=to
        ))
        deals[-1].start()
    own_w = local(w.at[:, :, at_cols(core * ch, ch)], wbuf.at[0, 0], local_sem.at[2])
    own_w.start()
    send_w = remote(
        w.at[:, :, at_cols((1 - core) * ch, ch)], wbuf.at[1, 0], misc_send.at[1], misc_recv.at[1], ctx=sib
    )
    send_w.start()
    spread = Spread(wbuf, w_send, w_recv, masks, me)
    stages = len(masks)
    keep = []

    def stored(chain, i):
        keep.append(local(wbuf.at[chain, i], wall.at[chain, i], out_sem.at[chain, i]))
        keep[-1].start()

    own_w.wait()
    spread.start(0, 0, range(0, min(1, stages)))
    stored(0, 0)
    send_w.wait_recv()
    spread.start(1, 0, range(0, min(1, stages)))
    stored(1, 0)

    own_pos.wait()
    send_pos.wait_recv()
    own_slots.wait()
    for deal in deals:
        deal.wait_recv()
    spread.start(0, 0, range(1, stages))
    spread.start(1, 0, range(1, stages))

    seat = lax.broadcasted_iota(jnp.int32, (rows, pos.shape[2]), 0)

    def place(b):
        total = None
        for c in range(chips):
            row = pbuf[b, pl.ds(2 * c + core, 1), :]
            pick = jnp.where(row == seat, 1.0, 0.0).astype(BF16)
            term = jnp.dot(pick, sbuf[c, b], preferred_element_type=F32)
            total = term if total is None else total + term
        return total.astype(BF16)

    part[...] = place(1 - core)
    give = remote(part, ppart, misc_send.at[2], misc_recv.at[2], ctx=sib)
    give.start()
    mine = place(core)
    give.wait_recv()
    own_rows = pl.ds(pl.multiple_of(core * rows, rows), rows)
    xbuf[own_rows, at_cols(z * dz, dz)] = mine + ppart[...]

    def tile(t):
        return xbuf.at[own_rows, at_cols(t * dz, dz)]

    def to_core(t):
        return remote(tile(t), tile(t), core_send.at[t], core_recv.at[t], ctx=sib)

    def other_tile(t):
        there = xbuf.at[pl.ds(pl.multiple_of((1 - core) * rows, rows), rows), at_cols(t * dz, dz)]
        return remote(there, there, core_send.at[t], core_recv.at[t], ctx=sib)

    def up(h, t):
        return remote(tile(t), tile(t), up_send.at[h], up_recv.at[h], fsdp=z + 1)

    def down(h, t):
        return remote(tile(t), tile(t), dn_send.at[h], dn_recv.at[h], fsdp=z - 1)

    to_core(z).start()
    for h in range(1, n):
        @pl.when((z < n - 1) & (z - h + 1 >= 0))
        def _():
            up(h, z - h + 1).start()

        @pl.when((z > 0) & (z + h - 1 <= n - 1))
        def _():
            down(h, z + h - 1).start()

        @pl.when(z - h >= 0)
        def _():
            up(h, z - h).wait_recv()
            to_core(z - h).start()

        @pl.when(z + h <= n - 1)
        def _():
            down(h, z + h).wait_recv()
            to_core(z + h).start()

        if h == 1 and spread.count > 1:
            for chain in (0, 1):
                spread.arrive(chain, 1)
                spread.start(chain, 1)
                stored(chain, 1)
    for t in range(n):
        other_tile(t).wait_recv()
    keep.append(local(xbuf, tokens, local_sem.at[3]))
    keep[-1].start()

    for i in range(spread.count):
        for chain in (0, 1):
            if i > 1:
                spread.arrive(chain, i)
                spread.start(chain, i)
                stored(chain, i)
            block = me ^ chain ^ spread.keys[chain][i]
            cols = at_cols(block * feats, feats)
            first, last = (i == 0 and chain == 0), (i == spread.count - 1 and chain == 1)

            def one(s, _, chain=chain, i=i, cols=cols, first=first, last=last):
                total = jnp.dot(xbuf[:, cols], wbuf[chain, i, s], preferred_element_type=F32)
                if not first:
                    total = total + acc[s]
                if last:
                    proj[s] = total.astype(BF16)
                else:
                    acc[s] = total
                return 0

            lax.fori_loop(0, streams, one, 0)

    total = 2 * rows

    def halos(up_to, down_to):
        return (
            remote(proj.at[pl.ds(1, 2), pl.ds(total - far, far)], up12, halo_send.at[0], halo_recv.at[0], ctx=up_to),
            remote(proj.at[0, pl.ds(total - pad, pad)], up0, halo_send.at[1], halo_recv.at[1], ctx=up_to),
            remote(proj.at[0, pl.ds(0, far)], down0, halo_send.at[2], halo_recv.at[2], ctx=down_to),
            remote(proj.at[pl.ds(1, 2), pl.ds(0, pad)], down12, halo_send.at[3], halo_recv.at[3], ctx=down_to),
        )

    edges = halos(me + 2, me - 2)

    @pl.when(chip < chips - 1)
    def _():
        edges[0].start()
        edges[1].start()

    @pl.when(chip > 0)
    def _():
        edges[2].start()
        edges[3].start()

    @pl.when(chip == 0)
    def _():
        up12[...] = jnp.zeros_like(up12)
        up0[...] = jnp.zeros_like(up0)

    @pl.when(chip == chips - 1)
    def _():
        down0[...] = jnp.zeros_like(down0)
        down12[...] = jnp.zeros_like(down12)

    @pl.when(chip > 0)
    def _():
        edges[0].wait_recv()
        edges[1].wait_recv()
        edges[2].wait_send()
        edges[3].wait_send()

    @pl.when(chip < chips - 1)
    def _():
        edges[2].wait_recv()
        edges[3].wait_recv()
        edges[0].wait_send()
        edges[1].wait_send()

    for h in range(1, n):
        @pl.when((z < n - 1) & (z - h + 1 >= 0))
        def _():
            up(h, z - h + 1).wait_send()

        @pl.when((z > 0) & (z + h - 1 <= n - 1))
        def _():
            down(h, z + h - 1).wait_send()
    for t in range(n):
        to_core(t).wait_send()
    for deal in deals + [send_pos, send_w, give]:
        deal.wait_send()
    spread.finish()
    for copy in keep:
        copy.wait()


def gather(w, slots, pos, rows, far, pad):
    n_ctx, n = lax.axis_size("ctx"), lax.axis_size("fsdp")
    chips = n_ctx // 2
    streams, feats, two = w.shape
    ch, dz = two // 2, slots.shape[2]
    total = 2 * rows
    any_space, vmem = pl.BlockSpec(memory_space=pl.ANY), pl.BlockSpec(memory_space=pltpu.VMEM)
    dma = pltpu.SemaphoreType.DMA

    def shape(*dims):
        return jax.ShapeDtypeStruct(dims, BF16)

    return pl.pallas_call(
        lambda *refs: gather_kernel((n_ctx, n, far, pad), *refs),
        in_specs=[any_space] * 3,
        out_specs=[vmem] * 5 + [any_space] * 2,
        out_shape=[
            shape(streams, total, ch), shape(2, far, ch), shape(pad, ch), shape(far, ch), shape(2, pad, ch),
            shape(total, n * dz), shape(2, chips, streams, feats, ch),
        ],
        scratch_shapes=[
            pltpu.VMEM((2, chips, streams, feats, ch), BF16),
            pltpu.VMEM((total, n * dz), BF16),
            pltpu.VMEM((chips, 2, slots.shape[1], dz), BF16),
            pltpu.VMEM((2, *pos.shape[1:]), jnp.int32),
            pltpu.VMEM((rows, dz), BF16),
            pltpu.VMEM((rows, dz), BF16),
            pltpu.VMEM((streams, total, ch), F32),
            dma((2, chips)), dma((2, chips)), dma((chips,)), dma((chips,)),
            dma((n,)), dma((n,)), dma((n,)), dma((n,)),
            dma((n,)), dma((n,)), dma((3,)), dma((3,)), dma((4,)), dma((2, chips)), dma((4,)), dma((4,)),
        ],
        compiler_params=pltpu.CompilerParams(
            collective_id=0, has_side_effects=True, vmem_limit_bytes=56 << 20
        ),
        cost_estimate=pl.CostEstimate(
            flops=2 * total * n * dz * streams * ch, bytes_accessed=40 << 20, transcendentals=0
        ),
        name="gather_and_project",
    )(w, slots, pos)


def reduce_kernel(
    sizes, grads, wall, left, gated, sums,
    wg, tg, gout, filt,
    gbuf, lbuf, acc, wgb, wv, xp, xs, xr, up_tx, up_rx, dn_tx, dn_rx, fbuf, ftot,
    g_send, g_recv, f_send, f_recv, up_send, up_recv, dn_send, dn_recv,
    core_send, core_recv, misc_send, misc_recv, local_sem, wv_sem,
):
    n_ctx, n = sizes
    me, z = lax.axis_index("ctx"), lax.axis_index("fsdp")
    core, chip = me % 2, me // 2
    chips = n_ctx // 2
    streams, rows, ch = gbuf.shape[2:]
    feats = lbuf.shape[1]
    dz = xp.shape[1] // n
    masks = chip_masks(n_ctx)
    sib = me ^ 1
    own_g = [
        local(grads.at[:, pl.ds(b * rows, rows)], gbuf.at[b, 0], local_sem.at[b]) for b in (0, 1)
    ]
    for copy in own_g:
        copy.start()
    spread = Spread(gbuf, g_send, g_recv, masks, me)
    wkeys = (walk(masks), walk(masks[::-1]))
    order = [(chain, i) for i in range(chips) for chain in (0, 1)]

    def fetch(j):
        chain, i = order[j]
        return local(wall.at[chain, i], wv.at[j % 2], wv_sem.at[j % 2])

    fetch(0).start()
    get_left = local(left, lbuf, local_sem.at[2])
    get_left.start()
    greet(n_ctx, n)
    for copy in own_g:
        copy.wait()
    for chain in (0, 1):
        spread.start(chain, 0)

    fbuf[chip] = sums[...]
    shares = []
    for k in range(2, n_ctx, 2):
        shares.append(remote(
            fbuf.at[chip], fbuf.at[chip], f_send.at[k // 2], f_recv.at[k // 2], ctx=me ^ k
        ))
        shares[-1].start()
    mine = at_cols(core * ch, ch)
    keep_gated = local(gated.at[pl.ds(core * rows, rows)], gout.at[:, mine], local_sem.at[3])
    give_gated = remote(
        gated.at[pl.ds((1 - core) * rows, rows)], gout.at[:, mine], misc_send.at[0], misc_recv.at[0], ctx=sib
    )
    keep_gated.start()
    give_gated.start()

    def to_core(block):
        cols = at_cols(block * feats, feats)
        return remote(xs.at[:, cols], xr.at[:, cols], core_send.at[block], core_recv.at[block], ctx=sib)

    for j, (chain, i) in enumerate(order):
        if j + 1 < len(order):
            fetch(j + 1).start()
        fetch(j).wait()
        block = me ^ chain ^ wkeys[chain][i]
        cols = at_cols(block * feats, feats)

        def back(b, j=j):
            total = None
            for s in range(streams):
                term = lax.dot_general(
                    gbuf[b, 0, s], wv[j % 2, s], (((1,), (1,)), ((), ())), preferred_element_type=F32
                )
                total = term if total is None else total + term
            return total

        xs[:, cols] = back(1 - core).astype(BF16)
        to_core(block).start()
        xp[:, cols] = back(core)

    step = 32

    def each(body):
        def one(r, _):
            body(pl.ds(pl.multiple_of(r * step, step), step))
            return 0

        lax.fori_loop(0, rows // step, one, 0)

    def weigh(chain, i):
        where = ((me - core) ^ spread.keys[chain][i]) + chain
        cols = at_cols(where * rows, rows)
        first = i == 0 and chain == 0

        def one(r, _):
            h, s = r // streams, r % streams
            total = jnp.dot(lbuf[h, :, cols], gbuf[chain, i, s], preferred_element_type=F32)
            acc[r] = total if first else acc[r] + total
            return 0

        lax.fori_loop(0, 2 * streams, one, 0)

    for block in range(n_ctx):
        to_core(block).wait_recv()
    get_left.wait()

    def up(s):
        return remote(up_tx.at[s - 1], up_rx.at[s - 1], up_send.at[s], up_recv.at[s], fsdp=z + 1)

    def down(s):
        return remote(dn_tx.at[s - 1], dn_rx.at[s - 1], dn_send.at[s], dn_recv.at[s], fsdp=z - 1)

    zz = n - 1 - z

    def send_tile(s, a, far_end, tx, rx):
        cols = at_cols(a * dz, dz)

        @pl.when(far_end == 0)
        def _():
            def body(at):
                tx[s - 1, at] = (xp[at, cols] + xr[at, cols].astype(F32)).astype(BF16)
            each(body)

        if s >= 2:
            @pl.when(far_end > 0)
            def _():
                def body(at):
                    total = xp[at, cols] + xr[at, cols].astype(F32) + rx[s - 2, at].astype(F32)
                    tx[s - 1, at] = total.astype(BF16)
                each(body)

    def line_start(s):
        last = min(s - 1, n - 2)

        @pl.when(z <= last)
        def _():
            send_tile(s, n - s + z, z, up_tx, up_rx)
            up(s).start()

        @pl.when(zz <= last)
        def _():
            send_tile(s, z + s - n, zz, dn_tx, dn_rx)
            down(s).start()

    def line_wait(s):
        last = min(s - 1, n - 2)

        @pl.when((z >= 1) & (z - 1 <= last))
        def _():
            up(s).wait_recv()

        @pl.when((zz >= 1) & (zz - 1 <= last))
        def _():
            down(s).wait_recv()

    todo = [("own", chain, 0) for chain in (0, 1)]
    line = iter(range(1, n))
    if n > 1:
        line_start(1)
    sent = 1
    for i in range(spread.count):
        for chain in (0, 1):
            if i:
                spread.arrive(chain, i)
                spread.start(chain, i)
        for chain in (0, 1):
            weigh(chain, i)
        if i >= 1 and sent < n - 1:
            line_wait(sent)
            sent += 1
            line_start(sent)
    while sent < n - 1:
        line_wait(sent)
        sent += 1
        line_start(sent)

    wgb[...] = acc[...].astype(BF16)
    give_w = remote(
        wgb.at[pl.ds(streams, streams)], wg.at[:, :, mine], misc_send.at[1], misc_recv.at[1], ctx=sib
    )
    give_w.start()
    keep_w = local(wgb.at[pl.ds(0, streams)], wg.at[:, :, mine], local_sem.at[4])
    keep_w.start()

    for share in shares:
        share.wait_recv()
    total = fbuf[0].astype(F32)
    for c in range(1, chips):
        total = total + fbuf[c].astype(F32)
    ftot[...] = total
    give_f = remote(ftot, filt.at[:, mine], misc_send.at[2], misc_recv.at[2], ctx=sib)
    give_f.start()
    keep_f = local(ftot, filt.at[:, mine], local_sem.at[5])
    keep_f.start()

    if n > 1:
        line_wait(n - 1)
    cols = at_cols(z * dz, dz)

    def final(at):
        acc_t = xp[at, cols] + xr[at, cols].astype(F32)
        if n > 1:
            acc_t = acc_t + jnp.where(z >= 1, up_rx[n - 2, at].astype(F32), 0.0)
            acc_t = acc_t + jnp.where(zz >= 1, dn_rx[n - 2, at].astype(F32), 0.0)
        tg[at] = acc_t.astype(BF16)

    each(final)

    for s in range(1, n):
        last = min(s - 1, n - 2)

        @pl.when(z <= last)
        def _():
            up(s).wait_send()

        @pl.when(zz <= last)
        def _():
            down(s).wait_send()
    for block in range(n_ctx):
        to_core(block).wait_send()
    spread.finish()
    for share in shares:
        share.wait_send()
    for copy in (give_gated, give_w, give_f):
        copy.wait()
    for copy in (keep_gated, keep_w, keep_f):
        copy.wait()


def reduce(grads, wall, left, gated, sums):
    n_ctx, n = lax.axis_size("ctx"), lax.axis_size("fsdp")
    chips = n_ctx // 2
    streams, total, ch = grads.shape
    rows = total // 2
    feats = left.shape[1]
    dim = feats * n_ctx
    dz = dim // n
    any_space, vmem = pl.BlockSpec(memory_space=pl.ANY), pl.BlockSpec(memory_space=pltpu.VMEM)
    dma = pltpu.SemaphoreType.DMA
    hops = max(n - 1, 1)
    return pl.pallas_call(
        lambda *refs: reduce_kernel((n_ctx, n), *refs),
        in_specs=[any_space] * 4 + [vmem],
        out_specs=[any_space, vmem, any_space, any_space],
        out_shape=[
            jax.ShapeDtypeStruct((streams, feats, 2 * ch), BF16),
            jax.ShapeDtypeStruct((rows, dz), BF16),
            jax.ShapeDtypeStruct((rows, 2 * ch), BF16),
            jax.ShapeDtypeStruct((sums.shape[0], 2 * ch), F32),
        ],
        scratch_shapes=[
            pltpu.VMEM((2, chips, streams, rows, ch), BF16),
            pltpu.VMEM(left.shape, BF16),
            pltpu.VMEM((2 * streams, feats, ch), F32),
            pltpu.VMEM((2 * streams, feats, ch), BF16),
            pltpu.VMEM((2, streams, feats, ch), BF16),
            pltpu.VMEM((rows, dim), F32),
            pltpu.VMEM((rows, dim), BF16),
            pltpu.VMEM((rows, dim), BF16),
            pltpu.VMEM((hops, rows, dz), BF16), pltpu.VMEM((hops, rows, dz), BF16),
            pltpu.VMEM((hops, rows, dz), BF16), pltpu.VMEM((hops, rows, dz), BF16),
            pltpu.VMEM((chips, *sums.shape), BF16),
            pltpu.VMEM(sums.shape, F32),
            dma((2, chips)), dma((2, chips)), dma((chips,)), dma((chips,)),
            dma((n,)), dma((n,)), dma((n,)), dma((n,)),
            dma((n_ctx,)), dma((n_ctx,)), dma((3,)), dma((3,)), dma((6,)), dma((2,)),
        ],
        compiler_params=pltpu.CompilerParams(
            collective_id=1, has_side_effects=True, vmem_limit_bytes=60 << 20
        ),
        cost_estimate=pl.CostEstimate(
            flops=4 * total * dim * streams * ch, bytes_accessed=40 << 20, transcendentals=0
        ),
        name="gather_and_reduce",
    )(grads, wall, left, gated, sums)


def conv_kernel(
    dims, proj, prev12, prev0, next0, next12, grads, next_grads, dist, room, short, long,
    gated, mixed, long_sums, short_sums,
    s0, s1, s2, go, f0, f1, f2, prod, back, gf, acc,
):
    rows, lead, short_pad, short_w, long_w, tail = dims
    f32 = jnp.float32
    s0[0:short_pad, :] = prev0[...].astype(f32)
    s0[short_pad : short_pad + rows, :] = proj[0].astype(f32)
    s0[short_pad + rows :, :] = next0[...].astype(f32)
    for k, ref in ((0, s1), (1, s2)):
        ref[0 : lead + short_pad, :] = prev12[k].astype(f32)
        ref[lead + short_pad : lead + short_pad + rows, :] = proj[1 + k].astype(f32)
        ref[lead + short_pad + rows :, :] = next12[k].astype(f32)
    go[0:rows, :] = grads[...].astype(f32)
    go[rows:, :] = next_grads[...].astype(f32)

    def rounded(x):
        return x.astype(jnp.bfloat16).astype(f32)

    step = 8 * 7 if (lead + rows + tail) % 56 == 0 else 8

    def lead_short(ref, taps, base, reach, n):
        total = jnp.zeros((n, LANES), f32)
        for j in range(short_w):
            x = ref[pl.ds(base + short_pad - j, n), :]
            total = total + jnp.where(reach >= j, x, 0.0) * taps[j : j + 1, :]
        return total

    def before(i, _):
        base = pl.multiple_of(i * step, 8)
        reach = dist[pl.ds(base, step), :]
        a = lead_short(s1, short[1], base, reach, step)
        b = lead_short(s2, short[2], base, reach, step)
        f1[pl.ds(base, step), :] = a
        f2[pl.ds(base, step), :] = b
        prod[pl.ds(base, step), :] = rounded(a * b)
        return 0

    lax.fori_loop(0, (lead + rows + tail) // step, before, 0)

    def after(i, _):
        base = pl.multiple_of(i * step, 8)
        reach = dist[pl.ds(base + lead, step), :]
        a = lead_short(s0, short[0], base, reach, step)
        f0[pl.ds(base, step), :] = a
        back[pl.ds(base, step), :] = rounded(go[pl.ds(base, step), :] * a)
        return 0

    lax.fori_loop(0, (rows + tail + lead) // step, after, 0)

    acc[...] = jnp.zeros_like(acc)
    unroll = 8

    def long_tile(base, n, own):
        reach = dist[pl.ds(base + lead, n), :]
        ahead = room[pl.ds(base, n), :]
        here = back[pl.ds(base, n), :]

        def taps_step(i, carry):
            carried, grad = carry
            for u in range(unroll):
                j = i * unroll + u
                tap = long[pl.ds(j, 1), :]
                x = jnp.where(reach >= j, prod[pl.ds(base + lead - j, n), :], 0.0)
                y = jnp.where(ahead >= j, back[pl.ds(base + j, n), :], 0.0)
                carried = carried + x * tap
                grad = grad + y * tap
                if own:
                    z = here * x
                    part = z[0:8, :]
                    for r in range(8, n, 8):
                        part = part + z[r : r + 8, :]
                    at = pl.multiple_of(j * 8, 8)
                    acc[pl.ds(at, 8), :] += part
            return carried, grad

        zero = jnp.zeros((n, LANES), f32)
        carried, grad = lax.fori_loop(0, long_w // unroll, taps_step, (zero, zero))
        if own:
            gated[pl.ds(base, n), :] = (f0[pl.ds(base, n), :] * carried).astype(gated.dtype)
        gf[0, pl.ds(base, n), :] = rounded(go[pl.ds(base, n), :] * carried)
        gf[1, pl.ds(base, n), :] = rounded(grad * f2[pl.ds(base + lead, n), :])
        gf[2, pl.ds(base, n), :] = rounded(grad * f1[pl.ds(base + lead, n), :])

    tile = 64 if rows % 64 == 0 else 8
    lax.fori_loop(
        0, rows // tile, lambda i, _: (long_tile(pl.multiple_of(i * tile, 8), tile, True), 0)[1], 0
    )
    for extra in range(0, tail, 8):
        long_tile(rows + extra, 8, False)
    long_sums[...] = jnp.sum(acc[...].reshape(long_w, 8, LANES), axis=1)

    short_sums[...] = jnp.zeros_like(short_sums)

    def last(i, _):
        base = pl.multiple_of(i * tile, 8)
        reach = dist[pl.ds(base + lead, tile), :]
        ahead = room[pl.ds(base, tile), :]
        for s, ref, off in ((0, s0, 0), (1, s1, lead), (2, s2, lead)):
            total = jnp.zeros((tile, LANES), f32)
            here = gf[s, pl.ds(base, tile), :]
            for j in range(short_w):
                y = jnp.where(ahead >= j, gf[s, pl.ds(base + j, tile), :], 0.0)
                total = total + y * short[s, j : j + 1, :]
                x = jnp.where(reach >= j, ref[pl.ds(base + off + short_pad - j, tile), :], 0.0)
                short_sums[s, j : j + 1, :] += jnp.sum(here * x, axis=0, keepdims=True)
            mixed[s, pl.ds(base, tile), :] = total.astype(mixed.dtype)
        return 0

    lax.fori_loop(0, rows // tile, last, 0)


def conv_block(proj, up, up0, down0, down12, grad_out, down_grads, short_taps, long_taps, contig_lengths):
    _, rows, chans = proj.shape
    short_w, long_w = short_taps.shape[1], long_taps.shape[0]
    short_pad = 16
    lead = round_up(long_w, 16)
    tail = round_up(short_w - 1, 8)
    far = lead + short_pad

    offset = lax.axis_index("ctx") // 2 * rows
    order = jnp.arange(contig_lengths.shape[0], dtype=jnp.int32)
    ends = jnp.sum(jnp.where(order[None, :] <= order[:, None], contig_lengths[None, :], 0), axis=1)
    begins = ends - contig_lengths
    at = offset - lead + jnp.arange(lead + rows + far, dtype=jnp.int32)
    first = jnp.max(jnp.where(begins[None, :] <= at[:, None], begins[None, :], 0), axis=1)
    dist = jnp.broadcast_to((at - first)[:, None], (at.shape[0], LANES))
    here = offset + jnp.arange(rows + short_pad, dtype=jnp.int32)
    big = jnp.int32(2**30)
    end = jnp.min(jnp.where(ends[None, :] > here[:, None], ends[None, :], big), axis=1)
    room = jnp.broadcast_to((end - 1 - here)[:, None], (here.shape[0], LANES))

    def block(*lead_dims):
        n = len(lead_dims)
        return pl.BlockSpec((*lead_dims, LANES), lambda i: (0,) * n + (i,))

    def whole(r):
        return pl.BlockSpec((r, LANES), lambda i: (0, 0))

    def vmem(*shape):
        return pltpu.VMEM((*shape, LANES), jnp.float32)

    span = lead + rows + tail
    dims = (rows, lead, short_pad, short_w, long_w, tail)
    return pl.pallas_call(
        lambda *refs: conv_kernel(dims, *refs),
        grid=(chans // LANES,),
        in_specs=[
            block(3, rows), block(2, far), block(short_pad), block(far), block(2, short_pad),
            block(rows), block(far), whole(dist.shape[0]), whole(room.shape[0]),
            block(3, short_w), block(long_w),
        ],
        out_specs=[block(rows), block(3, rows), block(long_w), block(3, 8 * -(-short_w // 8))],
        out_shape=[
            jax.ShapeDtypeStruct((rows, chans), jnp.bfloat16),
            jax.ShapeDtypeStruct((3, rows, chans), jnp.bfloat16),
            jax.ShapeDtypeStruct((long_w, chans), jnp.float32),
            jax.ShapeDtypeStruct((3, 8 * -(-short_w // 8), chans), jnp.float32),
        ],
        scratch_shapes=[
            vmem(short_pad + rows + far), vmem(far + rows + short_pad),
            vmem(far + rows + short_pad), vmem(rows + far),
            vmem(span), vmem(span), vmem(span), vmem(span), vmem(span),
            vmem(3, rows + short_pad), vmem(long_w * 8),
        ],
        compiler_params=pltpu.CompilerParams(vmem_limit_bytes=40 << 20),
        cost_estimate=pl.CostEstimate(
            flops=rows * chans * long_w * 10, bytes_accessed=rows * chans * 24, transcendentals=0
        ),
        name="hyena_filters",
    )(proj, up, up0, down0, down12, grad_out, down_grads, dist, room, short_taps, long_taps)


def on_device(loaded, slot_pos, contig_lengths, w_in, short_taps, long_taps, grad_out):
    me = lax.axis_index("ctx")
    core, pair = me % 2, me - me % 2
    rows, chans = grad_out.shape
    feats = w_in.shape[0]
    short_w, long_w = short_taps.shape[1], long_taps.shape[0]
    far, pad = round_up(long_w, 16) + 16, 16
    n_ctx = lax.axis_size("ctx")

    keep_c = half(grad_out, 1, core)
    grad_c = by_core(keep_c, swapped(half(grad_out, 1, 1 - core), 1), 0)
    short_c, long_c = half(short_taps, 2, core), half(long_taps, 1, core)
    down_grads = neighbour_rows(grad_c[:far], -1)

    proj, up12, up0, down0, down12, tokens, wall = gather(
        jnp.transpose(w_in, (1, 0, 2)), loaded[0], slot_pos, rows, far, pad
    )
    left = jnp.zeros((feats, rows * n_ctx), BF16)
    for mask in range(0, n_ctx, 2):
        x = lax.dynamic_slice_in_dim(tokens, (me ^ mask) * feats, feats, 1)
        x = swapped(x, mask) if mask else x
        left = lax.dynamic_update_slice_in_dim(left, x.T, (pair ^ mask) * rows, 1)
    left = jnp.stack([left, swapped(left, 1)])

    gated, grads, long_local, short_local = conv_block(
        proj, up12, up0, down0, down12, grad_c, down_grads, short_c, long_c, contig_lengths
    )
    sums = jnp.concatenate([long_local, short_local.reshape(-1, chans // 2)], 0).astype(BF16)
    count = sums.shape[0]
    sums = jnp.pad(sums, ((0, -count % 16), (0, 0)))
    weight_grads, token_grads, gated_out, filters = reduce(grads, wall, left, gated, sums)
    long_total = filters[:long_w]
    short_total = filters[long_w:count].reshape(3, -1, chans)[:, :short_w]
    return gated_out, token_grads, jnp.transpose(weight_grads, (1, 0, 2)), short_total, long_total


def solution(mesh):
    in_specs = (
        P("ctx", None, None, "fsdp"),
        P("ctx", None, None),
        P(),
        P("ctx", None, "fsdp"),
        P(None, None, "fsdp"),
        P(None, "fsdp"),
        P("ctx", "fsdp"),
    )
    out_specs = (
        P("ctx", "fsdp"),
        P("ctx", "fsdp"),
        P("ctx", None, "fsdp"),
        P(None, None, "fsdp"),
        P(None, "fsdp"),
    )
    return jax.shard_map(
        on_device, mesh=mesh, in_specs=in_specs, out_specs=out_specs, check_vma=False
    )
```

```python
import jax
import jax.numpy as jnp
from jax import lax
from jax.experimental import pallas as pl
from jax.experimental.pallas import tpu as pltpu
from jax.sharding import PartitionSpec as P

LANES = 128
F32, BF16 = jnp.float32, jnp.bfloat16


def round_up(x, to):
    return -(-x // to) * to


def swapped(x, mask):
    size = lax.axis_size("ctx")
    return lax.ppermute(x, "ctx", [(i, i ^ mask) for i in range(size)])


def chip_masks(size):
    masks, step = [], 2
    while step < size:
        masks.append(step)
        step *= 2
    return masks


def walk(masks):
    held = [0]
    for mask in masks:
        held = held + [k ^ mask for k in held]
    return held


def half(x, dim, which):
    width = x.shape[dim] // 2
    return lax.dynamic_slice_in_dim(x, which * width, width, dim)


def remote(src, dst, send, recv, **place):
    return pltpu.make_async_remote_copy(
        src_ref=src, dst_ref=dst, send_sem=send, recv_sem=recv,
        device_id=place, device_id_type=pl.DeviceIdType.MESH,
    )


def local(src, dst, sem):
    return pltpu.make_async_copy(src, dst, sem)


def at_cols(start, size):
    return pl.ds(pl.multiple_of(start, LANES), size)


def greet(n_ctx, n_line):
    me, z = lax.axis_index("ctx"), lax.axis_index("fsdp")
    barrier = pltpu.get_barrier_semaphore()
    others = [1] + [k for k in range(2, n_ctx, 2)]
    for k in others:
        pl.semaphore_signal(
            barrier, inc=1, device_id={"ctx": me ^ k}, device_id_type=pl.DeviceIdType.MESH
        )

    @pl.when(z > 0)
    def _():
        pl.semaphore_signal(
            barrier, inc=1, device_id={"fsdp": z - 1}, device_id_type=pl.DeviceIdType.MESH
        )

    @pl.when(z < n_line - 1)
    def _():
        pl.semaphore_signal(
            barrier, inc=1, device_id={"fsdp": z + 1}, device_id_type=pl.DeviceIdType.MESH
        )

    ends = jnp.where(z > 0, 1, 0) + jnp.where(z < n_line - 1, 1, 0)
    pl.semaphore_wait(barrier, len(others) + ends)


class Spread:
    def __init__(self, buf, send, recv, masks, me):
        self.buf, self.send, self.recv, self.me = buf, send, recv, me
        self.orders = (masks, masks[::-1])
        self.keys = tuple(walk(m) for m in self.orders)
        self.count = 1 << len(masks)

    def copy(self, chain, stage, i):
        to = (1 << stage) + i
        return remote(
            self.buf.at[chain, i], self.buf.at[chain, to],
            self.send.at[chain, to], self.recv.at[chain, to],
            ctx=self.me ^ self.orders[chain][stage],
        )

    def stages(self, i):
        return range(i.bit_length(), len(self.orders[0]))

    def start(self, chain, i, stages=None):
        for stage in self.stages(i) if stages is None else stages:
            self.copy(chain, stage, i).start()

    def arrive(self, chain, i):
        stage = i.bit_length() - 1
        self.copy(chain, stage, i - (1 << stage)).wait_recv()

    def finish(self):
        for chain in (0, 1):
            for i in range(self.count):
                for stage in self.stages(i):
                    self.copy(chain, stage, i).wait_send()


def gather_kernel(
    sizes, w, slots, pos, grad,
    proj, up12, up0, down0, down12, gext, wall, *rest
):
    n_ctx, n, far, pad = sizes
    turned, rest = rest[: n_ctx // 2], rest[n_ctx // 2 :]
    gather_body(n_ctx, n, far, pad, w, slots, pos, grad, proj, up12, up0, down0, down12, gext, wall, turned, *rest)


def gather_body(
    n_ctx, n, far, pad, w, slots, pos, grad,
    proj, up12, up0, down0, down12, gext, wall, turned,
    tbuf, wbuf, xbuf, sbuf, pbuf, part, ppart, acc,
    w_send, w_recv, s_send, s_recv, up_send, up_recv, dn_send, dn_recv,
    core_send, core_recv, misc_send, misc_recv, local_sem, out_sem, halo_send, halo_recv, turn_sem,
):
    me, z = lax.axis_index("ctx"), lax.axis_index("fsdp")
    core, chip = me % 2, me // 2
    chips = n_ctx // 2
    rows, dz = ppart.shape
    streams, feats, ch = wbuf.shape[2:]
    masks = chip_masks(n_ctx)
    greet(n_ctx, n)

    sib = me ^ 1
    own_pos = local(pos.at[0], pbuf.at[core], local_sem.at[0])
    own_pos.start()
    send_pos = remote(pos.at[0], pbuf.at[core], misc_send.at[0], misc_recv.at[0], ctx=sib)
    send_pos.start()
    own_slots = local(slots.at[pl.ds(2 * chip, 2)], sbuf.at[chip], local_sem.at[1])
    own_slots.start()
    deals = []
    for k in range(2, n_ctx, 2):
        to = me ^ k
        deals.append(remote(
            slots.at[pl.ds(to - core, 2)], sbuf.at[chip], s_send.at[k // 2], s_recv.at[k // 2], ctx=to
        ))
        deals[-1].start()
    own_w = local(w.at[:, :, at_cols(core * ch, ch)], wbuf.at[0, 0], local_sem.at[2])
    own_w.start()
    send_w = remote(
        w.at[:, :, at_cols((1 - core) * ch, ch)], wbuf.at[1, 0], misc_send.at[1], misc_recv.at[1], ctx=sib
    )
    send_w.start()
    own_rows = pl.ds(pl.multiple_of(core * rows, rows), rows)
    own_grad = local(grad.at[:, at_cols(core * ch, ch)], gext.at[own_rows], local_sem.at[3])
    own_grad.start()
    send_grad = remote(
        grad.at[:, at_cols((1 - core) * ch, ch)], gext.at[own_rows], misc_send.at[3], misc_recv.at[3], ctx=sib
    )
    send_grad.start()
    spread = Spread(wbuf, w_send, w_recv, masks, me)
    stages = len(masks)
    keep = []

    def stored(chain, i):
        keep.append(local(wbuf.at[chain, i], wall.at[chain, i], out_sem.at[chain, i]))
        keep[-1].start()

    own_w.wait()
    spread.start(0, 0, range(0, min(1, stages)))
    stored(0, 0)
    send_w.wait_recv()
    spread.start(1, 0, range(0, min(1, stages)))
    stored(1, 0)

    own_pos.wait()
    send_pos.wait_recv()
    own_slots.wait()
    for deal in deals:
        deal.wait_recv()
    spread.start(0, 0, range(1, stages))
    spread.start(1, 0, range(1, stages))

    seat = lax.broadcasted_iota(jnp.int32, (rows, pos.shape[2]), 0)

    def place(b):
        total = None
        for c in range(chips):
            row = pbuf[b, pl.ds(2 * c + core, 1), :]
            pick = jnp.where(row == seat, 1.0, 0.0).astype(BF16)
            term = jnp.dot(pick, sbuf[c, b], preferred_element_type=F32)
            total = term if total is None else total + term
        return total.astype(BF16)

    part[...] = place(1 - core)
    give = remote(part, ppart, misc_send.at[2], misc_recv.at[2], ctx=sib)
    give.start()
    mine = place(core)
    give.wait_recv()
    own_grad.wait()
    send_grad.wait_recv()
    edge_grad = remote(
        gext.at[pl.ds(0, far)], gext.at[pl.ds(2 * rows, far)], misc_send.at[4], misc_recv.at[4], ctx=me - 2
    )

    @pl.when(chip > 0)
    def _():
        edge_grad.start()

    xbuf[own_rows, at_cols(z * dz, dz)] = mine + ppart[...]

    def tile(t):
        return xbuf.at[own_rows, at_cols(t * dz, dz)]

    def to_core(t):
        return remote(tile(t), tile(t), core_send.at[t], core_recv.at[t], ctx=sib)

    def other_tile(t):
        there = xbuf.at[pl.ds(pl.multiple_of((1 - core) * rows, rows), rows), at_cols(t * dz, dz)]
        return remote(there, there, core_send.at[t], core_recv.at[t], ctx=sib)

    def up(h, t):
        return remote(tile(t), tile(t), up_send.at[h], up_recv.at[h], fsdp=z + 1)

    def down(h, t):
        return remote(tile(t), tile(t), dn_send.at[h], dn_recv.at[h], fsdp=z - 1)

    to_core(z).start()
    for h in range(1, n):
        @pl.when((z < n - 1) & (z - h + 1 >= 0))
        def _():
            up(h, z - h + 1).start()

        @pl.when((z > 0) & (z + h - 1 <= n - 1))
        def _():
            down(h, z + h - 1).start()

        @pl.when(z - h >= 0)
        def _():
            up(h, z - h).wait_recv()
            to_core(z - h).start()

        @pl.when(z + h <= n - 1)
        def _():
            down(h, z + h).wait_recv()
            to_core(z + h).start()

        if h == 1 and spread.count > 1:
            for chain in (0, 1):
                spread.arrive(chain, 1)
                spread.start(chain, 1)
                stored(chain, 1)
    for t in range(n):
        other_tile(t).wait_recv()
    for m in range(chips):
        tbuf[m] = xbuf[:, at_cols((me ^ (2 * m)) * feats, feats)].T
        keep.append(local(tbuf.at[m], turned[m], turn_sem.at[m]))
        keep[-1].start()

    for i in range(spread.count):
        for chain in (0, 1):
            if i > 1:
                spread.arrive(chain, i)
                spread.start(chain, i)
                stored(chain, i)
            block = me ^ chain ^ spread.keys[chain][i]
            cols = at_cols(block * feats, feats)
            first, last = (i == 0 and chain == 0), (i == spread.count - 1 and chain == 1)

            def one(s, _, chain=chain, i=i, cols=cols, first=first, last=last):
                total = jnp.dot(xbuf[:, cols], wbuf[chain, i, s], preferred_element_type=F32)
                if not first:
                    total = total + acc[s]
                if last:
                    proj[s] = total.astype(BF16)
                else:
                    acc[s] = total
                return 0

            lax.fori_loop(0, streams, one, 0)

    total = 2 * rows

    def halos(up_to, down_to):
        return (
            remote(proj.at[pl.ds(1, 2), pl.ds(total - far, far)], up12, halo_send.at[0], halo_recv.at[0], ctx=up_to),
            remote(proj.at[0, pl.ds(total - pad, pad)], up0, halo_send.at[1], halo_recv.at[1], ctx=up_to),
            remote(proj.at[0, pl.ds(0, far)], down0, halo_send.at[2], halo_recv.at[2], ctx=down_to),
            remote(proj.at[pl.ds(1, 2), pl.ds(0, pad)], down12, halo_send.at[3], halo_recv.at[3], ctx=down_to),
        )

    edges = halos(me + 2, me - 2)

    @pl.when(chip < chips - 1)
    def _():
        edges[0].start()
        edges[1].start()

    @pl.when(chip > 0)
    def _():
        edges[2].start()
        edges[3].start()

    @pl.when(chip == 0)
    def _():
        up12[...] = jnp.zeros_like(up12)
        up0[...] = jnp.zeros_like(up0)

    @pl.when(chip == chips - 1)
    def _():
        gext[pl.ds(2 * rows, far), :] = jnp.zeros((far, ch), BF16)
        down0[...] = jnp.zeros_like(down0)
        down12[...] = jnp.zeros_like(down12)

    @pl.when(chip > 0)
    def _():
        edges[0].wait_recv()
        edges[1].wait_recv()
        edges[2].wait_send()
        edges[3].wait_send()
        edge_grad.wait_send()

    @pl.when(chip < chips - 1)
    def _():
        edges[2].wait_recv()
        edges[3].wait_recv()
        edge_grad.wait_recv()
        edges[0].wait_send()
        edges[1].wait_send()

    for h in range(1, n):
        @pl.when((z < n - 1) & (z - h + 1 >= 0))
        def _():
            up(h, z - h + 1).wait_send()

        @pl.when((z > 0) & (z + h - 1 <= n - 1))
        def _():
            down(h, z + h - 1).wait_send()
    for t in range(n):
        to_core(t).wait_send()
    for deal in deals + [send_pos, send_w, send_grad, give]:
        deal.wait_send()
    spread.finish()
    for copy in keep:
        copy.wait()


def gather(w, slots, pos, grad, far, pad):
    n_ctx, n = lax.axis_size("ctx"), lax.axis_size("fsdp")
    chips = n_ctx // 2
    streams, feats, two = w.shape
    ch, dz = two // 2, slots.shape[2]
    rows = grad.shape[0]
    total = 2 * rows
    any_space, vmem = pl.BlockSpec(memory_space=pl.ANY), pl.BlockSpec(memory_space=pltpu.VMEM)
    dma = pltpu.SemaphoreType.DMA

    def shape(*dims):
        return jax.ShapeDtypeStruct(dims, BF16)

    return pl.pallas_call(
        lambda *refs: gather_kernel((n_ctx, n, far, pad), *refs),
        in_specs=[any_space] * 4,
        out_specs=[vmem] * 6 + [any_space] * (1 + chips),
        out_shape=[
            shape(streams, total, ch), shape(2, far, ch), shape(pad, ch), shape(far, ch), shape(2, pad, ch),
            shape(total + far, ch),
            shape(2, chips, streams, feats, ch),
        ] + [shape(feats, total)] * chips,
        scratch_shapes=[
            pltpu.VMEM((chips, feats, total), BF16),
            pltpu.VMEM((2, chips, streams, feats, ch), BF16),
            pltpu.VMEM((total, n * dz), BF16),
            pltpu.VMEM((chips, 2, slots.shape[1], dz), BF16),
            pltpu.VMEM((2, *pos.shape[1:]), jnp.int32),
            pltpu.VMEM((rows, dz), BF16),
            pltpu.VMEM((rows, dz), BF16),
            pltpu.VMEM((streams, total, ch), F32),
            dma((2, chips)), dma((2, chips)), dma((chips,)), dma((chips,)),
            dma((n,)), dma((n,)), dma((n,)), dma((n,)),
            dma((n,)), dma((n,)), dma((5,)), dma((5,)), dma((4,)), dma((2, chips)), dma((4,)), dma((4,)), dma((chips,)),
        ],
        compiler_params=pltpu.CompilerParams(
            collective_id=0, has_side_effects=True, vmem_limit_bytes=56 << 20
        ),
        cost_estimate=pl.CostEstimate(
            flops=2 * total * n * dz * streams * ch, bytes_accessed=40 << 20, transcendentals=0
        ),
        name="gather_and_project",
    )(w, slots, pos, grad)


def reduce_kernel(
    sizes, grads, wall, gated, sums, *rest
):
    chips = sizes[0] // 2
    reduce_body(sizes, grads, wall, gated, sums, rest[:chips], *rest[chips:])


def reduce_body(
    sizes, grads, wall, gated, sums, turned,
    wg, tg, gout, filt,
    gbuf, lbuf, acc, wgb, wv, xp, xs, xr, up_tx, up_rx, dn_tx, dn_rx, fbuf, ftot,
    g_send, g_recv, f_send, f_recv, up_send, up_recv, dn_send, dn_recv,
    core_send, core_recv, misc_send, misc_recv, local_sem, wv_sem, t_sem, t_send, t_recv,
):
    n_ctx, n = sizes
    me, z = lax.axis_index("ctx"), lax.axis_index("fsdp")
    core, chip = me % 2, me // 2
    chips = n_ctx // 2
    streams, rows, ch = gbuf.shape[2:]
    feats = lbuf.shape[1]
    dz = xp.shape[1] // n
    masks = chip_masks(n_ctx)
    sib = me ^ 1
    own_g = [
        local(grads.at[:, pl.ds(b * rows, rows)], gbuf.at[b, 0], local_sem.at[b]) for b in (0, 1)
    ]
    for copy in own_g:
        copy.start()
    spread = Spread(gbuf, g_send, g_recv, masks, me)
    wkeys = (walk(masks), walk(masks[::-1]))
    order = [(chain, i) for i in range(chips) for chain in (0, 1)]

    def fetch(j):
        chain, i = order[j]
        return local(wall.at[chain, i], wv.at[j % 2], wv_sem.at[j % 2])

    fetch(0).start()
    lefts, trades = [], []
    for m in range(chips):
        cols = at_cols(((me - core) ^ (2 * m)) * rows, 2 * rows)
        lefts.append(local(turned[m], lbuf.at[0, :, cols], t_sem.at[m]))
        trades.append(remote(turned[m], lbuf.at[1, :, cols], t_send.at[m], t_recv.at[m], ctx=sib))
        lefts[-1].start()
    greet(n_ctx, n)
    for copy in own_g:
        copy.wait()
    for chain in (0, 1):
        spread.start(chain, 0)
    for trade in trades:
        trade.start()

    fbuf[chip] = sums[...]
    shares = []
    for k in range(2, n_ctx, 2):
        shares.append(remote(
            fbuf.at[chip], fbuf.at[chip], f_send.at[k // 2], f_recv.at[k // 2], ctx=me ^ k
        ))
        shares[-1].start()
    mine = at_cols(core * ch, ch)
    keep_gated = local(gated.at[pl.ds(core * rows, rows)], gout.at[:, mine], local_sem.at[3])
    give_gated = remote(
        gated.at[pl.ds((1 - core) * rows, rows)], gout.at[:, mine], misc_send.at[0], misc_recv.at[0], ctx=sib
    )
    keep_gated.start()
    give_gated.start()

    def to_core(block):
        cols = at_cols(block * feats, feats)
        return remote(xs.at[:, cols], xr.at[:, cols], core_send.at[block], core_recv.at[block], ctx=sib)

    for j, (chain, i) in enumerate(order):
        if j + 1 < len(order):
            fetch(j + 1).start()
        fetch(j).wait()
        block = me ^ chain ^ wkeys[chain][i]
        cols = at_cols(block * feats, feats)

        def back(b, j=j):
            total = None
            for s in range(streams):
                term = lax.dot_general(
                    gbuf[b, 0, s], wv[j % 2, s], (((1,), (1,)), ((), ())), preferred_element_type=F32
                )
                total = term if total is None else total + term
            return total

        xs[:, cols] = back(1 - core).astype(BF16)
        to_core(block).start()
        xp[:, cols] = back(core)

    step = 32

    def each(body):
        def one(r, _):
            body(pl.ds(pl.multiple_of(r * step, step), step))
            return 0

        lax.fori_loop(0, rows // step, one, 0)

    def weigh(chain, i):
        where = ((me - core) ^ spread.keys[chain][i]) + chain
        cols = at_cols(where * rows, rows)
        first = i == 0 and chain == 0

        def one(r, _):
            h, s = r // streams, r % streams
            total = jnp.dot(lbuf[h, :, cols], gbuf[chain, i, s], preferred_element_type=F32)
            acc[r] = total if first else acc[r] + total
            return 0

        lax.fori_loop(0, 2 * streams, one, 0)

    for block in range(n_ctx):
        to_core(block).wait_recv()
    for left, trade in zip(lefts, trades):
        left.wait()
        trade.wait_recv()

    def up(s):
        return remote(up_tx.at[s - 1], up_rx.at[s - 1], up_send.at[s], up_recv.at[s], fsdp=z + 1)

    def down(s):
        return remote(dn_tx.at[s - 1], dn_rx.at[s - 1], dn_send.at[s], dn_recv.at[s], fsdp=z - 1)

    zz = n - 1 - z

    def send_tile(s, a, far_end, tx, rx):
        cols = at_cols(a * dz, dz)

        @pl.when(far_end == 0)
        def _():
            def body(at):
                tx[s - 1, at] = (xp[at, cols] + xr[at, cols].astype(F32)).astype(BF16)
            each(body)

        if s >= 2:
            @pl.when(far_end > 0)
            def _():
                def body(at):
                    total = xp[at, cols] + xr[at, cols].astype(F32) + rx[s - 2, at].astype(F32)
                    tx[s - 1, at] = total.astype(BF16)
                each(body)

    def line_start(s):
        last = min(s - 1, n - 2)

        @pl.when(z <= last)
        def _():
            send_tile(s, n - s + z, z, up_tx, up_rx)
            up(s).start()

        @pl.when(zz <= last)
        def _():
            send_tile(s, z + s - n, zz, dn_tx, dn_rx)
            down(s).start()

    def line_wait(s):
        last = min(s - 1, n - 2)

        @pl.when((z >= 1) & (z - 1 <= last))
        def _():
            up(s).wait_recv()

        @pl.when((zz >= 1) & (zz - 1 <= last))
        def _():
            down(s).wait_recv()

    todo = [("own", chain, 0) for chain in (0, 1)]
    line = iter(range(1, n))
    if n > 1:
        line_start(1)
    sent = 1
    for i in range(spread.count):
        for chain in (0, 1):
            if i:
                spread.arrive(chain, i)
                spread.start(chain, i)
        for chain in (0, 1):
            weigh(chain, i)
        if i >= 1 and sent < n - 1:
            line_wait(sent)
            sent += 1
            line_start(sent)
    while sent < n - 1:
        line_wait(sent)
        sent += 1
        line_start(sent)

    wgb[...] = acc[...].astype(BF16)
    give_w = remote(
        wgb.at[pl.ds(streams, streams)], wg.at[:, :, mine], misc_send.at[1], misc_recv.at[1], ctx=sib
    )
    give_w.start()
    keep_w = local(wgb.at[pl.ds(0, streams)], wg.at[:, :, mine], local_sem.at[4])
    keep_w.start()

    for share in shares:
        share.wait_recv()
    total = fbuf[0].astype(F32)
    for c in range(1, chips):
        total = total + fbuf[c].astype(F32)
    ftot[...] = total
    give_f = remote(ftot, filt.at[:, mine], misc_send.at[2], misc_recv.at[2], ctx=sib)
    give_f.start()
    keep_f = local(ftot, filt.at[:, mine], local_sem.at[5])
    keep_f.start()

    if n > 1:
        line_wait(n - 1)
    cols = at_cols(z * dz, dz)

    def final(at):
        acc_t = xp[at, cols] + xr[at, cols].astype(F32)
        if n > 1:
            acc_t = acc_t + jnp.where(z >= 1, up_rx[n - 2, at].astype(F32), 0.0)
            acc_t = acc_t + jnp.where(zz >= 1, dn_rx[n - 2, at].astype(F32), 0.0)
        tg[at] = acc_t.astype(BF16)

    each(final)

    for s in range(1, n):
        last = min(s - 1, n - 2)

        @pl.when(z <= last)
        def _():
            up(s).wait_send()

        @pl.when(zz <= last)
        def _():
            down(s).wait_send()
    for block in range(n_ctx):
        to_core(block).wait_send()
    spread.finish()
    for share in shares:
        share.wait_send()
    for trade in trades:
        trade.wait_send()
    for copy in (give_gated, give_w, give_f):
        copy.wait()
    for copy in (keep_gated, keep_w, keep_f):
        copy.wait()


def reduce(grads, wall, gated, sums, turned):
    n_ctx, n = lax.axis_size("ctx"), lax.axis_size("fsdp")
    chips = n_ctx // 2
    streams, total, ch = grads.shape
    rows = total // 2
    feats = turned[0].shape[0]
    dim = feats * n_ctx
    dz = dim // n
    any_space, vmem = pl.BlockSpec(memory_space=pl.ANY), pl.BlockSpec(memory_space=pltpu.VMEM)
    dma = pltpu.SemaphoreType.DMA
    hops = max(n - 1, 1)
    return pl.pallas_call(
        lambda *refs: reduce_kernel((n_ctx, n), *refs),
        in_specs=[any_space] * 3 + [vmem] + [any_space] * chips,
        out_specs=[any_space, vmem, any_space, any_space],
        out_shape=[
            jax.ShapeDtypeStruct((streams, feats, 2 * ch), BF16),
            jax.ShapeDtypeStruct((rows, dz), BF16),
            jax.ShapeDtypeStruct((rows, 2 * ch), BF16),
            jax.ShapeDtypeStruct((sums.shape[0], 2 * ch), F32),
        ],
        scratch_shapes=[
            pltpu.VMEM((2, chips, streams, rows, ch), BF16),
            pltpu.VMEM((2, feats, rows * n_ctx), BF16),
            pltpu.VMEM((2 * streams, feats, ch), F32),
            pltpu.VMEM((2 * streams, feats, ch), BF16),
            pltpu.VMEM((2, streams, feats, ch), BF16),
            pltpu.VMEM((rows, dim), F32),
            pltpu.VMEM((rows, dim), BF16),
            pltpu.VMEM((rows, dim), BF16),
            pltpu.VMEM((hops, rows, dz), BF16), pltpu.VMEM((hops, rows, dz), BF16),
            pltpu.VMEM((hops, rows, dz), BF16), pltpu.VMEM((hops, rows, dz), BF16),
            pltpu.VMEM((chips, *sums.shape), BF16),
            pltpu.VMEM(sums.shape, F32),
            dma((2, chips)), dma((2, chips)), dma((chips,)), dma((chips,)),
            dma((n,)), dma((n,)), dma((n,)), dma((n,)),
            dma((n_ctx,)), dma((n_ctx,)), dma((3,)), dma((3,)), dma((6,)), dma((2,)),
            dma((chips,)), dma((chips,)), dma((chips,)),
        ],
        compiler_params=pltpu.CompilerParams(
            collective_id=1, has_side_effects=True, vmem_limit_bytes=60 << 20
        ),
        cost_estimate=pl.CostEstimate(
            flops=4 * total * dim * streams * ch, bytes_accessed=40 << 20, transcendentals=0
        ),
        name="gather_and_reduce",
    )(grads, wall, gated, sums, *turned)


ROW = 8
LEAF = 2


def leaves(kind, size=ROW, buf=0, start=0, vec=(0, ROW), sign=1, rows=(0, ROW)):
    def split(size, buf, start, vec, adds):
        if size == LEAF:
            yield buf, start, vec, adds
            return
        h = size // 2
        step = {8: 1, 4: 2}[size]
        low, high, both = vec + (0,), vec + (1,), vec + (2,)
        yield from split(h, buf, start + h, both, adds + [(r + h, g) for r, g in adds])
        first = [(r, g) for r, g in adds]
        second = [(r + h, g) for r, g in adds]
        minus = lambda adds: [(r, -g) for r, g in adds]
        if kind == 0:
            yield from split(h, buf + step, start, high, first)
            yield from split(h, buf + step, start + h, low, minus(second))
        elif kind == 1:
            yield from split(h, buf + step, start + h, high, minus(first))
            yield from split(h, buf + step, start, low, second)
        else:
            yield from split(h, buf + step, start, low, first)
            yield from split(h, buf + step, start + h, high, minus(second))
    return list(split(ROW, 0, 0, (), [(0, 1)]))


def vector_parts(xs):
    parts = {(): xs}
    size = len(xs)
    while size > LEAF:
        size //= 2
        parts = {
            k + (m,): y
            for k, v in parts.items()
            for m, y in ((0, v[:size]), (1, v[size:]), (2, [a + b for a, b in zip(v[:size], v[size:])]))
        }
    return parts


KEYS = sorted(vector_parts([0] * ROW))
COUNT = len(KEYS)


def conv_kernel(
    dims, limits, near, proj, up12, up0, down0, down12, grads, short, long,
    gated, mixed, sums,
    s0, s1, s2, go, f0, f1, f2, prod, back, prod_less, back_less, leaves_l, seen, car, gf, acc, taps, taps_sums, few, out,
):
    rows, far, pad, short_w, long_w, spans, groups, seg, tail = dims

    def spread_rows(dst, at, pieces):
        size = dst.shape[0] // ROW
        for span in range(spans):
            base = span * seg + at
            for start, count, read in pieces:
                low, high = max(base, start), min(base + size, start + count)
                if low >= high:
                    continue
                for g in range(groups):
                    x = read(low - start, high - low, slice(g * LANES, (g + 1) * LANES)).astype(F32)
                    dst[pl.ds((low - base) * ROW + span * groups + g, high - low, stride=ROW), :] = x

    def piece(ref, start, *lead):
        return start, ref.shape[-2], lambda r, n, c: ref[(*lead, slice(r, r + n), c)]

    spread_rows(s0, -pad, [piece(up0, -pad), piece(proj, 0, 0), piece(down0, rows)])
    for k, dst in ((0, s1), (1, s2)):
        spread_rows(dst, -far, [piece(up12, -far, k), piece(proj, 0, 1 + k), piece(down12, rows, k)])
    spread_rows(go, 0, [piece(grads, 0)])
    for span in range(spans):
        for g in range(groups):
            c = slice(g * LANES, (g + 1) * LANES)
            taps[pl.ds(span * groups + g, long_w, stride=ROW), :] = long[:, c]
            for s in range(3):
                few[pl.ds(s * short_w * ROW + span * groups + g, short_w, stride=ROW), :] = short[s, :, c]

    def tile(ref, i):
        return ref[pl.ds(pl.multiple_of(i * ROW, ROW), ROW), :]

    def put(ref, i, x):
        ref[pl.ds(pl.multiple_of(i * ROW, ROW), ROW), :] = x

    def rounded(x):
        return x.astype(BF16).astype(F32)

    side = lax.broadcasted_iota(jnp.int32, (ROW, LANES), 0) // groups

    def bound(kind, i):
        x = jnp.full((ROW, LANES), near[kind, 0, i], jnp.int32)
        for span in range(1, spans):
            x = jnp.where(side == span, near[kind, span, i], x)
        return x

    def lead_short(ref, s, i0, off, r0, masked):
        xs = [tile(ref, i0 + off - short_w + 1 + k) for k in range(ROW + short_w - 1)]
        hs = [few[pl.ds((s * short_w + j) * ROW, ROW), :] for j in range(short_w)]
        res = []
        for b in range(ROW):
            total = hs[0] * xs[b + short_w - 1]
            if masked:
                far_b = bound(0, r0 + b)
                total = jnp.where(far_b >= 0, total, 0.0)
            for j in range(1, short_w):
                x = xs[b + short_w - 1 - j]
                if masked:
                    x = jnp.where(far_b >= j, x, 0.0)
                total = total + hs[j] * x
            res.append(total)
        return res

    lead = long_w

    def before(k, masked):
        i0 = k * ROW
        a = lead_short(s1, 1, i0, far - lead, i0, masked)
        for b in range(ROW):
            put(f1, i0 + b, a[b])
        d = lead_short(s2, 2, i0, far - lead, i0, masked)
        for b in range(ROW):
            put(f2, i0 + b, d[b])
            put(prod, i0 + b, rounded(a[b] * d[b]))

    def after(k, masked):
        i0 = k * ROW
        a = lead_short(s0, 0, i0, pad, i0 + lead, masked)
        for b in range(ROW):
            put(f0, i0 + b, a[b])
            put(back, i0 + b, rounded(tile(go, i0 + b) * a[b]))

    def pick(body, least, k):
        clear = limits[0, least] >= short_w - 1

        @pl.when(clear)
        def _():
            body(k, False)

        @pl.when(jnp.logical_not(clear))
        def _():
            body(k, True)

    count = (lead + seg + tail) // ROW
    lax.fori_loop(0, count, lambda k, _: (pick(before, k, k), 0)[1], 0)
    lax.fori_loop(0, count, lambda k, _: (pick(after, k + lead // ROW, k), 0)[1], 0)
    def differ(dst, ref):
        def step(k, _):
            for b in range(ROW):
                i = k * ROW + b
                x = [tile(ref, i + m) for m in (0, 4, 2, 6)]
                put(dst.at[0], i, x[0] - x[1])
                if LEAF < 4:
                    put(dst.at[1], i, x[0] - x[2])
                    put(dst.at[2], i, (x[0] - x[1]) - (x[2] - x[3]))
            return 0

        ref[pl.ds(count * ROW * ROW, ROW * ROW), :] = jnp.zeros((ROW * ROW, LANES), F32)
        lax.fori_loop(0, count, step, 0)

    differ(prod_less, prod)
    differ(back_less, back)

    def put_parts(ref, i, xs):
        parts = vector_parts(xs)
        for n, key in enumerate(KEYS):
            for m in range(LEAF):
                put(ref, (i * COUNT + n) * LEAF + m, parts[key][m])

    def tap_sums(k, _):
        put_parts(taps_sums, k, [tile(taps, k * ROW + j) for j in range(ROW)])
        return 0

    lax.fori_loop(0, long_w // ROW, tap_sums, 0)

    def products(kind, entry, vec):
        res = []
        for buf, start, key, _ in leaves(kind):
            n = KEYS.index(key)
            es = [entry(buf, start + m) for m in range(2 * LEAF - 1)]
            vs = [vec(n * LEAF + m) for m in range(LEAF)]
            for r in range(LEAF):
                total = None
                for m in range(LEAF):
                    at = {0: LEAF - 1 + r - m, 1: LEAF - 1 + m - r, 2: r + m}[kind]
                    term = es[at] * vs[m]
                    total = term if total is None else total + term
                res.append(total)
        return res

    def joined(kind, parts):
        res = [None] * ROW
        for n, (_, _, _, adds) in enumerate(leaves(kind)):
            for r, g in adds:
                for m in range(LEAF):
                    x = parts[n * LEAF + m]
                    at = r + m
                    if res[at] is None:
                        res[at] = x if g > 0 else -x
                    else:
                        res[at] = res[at] + x if g > 0 else res[at] - x
        return res

    def cached(ref, less):
        got = {}

        def entry_at(base):
            def entry(buf, m):
                if (buf, m) not in got:
                    got[buf, m] = tile(ref if buf == 0 else less.at[{1: 0, 2: 1, 3: 2}[buf]], base + m)
                return got[buf, m]
            return entry
        return entry_at

    def derived(xs):
        got = {(0, m): x for m, x in enumerate(xs)}

        def entry(buf, m):
            if (buf, m) not in got:
                low, step = {1: (0, 4), 2: (0, 2), 3: (1, 2)}[buf]
                got[buf, m] = entry(low, m) - entry(low, m + step)
            return got[buf, m]
        return entry

    acc[...] = jnp.zeros_like(acc)
    leaves_l[...] = jnp.zeros_like(leaves_l)
    zero = jnp.zeros((ROW, LANES), F32)

    def long_block(k, own):
        i0 = k * ROW
        if own:
            put_parts(seen, 0, [tile(back, i0 + b) for b in range(ROW)])
        size = COUNT * LEAF

        def before_window(j0):
            xs = [tile(prod, i0 + lead - j0 - ROW + 1 + m) for m in range(2 * ROW - 1)]
            reach = bound(0, i0 + lead) - j0
            return [jnp.where(reach >= ROW - 1 - m, x, 0.0) for m, x in enumerate(xs)]

        def after_window(j0):
            ys = [tile(back, i0 + j0 + m) for m in range(2 * ROW - 1)]
            room = bound(1, i0 + ROW - 1) + (ROW - 1 - j0)
            return [jnp.where(room >= m, y, 0.0) for m, y in enumerate(ys)]

        def ahead(jb, carry, masked):
            j0 = jb * ROW
            entry = derived(before_window(j0)) if masked else cached(prod, prod_less)(i0 + lead - j0 - ROW + 1)
            if own:
                olds = [tile(leaves_l, jb * size + n) for n in range(size)]
            parts = products(0, entry, lambda n: tile(taps_sums, jb * size + n))
            carry = tuple(c + x for c, x in zip(carry, parts))
            if own:
                parts = products(1, entry, lambda n: tile(seen, n))
                for n in range(size):
                    put(leaves_l, jb * size + n, olds[n] + parts[n])
            return carry

        def ahead_rows(jb, carry, first):
            j0 = jb * ROW
            reach = [bound(0, i0 + lead + b) - j0 for b in range(ROW)]
            hs = [tile(taps, j0 + j) for j in range(ROW)]
            if first:
                xs = [tile(prod, i0 + lead - j0 - ROW + 1 + m) for m in range(2 * ROW - 1)]
            else:
                xs = before_window(j0)
            total = [zero] * ROW
            if own:
                zs = [tile(back, i0 + b) for b in range(ROW)]
                if not first:
                    zs = [jnp.where(reach[b] >= 0, z, 0.0) for b, z in enumerate(zs)]
                parts = [tile(acc, j0 + j) for j in range(ROW)]
            for j in range(ROW):
                for b in range(ROW):
                    x = xs[b - j + ROW - 1]
                    if first:
                        x = jnp.where(reach[b] >= j, x, 0.0)
                    total[b] = total[b] + hs[j] * x
                    if own:
                        parts[j] = parts[j] + zs[b] * x
            if own:
                for j in range(ROW):
                    put(acc, j0 + j, parts[j])
            if not first:
                total = [jnp.where(reach[b] >= 0, x, 0.0) for b, x in enumerate(total)]
            return tuple(c + x for c, x in zip(carry, total))

        def behind(jb, carry, masked):
            j0 = jb * ROW
            entry = derived(after_window(j0)) if masked else cached(back, back_less)(i0 + j0)
            parts = products(2, entry, lambda n: tile(taps_sums, jb * size + n))
            return tuple(c + x for c, x in zip(carry, parts))

        def behind_rows(jb, carry, first):
            j0 = jb * ROW
            room = [bound(1, i0 + b) - j0 for b in range(ROW)]
            hs = [tile(taps, j0 + j) for j in range(ROW)]
            ys = [tile(back, i0 + j0 + m) for m in range(2 * ROW - 1)] if first else after_window(j0)
            total = [zero] * ROW
            for j in range(ROW):
                for b in range(ROW):
                    y = ys[b + j]
                    if first:
                        y = jnp.where(room[b] >= j, y, 0.0)
                    total[b] = total[b] + hs[j] * y
            if not first:
                total = [jnp.where(room[b] >= 0, x, 0.0) for b, x in enumerate(total)]
            return tuple(c + x for c, x in zip(carry, total))

        even = limits[4, k + lead // ROW] == 1

        def all_of(kind, low, high, at, whole, by_row):
            some = jnp.minimum((limits[high, at] + ROW) // ROW, long_w // ROW)
            full = jnp.where(even, jnp.minimum((limits[low, at] + 1) // ROW, long_w // ROW), 0)
            middle = jnp.where(even, some, 0)
            pairs = jnp.where(even, some, jnp.minimum(some, 1))
            total = lax.fori_loop(0, full, lambda j, c: whole(j, c, False), (zero,) * size)
            total = lax.fori_loop(full, middle, lambda j, c: whole(j, c, True), total)
            total = tuple(joined(kind, total))
            total = lax.fori_loop(middle, pairs, lambda j, c: by_row(j, c, True), total)
            return lax.fori_loop(pairs, some, lambda j, c: by_row(j, c, False), total)

        carry = all_of(0, 0, 1, k + lead // ROW, ahead, ahead_rows)
        grad = all_of(2, 2, 3, k, behind, behind_rows)
        for b in range(ROW):
            put(gf.at[0], i0 + b, rounded(tile(go, i0 + b) * carry[b]))
            put(gf.at[1], i0 + b, rounded(grad[b] * tile(f2, i0 + lead + b)))
            put(gf.at[2], i0 + b, rounded(grad[b] * tile(f1, i0 + lead + b)))
            if own:
                put(car, i0 + b, tile(f0, i0 + b) * carry[b])

    lax.fori_loop(0, seg // ROW, lambda k, _: (long_block(k, True), 0)[1], 0)
    for k in range(seg // ROW, (seg + tail) // ROW):
        long_block(k, False)

    def join_long(k, _):
        got = joined(1, [tile(leaves_l, k * COUNT * LEAF + n) for n in range(COUNT * LEAF)])
        for j in range(ROW):
            put(acc, k * ROW + j, tile(acc, k * ROW + j) + got[j])
        return 0

    lax.fori_loop(0, long_w // ROW, join_long, 0)

    def last(k, carry, s, src, off, masked):
        i0 = k * ROW
        ys = [tile(gf.at[s], i0 + m) for m in range(ROW + short_w - 1)]
        xs = [tile(src, i0 + off - short_w + 1 + m) for m in range(ROW + short_w - 1)]
        hs = [few[pl.ds((s * short_w + j) * ROW, ROW), :] for j in range(short_w)]
        parts = list(carry)
        for b in range(ROW):
            total = None
            if masked:
                room, reach = bound(1, i0 + b), bound(0, i0 + lead + b)
            for j in range(short_w):
                y, x = ys[b + j], xs[b + short_w - 1 - j]
                if masked:
                    y = jnp.where(room >= j, y, 0.0)
                    x = jnp.where(reach >= j, x, 0.0)
                total = hs[j] * y if total is None else total + hs[j] * y
                parts[j] = parts[j] + ys[b] * x
            put(out.at[s], i0 + b, total)
        return tuple(parts)

    for s, src, off in ((0, s0, pad), (1, s1, far), (2, s2, far)):
        def step(k, carry, s=s, src=src, off=off):
            least = jnp.minimum(limits[0, k + lead // ROW], limits[2, k])
            return lax.cond(
                least >= short_w - 1,
                lambda: last(k, carry, s, src, off, False),
                lambda: last(k, carry, s, src, off, True),
            )

        parts = lax.fori_loop(0, seg // ROW, step, (zero,) * short_w)
        for j in range(short_w):
            put(acc, long_w + s * ROW + j, parts[j])

    total_rows = acc.shape[0] // ROW
    for g in range(groups):
        c = slice(g * LANES, (g + 1) * LANES)
        total = None
        for span in range(spans):
            r = span * groups + g
            own = pl.ds(span * seg, seg)
            gated[own, c] = car[pl.ds(r, seg, stride=ROW), :].astype(BF16)
            for s in range(3):
                mixed[s, own, c] = out[s, pl.ds(r, seg, stride=ROW), :].astype(BF16)
            x = acc[pl.ds(r, total_rows, stride=ROW), :]
            total = x if total is None else total + x
        sums[:, c] = total.astype(BF16)


def conv_block(proj, up12, up0, down0, down12, grad_out, short_taps, long_taps, contig_lengths):
    _, rows, chans = proj.shape
    short_w, long_w = short_taps.shape[1], long_taps.shape[0]
    far, pad = up12.shape[1], up0.shape[0]
    groups = chans // LANES
    spans = ROW // groups
    seg, tail = rows // spans, ROW
    lead = long_w

    offset = lax.axis_index("ctx") // 2 * rows
    order = jnp.arange(contig_lengths.shape[0], dtype=jnp.int32)
    ends = jnp.sum(jnp.where(order[None, :] <= order[:, None], contig_lengths[None, :], 0), axis=1)
    begins = ends - contig_lengths
    span = jnp.arange(spans, dtype=jnp.int32) * seg
    count = lead + seg + tail + lead
    at = offset - lead + jnp.arange(count, dtype=jnp.int32)[:, None] + span[None, :]
    first = jnp.max(jnp.where(begins[None, None, :] <= at[:, :, None], begins[None, None, :], 0), axis=2)
    reach = at - first
    here = at[lead : lead + seg + tail]
    end = jnp.min(jnp.where(ends[None, None, :] > here[:, :, None], ends[None, None, :], jnp.int32(2**30)), axis=2)
    room = end - 1 - here

    near = jnp.stack([reach.T, jnp.pad(room.T, ((0, 0), (0, count - room.shape[0])))])

    def blocks(x, how):
        return jnp.pad(how(x.reshape(-1, ROW * spans), axis=1), (0, (count - x.shape[0]) // ROW))

    limits = jnp.stack([
        blocks(reach, jnp.min), blocks(reach, jnp.max), blocks(room, jnp.min), blocks(room, jnp.max),
        jnp.all(reach[ROW - 1 :: ROW] - reach[::ROW] == ROW - 1, axis=1).astype(jnp.int32),
    ])

    def vmem(n):
        return pltpu.VMEM((n * ROW, LANES), F32)

    dims = (rows, far, pad, short_w, long_w, spans, groups, seg, tail)
    size = lead + seg + tail
    in_vmem = pl.BlockSpec(memory_space=pltpu.VMEM)
    return pl.pallas_call(
        lambda *refs: conv_kernel(dims, *refs),
        in_specs=[pl.BlockSpec(memory_space=pltpu.SMEM)] * 2 + [in_vmem] * 8,
        out_specs=[in_vmem] * 3,
        out_shape=[
            jax.ShapeDtypeStruct((rows, chans), BF16),
            jax.ShapeDtypeStruct((3, rows, chans), BF16),
            jax.ShapeDtypeStruct((long_w + 4 * ROW, chans), BF16),
        ],
        scratch_shapes=[
            vmem(pad + seg + far), vmem(far + seg + pad), vmem(far + seg + pad), vmem(seg + far),
            vmem(size), vmem(size), vmem(size), vmem(size + ROW), vmem(size + ROW),
            pltpu.VMEM((3, size * ROW, LANES), F32), pltpu.VMEM((3, size * ROW, LANES), F32),
            vmem(long_w // ROW * COUNT * LEAF), vmem(COUNT * LEAF), vmem(seg + tail),
            pltpu.VMEM((3, (seg + 2 * tail) * ROW, LANES), F32),
            vmem(long_w + 4 * ROW), vmem(long_w), vmem(long_w // ROW * COUNT * LEAF), vmem(3 * short_w),
            pltpu.VMEM((3, seg * ROW, LANES), F32),
        ],
        compiler_params=pltpu.CompilerParams(vmem_limit_bytes=56 << 20),
        cost_estimate=pl.CostEstimate(
            flops=rows * chans * long_w * 1000, bytes_accessed=rows * chans * 24, transcendentals=0
        ),
        name="hyena_filters",
    )(limits, near, proj, up12, up0, down0, down12, grad_out, short_taps, long_taps)


def on_device(loaded, slot_pos, contig_lengths, w_in, short_taps, long_taps, grad_out):
    me = lax.axis_index("ctx")
    core = me % 2
    chans = grad_out.shape[1]
    short_w, long_w = short_taps.shape[1], long_taps.shape[0]
    far, pad = round_up(long_w, 16) + 16, 16
    n_ctx = lax.axis_size("ctx")

    short_c, long_c = half(short_taps, 2, core), half(long_taps, 1, core)
    proj, up12, up0, down0, down12, grad_c, wall, *turned = gather(
        jnp.transpose(w_in, (1, 0, 2)), loaded[0], slot_pos, grad_out, far, pad
    )
    turned = [swapped(x, 2 * m) if m else x for m, x in enumerate(turned)]
    gated, grads, sums = conv_block(
        proj, up12, up0, down0, down12, grad_c, short_c, long_c, contig_lengths
    )
    weight_grads, token_grads, gated_out, filters = reduce(grads, wall, gated, sums, turned)
    long_total = filters[:long_w]
    short_total = filters[long_w : long_w + 24].reshape(3, 8, chans)[:, :short_w]
    return gated_out, token_grads, jnp.transpose(weight_grads, (1, 0, 2)), short_total, long_total


def solution(mesh):
    in_specs = (
        P("ctx", None, None, "fsdp"),
        P("ctx", None, None),
        P(),
        P("ctx", None, "fsdp"),
        P(None, None, "fsdp"),
        P(None, "fsdp"),
        P("ctx", "fsdp"),
    )
    out_specs = (
        P("ctx", "fsdp"),
        P("ctx", "fsdp"),
        P("ctx", None, "fsdp"),
        P(None, None, "fsdp"),
        P(None, "fsdp"),
    )
    return jax.shard_map(
        on_device, mesh=mesh, in_specs=in_specs, out_specs=out_specs, check_vma=False
    )
```

```python
import jax
import jax.numpy as jnp
from jax import lax
from jax.experimental import pallas as pl
from jax.experimental.pallas import tpu as pltpu
from jax.sharding import PartitionSpec as P

LANES = 128
F32, BF16 = jnp.float32, jnp.bfloat16


def round_up(x, to):
    return -(-x // to) * to


def swapped(x, mask):
    size = lax.axis_size("ctx")
    return lax.ppermute(x, "ctx", [(i, i ^ mask) for i in range(size)])


def chip_masks(size):
    masks, step = [], 2
    while step < size:
        masks.append(step)
        step *= 2
    return masks


def walk(masks):
    held = [0]
    for mask in masks:
        held = held + [k ^ mask for k in held]
    return held


def half(x, dim, which):
    width = x.shape[dim] // 2
    return lax.dynamic_slice_in_dim(x, which * width, width, dim)


def remote(src, dst, send, recv, **place):
    return pltpu.make_async_remote_copy(
        src_ref=src, dst_ref=dst, send_sem=send, recv_sem=recv,
        device_id=place, device_id_type=pl.DeviceIdType.MESH,
    )


def local(src, dst, sem):
    return pltpu.make_async_copy(src, dst, sem)


def at_cols(start, size):
    return pl.ds(pl.multiple_of(start, LANES), size)


def greet(n_ctx, n_line):
    me, z = lax.axis_index("ctx"), lax.axis_index("fsdp")
    barrier = pltpu.get_barrier_semaphore()
    others = [1] + [k for k in range(2, n_ctx, 2)]
    for k in others:
        pl.semaphore_signal(
            barrier, inc=1, device_id={"ctx": me ^ k}, device_id_type=pl.DeviceIdType.MESH
        )

    @pl.when(z > 0)
    def _():
        pl.semaphore_signal(
            barrier, inc=1, device_id={"fsdp": z - 1}, device_id_type=pl.DeviceIdType.MESH
        )

    @pl.when(z < n_line - 1)
    def _():
        pl.semaphore_signal(
            barrier, inc=1, device_id={"fsdp": z + 1}, device_id_type=pl.DeviceIdType.MESH
        )

    ends = jnp.where(z > 0, 1, 0) + jnp.where(z < n_line - 1, 1, 0)
    pl.semaphore_wait(barrier, len(others) + ends)


class Spread:
    def __init__(self, buf, send, recv, masks, me):
        self.buf, self.send, self.recv, self.me = buf, send, recv, me
        self.orders = (masks, masks[::-1])
        self.keys = tuple(walk(m) for m in self.orders)
        self.count = 1 << len(masks)

    def copy(self, chain, stage, i):
        to = (1 << stage) + i
        return remote(
            self.buf.at[chain, i], self.buf.at[chain, to],
            self.send.at[chain, to], self.recv.at[chain, to],
            ctx=self.me ^ self.orders[chain][stage],
        )

    def stages(self, i):
        return range(i.bit_length(), len(self.orders[0]))

    def start(self, chain, i, stages=None):
        for stage in self.stages(i) if stages is None else stages:
            self.copy(chain, stage, i).start()

    def arrive(self, chain, i):
        stage = i.bit_length() - 1
        self.copy(chain, stage, i - (1 << stage)).wait_recv()

    def finish(self):
        for chain in (0, 1):
            for i in range(self.count):
                for stage in self.stages(i):
                    self.copy(chain, stage, i).wait_send()


def gather_kernel(
    sizes, w, slots, pos, grad,
    proj, up12, up0, down0, down12, gext, wall, *rest
):
    n_ctx, n, far, pad = sizes
    turned, rest = rest[: n_ctx // 2], rest[n_ctx // 2 :]
    gather_body(n_ctx, n, far, pad, w, slots, pos, grad, proj, up12, up0, down0, down12, gext, wall, turned, *rest)


def gather_body(
    n_ctx, n, far, pad, w, slots, pos, grad,
    proj, up12, up0, down0, down12, gext, wall, turned,
    tbuf, wbuf, xbuf, sbuf, pbuf, part, ppart, acc,
    w_send, w_recv, s_send, s_recv, up_send, up_recv, dn_send, dn_recv,
    core_send, core_recv, misc_send, misc_recv, local_sem, out_sem, halo_send, halo_recv, turn_sem,
):
    me, z = lax.axis_index("ctx"), lax.axis_index("fsdp")
    core, chip = me % 2, me // 2
    chips = n_ctx // 2
    rows, dz = ppart.shape
    streams, feats, ch = wbuf.shape[2:]
    masks = chip_masks(n_ctx)
    greet(n_ctx, n)

    sib = me ^ 1
    own_pos = local(pos.at[0], pbuf.at[core], local_sem.at[0])
    own_pos.start()
    send_pos = remote(pos.at[0], pbuf.at[core], misc_send.at[0], misc_recv.at[0], ctx=sib)
    send_pos.start()
    own_slots = local(slots.at[pl.ds(2 * chip, 2)], sbuf.at[chip], local_sem.at[1])
    own_slots.start()
    deals = []
    for k in range(2, n_ctx, 2):
        to = me ^ k
        deals.append(remote(
            slots.at[pl.ds(to - core, 2)], sbuf.at[chip], s_send.at[k // 2], s_recv.at[k // 2], ctx=to
        ))
        deals[-1].start()
    own_w = local(w.at[:, :, at_cols(core * ch, ch)], wbuf.at[0, 0], local_sem.at[2])
    own_w.start()
    send_w = remote(
        w.at[:, :, at_cols((1 - core) * ch, ch)], wbuf.at[1, 0], misc_send.at[1], misc_recv.at[1], ctx=sib
    )
    send_w.start()
    own_rows = pl.ds(pl.multiple_of(core * rows, rows), rows)
    own_grad = local(grad.at[:, at_cols(core * ch, ch)], gext.at[own_rows], local_sem.at[3])
    own_grad.start()
    send_grad = remote(
        grad.at[:, at_cols((1 - core) * ch, ch)], gext.at[own_rows], misc_send.at[3], misc_recv.at[3], ctx=sib
    )
    send_grad.start()
    spread = Spread(wbuf, w_send, w_recv, masks, me)
    stages = len(masks)
    keep = []

    def stored(chain, i):
        keep.append(local(wbuf.at[chain, i], wall.at[chain, i], out_sem.at[chain, i]))
        keep[-1].start()

    own_w.wait()
    spread.start(0, 0, range(0, min(1, stages)))
    stored(0, 0)
    send_w.wait_recv()
    spread.start(1, 0, range(0, min(1, stages)))
    stored(1, 0)

    own_pos.wait()
    send_pos.wait_recv()
    own_slots.wait()
    for deal in deals:
        deal.wait_recv()
    spread.start(0, 0, range(1, stages))
    spread.start(1, 0, range(1, stages))

    seat = lax.broadcasted_iota(jnp.int32, (rows, pos.shape[2]), 0)

    def place(b):
        total = None
        for c in range(chips):
            row = pbuf[b, pl.ds(2 * c + core, 1), :]
            pick = jnp.where(row == seat, 1.0, 0.0).astype(BF16)
            term = jnp.dot(pick, sbuf[c, b], preferred_element_type=F32)
            total = term if total is None else total + term
        return total.astype(BF16)

    part[...] = place(1 - core)
    give = remote(part, ppart, misc_send.at[2], misc_recv.at[2], ctx=sib)
    give.start()
    mine = place(core)
    give.wait_recv()
    own_grad.wait()
    send_grad.wait_recv()
    edge_grad = remote(
        gext.at[pl.ds(0, far)], gext.at[pl.ds(2 * rows, far)], misc_send.at[4], misc_recv.at[4], ctx=me - 2
    )

    @pl.when(chip > 0)
    def _():
        edge_grad.start()

    xbuf[own_rows, at_cols(z * dz, dz)] = mine + ppart[...]

    def tile(t):
        return xbuf.at[own_rows, at_cols(t * dz, dz)]

    def to_core(t):
        return remote(tile(t), tile(t), core_send.at[t], core_recv.at[t], ctx=sib)

    def other_tile(t):
        there = xbuf.at[pl.ds(pl.multiple_of((1 - core) * rows, rows), rows), at_cols(t * dz, dz)]
        return remote(there, there, core_send.at[t], core_recv.at[t], ctx=sib)

    def up(h, t):
        return remote(tile(t), tile(t), up_send.at[h], up_recv.at[h], fsdp=z + 1)

    def down(h, t):
        return remote(tile(t), tile(t), dn_send.at[h], dn_recv.at[h], fsdp=z - 1)

    to_core(z).start()
    for h in range(1, n):
        @pl.when((z < n - 1) & (z - h + 1 >= 0))
        def _():
            up(h, z - h + 1).start()

        @pl.when((z > 0) & (z + h - 1 <= n - 1))
        def _():
            down(h, z + h - 1).start()

        @pl.when(z - h >= 0)
        def _():
            up(h, z - h).wait_recv()
            to_core(z - h).start()

        @pl.when(z + h <= n - 1)
        def _():
            down(h, z + h).wait_recv()
            to_core(z + h).start()

        if h == 1 and spread.count > 1:
            for chain in (0, 1):
                spread.arrive(chain, 1)
                spread.start(chain, 1)
                stored(chain, 1)
    for t in range(n):
        other_tile(t).wait_recv()
    for m in range(chips):
        tbuf[m] = xbuf[:, at_cols((me ^ (2 * m)) * feats, feats)].T
        keep.append(local(tbuf.at[m], turned[m], turn_sem.at[m]))
        keep[-1].start()

    for i in range(spread.count):
        for chain in (0, 1):
            if i > 1:
                spread.arrive(chain, i)
                spread.start(chain, i)
                stored(chain, i)
            block = me ^ chain ^ spread.keys[chain][i]
            cols = at_cols(block * feats, feats)
            first, last = (i == 0 and chain == 0), (i == spread.count - 1 and chain == 1)

            def one(s, _, chain=chain, i=i, cols=cols, first=first, last=last):
                total = jnp.dot(xbuf[:, cols], wbuf[chain, i, s], preferred_element_type=F32)
                if not first:
                    total = total + acc[s]
                if last:
                    proj[s] = total.astype(BF16)
                else:
                    acc[s] = total
                return 0

            lax.fori_loop(0, streams, one, 0)

    total = 2 * rows

    def halos(up_to, down_to):
        return (
            remote(proj.at[pl.ds(1, 2), pl.ds(total - far, far)], up12, halo_send.at[0], halo_recv.at[0], ctx=up_to),
            remote(proj.at[0, pl.ds(total - pad, pad)], up0, halo_send.at[1], halo_recv.at[1], ctx=up_to),
            remote(proj.at[0, pl.ds(0, far)], down0, halo_send.at[2], halo_recv.at[2], ctx=down_to),
            remote(proj.at[pl.ds(1, 2), pl.ds(0, pad)], down12, halo_send.at[3], halo_recv.at[3], ctx=down_to),
        )

    edges = halos(me + 2, me - 2)

    @pl.when(chip < chips - 1)
    def _():
        edges[0].start()
        edges[1].start()

    @pl.when(chip > 0)
    def _():
        edges[2].start()
        edges[3].start()

    @pl.when(chip == 0)
    def _():
        up12[...] = jnp.zeros_like(up12)
        up0[...] = jnp.zeros_like(up0)

    @pl.when(chip == chips - 1)
    def _():
        gext[pl.ds(2 * rows, far), :] = jnp.zeros((far, ch), BF16)
        down0[...] = jnp.zeros_like(down0)
        down12[...] = jnp.zeros_like(down12)

    @pl.when(chip > 0)
    def _():
        edges[0].wait_recv()
        edges[1].wait_recv()
        edges[2].wait_send()
        edges[3].wait_send()
        edge_grad.wait_send()

    @pl.when(chip < chips - 1)
    def _():
        edges[2].wait_recv()
        edges[3].wait_recv()
        edge_grad.wait_recv()
        edges[0].wait_send()
        edges[1].wait_send()

    for h in range(1, n):
        @pl.when((z < n - 1) & (z - h + 1 >= 0))
        def _():
            up(h, z - h + 1).wait_send()

        @pl.when((z > 0) & (z + h - 1 <= n - 1))
        def _():
            down(h, z + h - 1).wait_send()
    for t in range(n):
        to_core(t).wait_send()
    for deal in deals + [send_pos, send_w, send_grad, give]:
        deal.wait_send()
    spread.finish()
    for copy in keep:
        copy.wait()


def gather(w, slots, pos, grad, far, pad):
    n_ctx, n = lax.axis_size("ctx"), lax.axis_size("fsdp")
    chips = n_ctx // 2
    streams, feats, two = w.shape
    ch, dz = two // 2, slots.shape[2]
    rows = grad.shape[0]
    total = 2 * rows
    any_space, vmem = pl.BlockSpec(memory_space=pl.ANY), pl.BlockSpec(memory_space=pltpu.VMEM)
    dma = pltpu.SemaphoreType.DMA

    def shape(*dims):
        return jax.ShapeDtypeStruct(dims, BF16)

    return pl.pallas_call(
        lambda *refs: gather_kernel((n_ctx, n, far, pad), *refs),
        in_specs=[any_space] * 4,
        out_specs=[vmem] * 6 + [any_space] * (1 + chips),
        out_shape=[
            shape(streams, total, ch), shape(2, far, ch), shape(pad, ch), shape(far, ch), shape(2, pad, ch),
            shape(total + far, ch),
            shape(2, chips, streams, feats, ch),
        ] + [shape(feats, total)] * chips,
        scratch_shapes=[
            pltpu.VMEM((chips, feats, total), BF16),
            pltpu.VMEM((2, chips, streams, feats, ch), BF16),
            pltpu.VMEM((total, n * dz), BF16),
            pltpu.VMEM((chips, 2, slots.shape[1], dz), BF16),
            pltpu.VMEM((2, *pos.shape[1:]), jnp.int32),
            pltpu.VMEM((rows, dz), BF16),
            pltpu.VMEM((rows, dz), BF16),
            pltpu.VMEM((streams, total, ch), F32),
            dma((2, chips)), dma((2, chips)), dma((chips,)), dma((chips,)),
            dma((n,)), dma((n,)), dma((n,)), dma((n,)),
            dma((n,)), dma((n,)), dma((5,)), dma((5,)), dma((4,)), dma((2, chips)), dma((4,)), dma((4,)), dma((chips,)),
        ],
        compiler_params=pltpu.CompilerParams(
            collective_id=0, has_side_effects=True, vmem_limit_bytes=56 << 20
        ),
        cost_estimate=pl.CostEstimate(
            flops=2 * total * n * dz * streams * ch, bytes_accessed=40 << 20, transcendentals=0
        ),
        name="gather_and_project",
    )(w, slots, pos, grad)


def reduce_kernel(
    sizes, grads, wall, gated, sums, *rest
):
    chips = sizes[0] // 2
    reduce_body(sizes, grads, wall, gated, sums, rest[:chips], *rest[chips:])


def reduce_body(
    sizes, grads, wall, gated, sums, turned,
    wg, tg, gout, filt,
    gbuf, lbuf, acc, wgb, wv, xp, xs, xr, up_tx, up_rx, dn_tx, dn_rx, fbuf, ftot,
    g_send, g_recv, f_send, f_recv, up_send, up_recv, dn_send, dn_recv,
    core_send, core_recv, misc_send, misc_recv, local_sem, wv_sem, t_sem, t_send, t_recv,
):
    n_ctx, n = sizes
    me, z = lax.axis_index("ctx"), lax.axis_index("fsdp")
    core, chip = me % 2, me // 2
    chips = n_ctx // 2
    streams, rows, ch = gbuf.shape[2:]
    feats = lbuf.shape[1]
    dz = xp.shape[1] // n
    masks = chip_masks(n_ctx)
    sib = me ^ 1
    own_g = [
        local(grads.at[:, pl.ds(b * rows, rows)], gbuf.at[b, 0], local_sem.at[b]) for b in (0, 1)
    ]
    for copy in own_g:
        copy.start()
    spread = Spread(gbuf, g_send, g_recv, masks, me)
    wkeys = (walk(masks), walk(masks[::-1]))
    order = [(chain, i) for i in range(chips) for chain in (0, 1)]

    def fetch(j):
        chain, i = order[j]
        return local(wall.at[chain, i], wv.at[j % 2], wv_sem.at[j % 2])

    fetch(0).start()
    lefts, trades = [], []
    for m in range(chips):
        cols = at_cols(((me - core) ^ (2 * m)) * rows, 2 * rows)
        lefts.append(local(turned[m], lbuf.at[0, :, cols], t_sem.at[m]))
        trades.append(remote(turned[m], lbuf.at[1, :, cols], t_send.at[m], t_recv.at[m], ctx=sib))
        lefts[-1].start()
    greet(n_ctx, n)
    for copy in own_g:
        copy.wait()
    for chain in (0, 1):
        spread.start(chain, 0)
    for trade in trades:
        trade.start()

    fbuf[chip] = sums[...]
    shares = []
    for k in range(2, n_ctx, 2):
        shares.append(remote(
            fbuf.at[chip], fbuf.at[chip], f_send.at[k // 2], f_recv.at[k // 2], ctx=me ^ k
        ))
    mine = at_cols(core * ch, ch)
    keep_gated = local(gated.at[pl.ds(core * rows, rows)], gout.at[:, mine], local_sem.at[3])
    give_gated = remote(
        gated.at[pl.ds((1 - core) * rows, rows)], gout.at[:, mine], misc_send.at[0], misc_recv.at[0], ctx=sib
    )
    keep_gated.start()
    give_gated.start()

    def to_core(block):
        cols = at_cols(block * feats, feats)
        return remote(xs.at[:, cols], xr.at[:, cols], core_send.at[block], core_recv.at[block], ctx=sib)

    for j, (chain, i) in enumerate(order):
        if j + 1 < len(order):
            fetch(j + 1).start()
        fetch(j).wait()
        block = me ^ chain ^ wkeys[chain][i]
        cols = at_cols(block * feats, feats)

        def back(b, j=j):
            total = None
            for s in range(streams):
                term = lax.dot_general(
                    gbuf[b, 0, s], wv[j % 2, s], (((1,), (1,)), ((), ())), preferred_element_type=F32
                )
                total = term if total is None else total + term
            return total

        xs[:, cols] = back(1 - core).astype(BF16)
        to_core(block).start()
        xp[:, cols] = back(core)

    step = 32

    def each(body):
        def one(r, _):
            body(pl.ds(pl.multiple_of(r * step, step), step))
            return 0

        lax.fori_loop(0, rows // step, one, 0)

    def weigh(chain, i, halves=(0, 1), end=False):
        where = ((me - core) ^ spread.keys[chain][i]) + chain
        cols = at_cols(where * rows, rows)
        first = i == 0 and chain == 0

        def one(r, _):
            h, s = r // streams, r % streams
            total = jnp.dot(lbuf[h, :, cols], gbuf[chain, i, s], preferred_element_type=F32)
            if not first:
                total = acc[r] + total
            if end:
                wgb[r] = total.astype(BF16)
            else:
                acc[r] = total
            return 0

        lax.fori_loop(halves[0] * streams, (halves[-1] + 1) * streams, one, 0)

    for block in range(n_ctx):
        to_core(block).wait_recv()
    for left, trade in zip(lefts, trades):
        left.wait()
        trade.wait_recv()

    def up(s):
        return remote(up_tx.at[s - 1], up_rx.at[s - 1], up_send.at[s], up_recv.at[s], fsdp=z + 1)

    def down(s):
        return remote(dn_tx.at[s - 1], dn_rx.at[s - 1], dn_send.at[s], dn_recv.at[s], fsdp=z - 1)

    zz = n - 1 - z

    def send_tile(s, a, far_end, tx, rx):
        cols = at_cols(a * dz, dz)

        @pl.when(far_end == 0)
        def _():
            def body(at):
                tx[s - 1, at] = (xp[at, cols] + xr[at, cols].astype(F32)).astype(BF16)
            each(body)

        if s >= 2:
            @pl.when(far_end > 0)
            def _():
                def body(at):
                    total = xp[at, cols] + xr[at, cols].astype(F32) + rx[s - 2, at].astype(F32)
                    tx[s - 1, at] = total.astype(BF16)
                each(body)

    def line_start(s):
        last = min(s - 1, n - 2)

        @pl.when(z <= last)
        def _():
            send_tile(s, n - s + z, z, up_tx, up_rx)
            up(s).start()

        @pl.when(zz <= last)
        def _():
            send_tile(s, z + s - n, zz, dn_tx, dn_rx)
            down(s).start()

    def line_wait(s):
        last = min(s - 1, n - 2)

        @pl.when((z >= 1) & (z - 1 <= last))
        def _():
            up(s).wait_recv()

        @pl.when((zz >= 1) & (zz - 1 <= last))
        def _():
            down(s).wait_recv()

    if n > 1:
        line_start(1)
    sent = 1
    for i in range(spread.count):
        for chain in (0, 1):
            if i:
                spread.arrive(chain, i)
                spread.start(chain, i)
        if i == spread.count - 1:
            break
        for chain in (0, 1):
            weigh(chain, i)
        if i >= 1 and sent < n - 1:
            line_wait(sent)
            sent += 1
            line_start(sent)
    for share in shares:
        share.start()
    give_w = remote(
        wgb.at[pl.ds(streams, streams)], wg.at[:, :, mine], misc_send.at[1], misc_recv.at[1], ctx=sib
    )
    keep_w = local(wgb.at[pl.ds(0, streams)], wg.at[:, :, mine], local_sem.at[4])
    for h, copy in ((1, give_w), (0, keep_w)):
        weigh(0, spread.count - 1, (h,))
        weigh(1, spread.count - 1, (h,), end=True)
        copy.start()
    while sent < n - 1:
        line_wait(sent)
        sent += 1
        line_start(sent)

    for share in shares:
        share.wait_recv()
    total = fbuf[0].astype(F32)
    for c in range(1, chips):
        total = total + fbuf[c].astype(F32)
    ftot[...] = total
    give_f = remote(ftot, filt.at[:, mine], misc_send.at[2], misc_recv.at[2], ctx=sib)
    give_f.start()
    keep_f = local(ftot, filt.at[:, mine], local_sem.at[5])
    keep_f.start()

    if n > 1:
        line_wait(n - 1)
    cols = at_cols(z * dz, dz)

    def final(at):
        acc_t = xp[at, cols] + xr[at, cols].astype(F32)
        if n > 1:
            acc_t = acc_t + jnp.where(z >= 1, up_rx[n - 2, at].astype(F32), 0.0)
            acc_t = acc_t + jnp.where(zz >= 1, dn_rx[n - 2, at].astype(F32), 0.0)
        tg[at] = acc_t.astype(BF16)

    each(final)

    for s in range(1, n):
        last = min(s - 1, n - 2)

        @pl.when(z <= last)
        def _():
            up(s).wait_send()

        @pl.when(zz <= last)
        def _():
            down(s).wait_send()
    for block in range(n_ctx):
        to_core(block).wait_send()
    spread.finish()
    for share in shares:
        share.wait_send()
    for trade in trades:
        trade.wait_send()
    for copy in (give_gated, give_w, give_f):
        copy.wait()
    for copy in (keep_gated, keep_w, keep_f):
        copy.wait()


def reduce(grads, wall, gated, sums, turned):
    n_ctx, n = lax.axis_size("ctx"), lax.axis_size("fsdp")
    chips = n_ctx // 2
    streams, total, ch = grads.shape
    rows = total // 2
    feats = turned[0].shape[0]
    dim = feats * n_ctx
    dz = dim // n
    any_space, vmem = pl.BlockSpec(memory_space=pl.ANY), pl.BlockSpec(memory_space=pltpu.VMEM)
    dma = pltpu.SemaphoreType.DMA
    hops = max(n - 1, 1)
    return pl.pallas_call(
        lambda *refs: reduce_kernel((n_ctx, n), *refs),
        in_specs=[any_space] * 3 + [vmem] + [any_space] * chips,
        out_specs=[any_space, vmem, any_space, any_space],
        out_shape=[
            jax.ShapeDtypeStruct((streams, feats, 2 * ch), BF16),
            jax.ShapeDtypeStruct((rows, dz), BF16),
            jax.ShapeDtypeStruct((rows, 2 * ch), BF16),
            jax.ShapeDtypeStruct((sums.shape[0], 2 * ch), F32),
        ],
        scratch_shapes=[
            pltpu.VMEM((2, chips, streams, rows, ch), BF16),
            pltpu.VMEM((2, feats, rows * n_ctx), BF16),
            pltpu.VMEM((2 * streams, feats, ch), F32),
            pltpu.VMEM((2 * streams, feats, ch), BF16),
            pltpu.VMEM((2, streams, feats, ch), BF16),
            pltpu.VMEM((rows, dim), F32),
            pltpu.VMEM((rows, dim), BF16),
            pltpu.VMEM((rows, dim), BF16),
            pltpu.VMEM((hops, rows, dz), BF16), pltpu.VMEM((hops, rows, dz), BF16),
            pltpu.VMEM((hops, rows, dz), BF16), pltpu.VMEM((hops, rows, dz), BF16),
            pltpu.VMEM((chips, *sums.shape), BF16),
            pltpu.VMEM(sums.shape, F32),
            dma((2, chips)), dma((2, chips)), dma((chips,)), dma((chips,)),
            dma((n,)), dma((n,)), dma((n,)), dma((n,)),
            dma((n_ctx,)), dma((n_ctx,)), dma((3,)), dma((3,)), dma((6,)), dma((2,)),
            dma((chips,)), dma((chips,)), dma((chips,)),
        ],
        compiler_params=pltpu.CompilerParams(
            collective_id=1, has_side_effects=True, vmem_limit_bytes=60 << 20
        ),
        cost_estimate=pl.CostEstimate(
            flops=4 * total * dim * streams * ch, bytes_accessed=40 << 20, transcendentals=0
        ),
        name="gather_and_reduce",
    )(grads, wall, gated, sums, *turned)


ROW = 8
LEAF = 2


def leaves(kind, size=ROW, buf=0, start=0, vec=(0, ROW), sign=1, rows=(0, ROW)):
    def split(size, buf, start, vec, adds):
        if size == LEAF:
            yield buf, start, vec, adds
            return
        h = size // 2
        step = {8: 1, 4: 2}[size]
        low, high, both = vec + (0,), vec + (1,), vec + (2,)
        yield from split(h, buf, start + h, both, adds + [(r + h, g) for r, g in adds])
        first = [(r, g) for r, g in adds]
        second = [(r + h, g) for r, g in adds]
        minus = lambda adds: [(r, -g) for r, g in adds]
        if kind == 0:
            yield from split(h, buf + step, start, high, first)
            yield from split(h, buf + step, start + h, low, minus(second))
        elif kind == 1:
            yield from split(h, buf + step, start + h, high, minus(first))
            yield from split(h, buf + step, start, low, second)
        else:
            yield from split(h, buf + step, start, low, first)
            yield from split(h, buf + step, start + h, high, minus(second))
    return list(split(ROW, 0, 0, (), [(0, 1)]))


def vector_parts(xs):
    parts = {(): xs}
    size = len(xs)
    while size > LEAF:
        size //= 2
        parts = {
            k + (m,): y
            for k, v in parts.items()
            for m, y in ((0, v[:size]), (1, v[size:]), (2, [a + b for a, b in zip(v[:size], v[size:])]))
        }
    return parts


KEYS = sorted(vector_parts([0] * ROW))
COUNT = len(KEYS)


def conv_kernel(
    dims, limits, near, proj, up12, up0, down0, down12, grads, short, long,
    gated, mixed, sums,
    s0, s1, s2, go, f0, f1, f2, prod, back, prod_less, back_less, leaves_l, seen, car, gf, acc, taps, taps_sums, few, out,
):
    rows, far, pad, short_w, long_w, spans, groups, seg, tail = dims

    def spread_rows(dst, at, pieces):
        size = dst.shape[0] // ROW
        for span in range(spans):
            base = span * seg + at
            for start, count, read in pieces:
                low, high = max(base, start), min(base + size, start + count)
                if low >= high:
                    continue
                for g in range(groups):
                    x = read(low - start, high - low, slice(g * LANES, (g + 1) * LANES)).astype(F32)
                    dst[pl.ds((low - base) * ROW + span * groups + g, high - low, stride=ROW), :] = x

    def piece(ref, start, *lead):
        return start, ref.shape[-2], lambda r, n, c: ref[(*lead, slice(r, r + n), c)]

    spread_rows(s0, -pad, [piece(up0, -pad), piece(proj, 0, 0), piece(down0, rows)])
    for k, dst in ((0, s1), (1, s2)):
        spread_rows(dst, -far, [piece(up12, -far, k), piece(proj, 0, 1 + k), piece(down12, rows, k)])
    spread_rows(go, 0, [piece(grads, 0)])
    for span in range(spans):
        for g in range(groups):
            c = slice(g * LANES, (g + 1) * LANES)
            taps[pl.ds(span * groups + g, long_w, stride=ROW), :] = long[:, c]
            for s in range(3):
                few[pl.ds(s * short_w * ROW + span * groups + g, short_w, stride=ROW), :] = short[s, :, c]

    def tile(ref, i):
        return ref[pl.ds(pl.multiple_of(i * ROW, ROW), ROW), :]

    def put(ref, i, x):
        ref[pl.ds(pl.multiple_of(i * ROW, ROW), ROW), :] = x

    def rounded(x):
        return x.astype(BF16).astype(F32)

    side = lax.broadcasted_iota(jnp.int32, (ROW, LANES), 0) // groups

    def bound(kind, i):
        x = jnp.full((ROW, LANES), near[kind, 0, i], jnp.int32)
        for span in range(1, spans):
            x = jnp.where(side == span, near[kind, span, i], x)
        return x

    def lead_short(ref, s, i0, off, r0, masked):
        xs = [tile(ref, i0 + off - short_w + 1 + k) for k in range(ROW + short_w - 1)]
        hs = [few[pl.ds((s * short_w + j) * ROW, ROW), :] for j in range(short_w)]
        res = []
        for b in range(ROW):
            total = hs[0] * xs[b + short_w - 1]
            if masked:
                far_b = bound(0, r0 + b)
                total = jnp.where(far_b >= 0, total, 0.0)
            for j in range(1, short_w):
                x = xs[b + short_w - 1 - j]
                if masked:
                    x = jnp.where(far_b >= j, x, 0.0)
                total = total + hs[j] * x
            res.append(total)
        return res

    lead = long_w

    def before(k, masked):
        i0 = k * ROW
        a = lead_short(s1, 1, i0, far - lead, i0, masked)
        for b in range(ROW):
            put(f1, i0 + b, a[b])
        d = lead_short(s2, 2, i0, far - lead, i0, masked)
        for b in range(ROW):
            put(f2, i0 + b, d[b])
            put(prod, i0 + b, rounded(a[b] * d[b]))

    def after(k, masked):
        i0 = k * ROW
        a = lead_short(s0, 0, i0, pad, i0 + lead, masked)
        for b in range(ROW):
            put(f0, i0 + b, a[b])
            put(back, i0 + b, rounded(tile(go, i0 + b) * a[b]))

    def pick(body, least, k):
        clear = limits[0, least] >= short_w - 1

        @pl.when(clear)
        def _():
            body(k, False)

        @pl.when(jnp.logical_not(clear))
        def _():
            body(k, True)

    count = (lead + seg + tail) // ROW
    lax.fori_loop(0, count, lambda k, _: (pick(before, k, k), 0)[1], 0)
    lax.fori_loop(0, count, lambda k, _: (pick(after, k + lead // ROW, k), 0)[1], 0)
    def differ(dst, ref):
        def step(k, _):
            for b in range(ROW):
                i = k * ROW + b
                x = [tile(ref, i + m) for m in (0, 4, 2, 6)]
                put(dst.at[0], i, x[0] - x[1])
                if LEAF < 4:
                    put(dst.at[1], i, x[0] - x[2])
                    put(dst.at[2], i, (x[0] - x[1]) - (x[2] - x[3]))
            return 0

        ref[pl.ds(count * ROW * ROW, ROW * ROW), :] = jnp.zeros((ROW * ROW, LANES), F32)
        lax.fori_loop(0, count, step, 0)

    differ(prod_less, prod)
    differ(back_less, back)

    def put_parts(ref, i, xs):
        parts = vector_parts(xs)
        for n, key in enumerate(KEYS):
            for m in range(LEAF):
                put(ref, (i * COUNT + n) * LEAF + m, parts[key][m])

    def tap_sums(k, _):
        put_parts(taps_sums, k, [tile(taps, k * ROW + j) for j in range(ROW)])
        return 0

    lax.fori_loop(0, long_w // ROW, tap_sums, 0)

    def products(kind, entry, vec):
        res = []
        for buf, start, key, _ in leaves(kind):
            n = KEYS.index(key)
            es = [entry(buf, start + m) for m in range(2 * LEAF - 1)]
            vs = [vec(n * LEAF + m) for m in range(LEAF)]
            for r in range(LEAF):
                total = None
                for m in range(LEAF):
                    at = {0: LEAF - 1 + r - m, 1: LEAF - 1 + m - r, 2: r + m}[kind]
                    term = es[at] * vs[m]
                    total = term if total is None else total + term
                res.append(total)
        return res

    def joined(kind, parts):
        res = [None] * ROW
        for n, (_, _, _, adds) in enumerate(leaves(kind)):
            for r, g in adds:
                for m in range(LEAF):
                    x = parts[n * LEAF + m]
                    at = r + m
                    if res[at] is None:
                        res[at] = x if g > 0 else -x
                    else:
                        res[at] = res[at] + x if g > 0 else res[at] - x
        return res

    def cached(ref, less):
        got = {}

        def entry_at(base):
            def entry(buf, m):
                if (buf, m) not in got:
                    got[buf, m] = tile(ref if buf == 0 else less.at[{1: 0, 2: 1, 3: 2}[buf]], base + m)
                return got[buf, m]
            return entry
        return entry_at

    def derived(xs):
        got = {(0, m): x for m, x in enumerate(xs)}

        def entry(buf, m):
            if (buf, m) not in got:
                low, step = {1: (0, 4), 2: (0, 2), 3: (1, 2)}[buf]
                got[buf, m] = entry(low, m) - entry(low, m + step)
            return got[buf, m]
        return entry

    acc[...] = jnp.zeros_like(acc)
    leaves_l[...] = jnp.zeros_like(leaves_l)
    zero = jnp.zeros((ROW, LANES), F32)

    def long_block(k, own):
        i0 = k * ROW
        if own:
            put_parts(seen, 0, [tile(back, i0 + b) for b in range(ROW)])
        size = COUNT * LEAF

        def before_window(j0):
            xs = [tile(prod, i0 + lead - j0 - ROW + 1 + m) for m in range(2 * ROW - 1)]
            reach = bound(0, i0 + lead) - j0
            return [jnp.where(reach >= ROW - 1 - m, x, 0.0) for m, x in enumerate(xs)]

        def after_window(j0):
            ys = [tile(back, i0 + j0 + m) for m in range(2 * ROW - 1)]
            room = bound(1, i0 + ROW - 1) + (ROW - 1 - j0)
            return [jnp.where(room >= m, y, 0.0) for m, y in enumerate(ys)]

        def ahead(jb, carry, masked):
            j0 = jb * ROW
            entry = derived(before_window(j0)) if masked else cached(prod, prod_less)(i0 + lead - j0 - ROW + 1)
            if own:
                olds = [tile(leaves_l, jb * size + n) for n in range(size)]
            parts = products(0, entry, lambda n: tile(taps_sums, jb * size + n))
            carry = tuple(c + x for c, x in zip(carry, parts))
            if own:
                parts = products(1, entry, lambda n: tile(seen, n))
                for n in range(size):
                    put(leaves_l, jb * size + n, olds[n] + parts[n])
            return carry

        def ahead_rows(jb, carry, first):
            j0 = jb * ROW
            reach = [bound(0, i0 + lead + b) - j0 for b in range(ROW)]
            hs = [tile(taps, j0 + j) for j in range(ROW)]
            if first:
                xs = [tile(prod, i0 + lead - j0 - ROW + 1 + m) for m in range(2 * ROW - 1)]
            else:
                xs = before_window(j0)
            total = [zero] * ROW
            if own:
                zs = [tile(back, i0 + b) for b in range(ROW)]
                if not first:
                    zs = [jnp.where(reach[b] >= 0, z, 0.0) for b, z in enumerate(zs)]
                parts = [tile(acc, j0 + j) for j in range(ROW)]
            for j in range(ROW):
                for b in range(ROW):
                    x = xs[b - j + ROW - 1]
                    if first:
                        x = jnp.where(reach[b] >= j, x, 0.0)
                    total[b] = total[b] + hs[j] * x
                    if own:
                        parts[j] = parts[j] + zs[b] * x
            if own:
                for j in range(ROW):
                    put(acc, j0 + j, parts[j])
            if not first:
                total = [jnp.where(reach[b] >= 0, x, 0.0) for b, x in enumerate(total)]
            return tuple(c + x for c, x in zip(carry, total))

        def behind(jb, carry, masked):
            j0 = jb * ROW
            entry = derived(after_window(j0)) if masked else cached(back, back_less)(i0 + j0)
            parts = products(2, entry, lambda n: tile(taps_sums, jb * size + n))
            return tuple(c + x for c, x in zip(carry, parts))

        def behind_rows(jb, carry, first):
            j0 = jb * ROW
            room = [bound(1, i0 + b) - j0 for b in range(ROW)]
            hs = [tile(taps, j0 + j) for j in range(ROW)]
            ys = [tile(back, i0 + j0 + m) for m in range(2 * ROW - 1)] if first else after_window(j0)
            total = [zero] * ROW
            for j in range(ROW):
                for b in range(ROW):
                    y = ys[b + j]
                    if first:
                        y = jnp.where(room[b] >= j, y, 0.0)
                    total[b] = total[b] + hs[j] * y
            if not first:
                total = [jnp.where(room[b] >= 0, x, 0.0) for b, x in enumerate(total)]
            return tuple(c + x for c, x in zip(carry, total))

        even = limits[4, k + lead // ROW] == 1

        def all_of(kind, low, high, at, whole, by_row):
            some = jnp.minimum((limits[high, at] + ROW) // ROW, long_w // ROW)
            full = jnp.where(even, jnp.minimum((limits[low, at] + 1) // ROW, long_w // ROW), 0)
            middle = jnp.where(even, some, 0)
            pairs = jnp.where(even, some, jnp.minimum(some, 1))
            total = lax.fori_loop(0, full, lambda j, c: whole(j, c, False), (zero,) * size)
            total = lax.fori_loop(full, middle, lambda j, c: whole(j, c, True), total)
            total = tuple(joined(kind, total))
            total = lax.fori_loop(middle, pairs, lambda j, c: by_row(j, c, True), total)
            return lax.fori_loop(pairs, some, lambda j, c: by_row(j, c, False), total)

        carry = all_of(0, 0, 1, k + lead // ROW, ahead, ahead_rows)
        grad = all_of(2, 2, 3, k, behind, behind_rows)
        for b in range(ROW):
            put(gf.at[0], i0 + b, rounded(tile(go, i0 + b) * carry[b]))
            put(gf.at[1], i0 + b, rounded(grad[b] * tile(f2, i0 + lead + b)))
            put(gf.at[2], i0 + b, rounded(grad[b] * tile(f1, i0 + lead + b)))
            if own:
                put(car, i0 + b, tile(f0, i0 + b) * carry[b])

    lax.fori_loop(0, seg // ROW, lambda k, _: (long_block(k, True), 0)[1], 0)
    for k in range(seg // ROW, (seg + tail) // ROW):
        long_block(k, False)

    def join_long(k, _):
        got = joined(1, [tile(leaves_l, k * COUNT * LEAF + n) for n in range(COUNT * LEAF)])
        for j in range(ROW):
            put(acc, k * ROW + j, tile(acc, k * ROW + j) + got[j])
        return 0

    lax.fori_loop(0, long_w // ROW, join_long, 0)

    def last(k, carry, s, src, off, masked):
        i0 = k * ROW
        ys = [tile(gf.at[s], i0 + m) for m in range(ROW + short_w - 1)]
        xs = [tile(src, i0 + off - short_w + 1 + m) for m in range(ROW + short_w - 1)]
        hs = [few[pl.ds((s * short_w + j) * ROW, ROW), :] for j in range(short_w)]
        parts = list(carry)
        for b in range(ROW):
            total = None
            if masked:
                room, reach = bound(1, i0 + b), bound(0, i0 + lead + b)
            for j in range(short_w):
                y, x = ys[b + j], xs[b + short_w - 1 - j]
                if masked:
                    y = jnp.where(room >= j, y, 0.0)
                    x = jnp.where(reach >= j, x, 0.0)
                total = hs[j] * y if total is None else total + hs[j] * y
                parts[j] = parts[j] + ys[b] * x
            put(out.at[s], i0 + b, total)
        return tuple(parts)

    for s, src, off in ((0, s0, pad), (1, s1, far), (2, s2, far)):
        def step(k, carry, s=s, src=src, off=off):
            least = jnp.minimum(limits[0, k + lead // ROW], limits[2, k])
            return lax.cond(
                least >= short_w - 1,
                lambda: last(k, carry, s, src, off, False),
                lambda: last(k, carry, s, src, off, True),
            )

        parts = lax.fori_loop(0, seg // ROW, step, (zero,) * short_w)
        for j in range(short_w):
            put(acc, long_w + s * ROW + j, parts[j])

    total_rows = acc.shape[0] // ROW
    for g in range(groups):
        c = slice(g * LANES, (g + 1) * LANES)
        total = None
        for span in range(spans):
            r = span * groups + g
            own = pl.ds(span * seg, seg)
            gated[own, c] = car[pl.ds(r, seg, stride=ROW), :].astype(BF16)
            for s in range(3):
                mixed[s, own, c] = out[s, pl.ds(r, seg, stride=ROW), :].astype(BF16)
            x = acc[pl.ds(r, total_rows, stride=ROW), :]
            total = x if total is None else total + x
        sums[:, c] = total.astype(BF16)


def conv_block(proj, up12, up0, down0, down12, grad_out, short_taps, long_taps, contig_lengths):
    _, rows, chans = proj.shape
    short_w, long_w = short_taps.shape[1], long_taps.shape[0]
    far, pad = up12.shape[1], up0.shape[0]
    groups = chans // LANES
    spans = ROW // groups
    seg, tail = rows // spans, ROW
    lead = long_w

    offset = lax.axis_index("ctx") // 2 * rows
    order = jnp.arange(contig_lengths.shape[0], dtype=jnp.int32)
    ends = jnp.sum(jnp.where(order[None, :] <= order[:, None], contig_lengths[None, :], 0), axis=1)
    begins = ends - contig_lengths
    span = jnp.arange(spans, dtype=jnp.int32) * seg
    count = lead + seg + tail + lead
    at = offset - lead + jnp.arange(count, dtype=jnp.int32)[:, None] + span[None, :]
    first = jnp.max(jnp.where(begins[None, None, :] <= at[:, :, None], begins[None, None, :], 0), axis=2)
    reach = at - first
    here = at[lead : lead + seg + tail]
    end = jnp.min(jnp.where(ends[None, None, :] > here[:, :, None], ends[None, None, :], jnp.int32(2**30)), axis=2)
    room = end - 1 - here

    near = jnp.stack([reach.T, jnp.pad(room.T, ((0, 0), (0, count - room.shape[0])))])

    def blocks(x, how):
        return jnp.pad(how(x.reshape(-1, ROW * spans), axis=1), (0, (count - x.shape[0]) // ROW))

    limits = jnp.stack([
        blocks(reach, jnp.min), blocks(reach, jnp.max), blocks(room, jnp.min), blocks(room, jnp.max),
        jnp.all(reach[ROW - 1 :: ROW] - reach[::ROW] == ROW - 1, axis=1).astype(jnp.int32),
    ])

    def vmem(n):
        return pltpu.VMEM((n * ROW, LANES), F32)

    dims = (rows, far, pad, short_w, long_w, spans, groups, seg, tail)
    size = lead + seg + tail
    in_vmem = pl.BlockSpec(memory_space=pltpu.VMEM)
    return pl.pallas_call(
        lambda *refs: conv_kernel(dims, *refs),
        in_specs=[pl.BlockSpec(memory_space=pltpu.SMEM)] * 2 + [in_vmem] * 8,
        out_specs=[in_vmem] * 3,
        out_shape=[
            jax.ShapeDtypeStruct((rows, chans), BF16),
            jax.ShapeDtypeStruct((3, rows, chans), BF16),
            jax.ShapeDtypeStruct((long_w + 4 * ROW, chans), BF16),
        ],
        scratch_shapes=[
            vmem(pad + seg + far), vmem(far + seg + pad), vmem(far + seg + pad), vmem(seg + far),
            vmem(size), vmem(size), vmem(size), vmem(size + ROW), vmem(size + ROW),
            pltpu.VMEM((3, size * ROW, LANES), F32), pltpu.VMEM((3, size * ROW, LANES), F32),
            vmem(long_w // ROW * COUNT * LEAF), vmem(COUNT * LEAF), vmem(seg + tail),
            pltpu.VMEM((3, (seg + 2 * tail) * ROW, LANES), F32),
            vmem(long_w + 4 * ROW), vmem(long_w), vmem(long_w // ROW * COUNT * LEAF), vmem(3 * short_w),
            pltpu.VMEM((3, seg * ROW, LANES), F32),
        ],
        compiler_params=pltpu.CompilerParams(vmem_limit_bytes=56 << 20),
        cost_estimate=pl.CostEstimate(
            flops=rows * chans * long_w * 1000, bytes_accessed=rows * chans * 24, transcendentals=0
        ),
        name="hyena_filters",
    )(limits, near, proj, up12, up0, down0, down12, grad_out, short_taps, long_taps)


def deliver(weights, tokens, gated, filters, long_w, short_w):
    streams, feats, chans = weights.shape

    def kernel(w, t, g, f, w_out, t_out, g_out, short_out, long_out):
        w_out[...] = w[...]

        @pl.when(pl.program_id(0) == 0)
        def _():
            t_out[...] = t[...]
            g_out[...] = g[...]
            long_out[...] = f[pl.ds(0, long_w), :]
            for s in range(streams):
                short_out[s] = f[pl.ds(long_w + ROW * s, short_w), :]

    def whole(*dims):
        return pl.BlockSpec(dims, lambda s: (0,) * len(dims))

    part = pl.BlockSpec((None, feats, chans), lambda s: (s, 0, 0))
    short_shape = (streams, short_w, chans)
    return pl.pallas_call(
        kernel,
        grid=(streams,),
        in_specs=[part, whole(*tokens.shape), whole(*gated.shape), whole(*filters.shape)],
        out_specs=[part, whole(*tokens.shape), whole(*gated.shape), whole(*short_shape), whole(long_w, chans)],
        out_shape=[
            jax.ShapeDtypeStruct(weights.shape, BF16),
            jax.ShapeDtypeStruct(tokens.shape, BF16),
            jax.ShapeDtypeStruct(gated.shape, BF16),
            jax.ShapeDtypeStruct(short_shape, F32),
            jax.ShapeDtypeStruct((long_w, chans), F32),
        ],
        compiler_params=pltpu.CompilerParams(vmem_limit_bytes=56 << 20),
        cost_estimate=pl.CostEstimate(flops=0, bytes_accessed=4 * weights.size, transcendentals=0),
        name="deliver",
    )(weights, tokens, gated, filters)


def on_device(loaded, slot_pos, contig_lengths, w_in, short_taps, long_taps, grad_out):
    me = lax.axis_index("ctx")
    core = me % 2
    chans = grad_out.shape[1]
    short_w, long_w = short_taps.shape[1], long_taps.shape[0]
    far, pad = round_up(long_w, 16) + 16, 16
    n_ctx = lax.axis_size("ctx")

    short_c, long_c = half(short_taps, 2, core), half(long_taps, 1, core)
    proj, up12, up0, down0, down12, grad_c, wall, *turned = gather(
        jnp.transpose(w_in, (1, 0, 2)), loaded[0], slot_pos, grad_out, far, pad
    )
    turned = [swapped(x, 2 * m) if m else x for m, x in enumerate(turned)]
    gated, grads, sums = conv_block(
        proj, up12, up0, down0, down12, grad_c, short_c, long_c, contig_lengths
    )
    results = reduce(grads, wall, gated, sums, turned)
    weight_grads, token_grads, gated_out, short_total, long_total = deliver(*results, long_w, short_w)
    return gated_out, token_grads, jnp.transpose(weight_grads, (1, 0, 2)), short_total, long_total


def solution(mesh):
    in_specs = (
        P("ctx", None, None, "fsdp"),
        P("ctx", None, None),
        P(),
        P("ctx", None, "fsdp"),
        P(None, None, "fsdp"),
        P(None, "fsdp"),
        P("ctx", "fsdp"),
    )
    out_specs = (
        P("ctx", "fsdp"),
        P("ctx", "fsdp"),
        P("ctx", None, "fsdp"),
        P(None, None, "fsdp"),
        P(None, "fsdp"),
    )
    return jax.shard_map(
        on_device, mesh=mesh, in_specs=in_specs, out_specs=out_specs, check_vma=False
    )
```

```python
import jax
import jax.numpy as jnp
from jax import lax
from jax.experimental import pallas as pl
from jax.experimental.pallas import tpu as pltpu
from jax.sharding import PartitionSpec as P

LANES = 128
F32, BF16 = jnp.float32, jnp.bfloat16


def round_up(x, to):
    return -(-x // to) * to


def swapped(x, mask):
    size = lax.axis_size("ctx")
    return lax.ppermute(x, "ctx", [(i, i ^ mask) for i in range(size)])


def chip_masks(size):
    masks, step = [], 2
    while step < size:
        masks.append(step)
        step *= 2
    return masks


def walk(masks):
    held = [0]
    for mask in masks:
        held = held + [k ^ mask for k in held]
    return held


def half(x, dim, which):
    width = x.shape[dim] // 2
    return lax.dynamic_slice_in_dim(x, which * width, width, dim)


def remote(src, dst, send, recv, **place):
    return pltpu.make_async_remote_copy(
        src_ref=src, dst_ref=dst, send_sem=send, recv_sem=recv,
        device_id=place, device_id_type=pl.DeviceIdType.MESH,
    )


def local(src, dst, sem):
    return pltpu.make_async_copy(src, dst, sem)


def at_cols(start, size):
    return pl.ds(pl.multiple_of(start, LANES), size)


def greet(n_ctx, n_line):
    me, z = lax.axis_index("ctx"), lax.axis_index("fsdp")
    barrier = pltpu.get_barrier_semaphore()
    others = [1] + [k for k in range(2, n_ctx, 2)]
    for k in others:
        pl.semaphore_signal(
            barrier, inc=1, device_id={"ctx": me ^ k}, device_id_type=pl.DeviceIdType.MESH
        )

    @pl.when(z > 0)
    def _():
        pl.semaphore_signal(
            barrier, inc=1, device_id={"fsdp": z - 1}, device_id_type=pl.DeviceIdType.MESH
        )

    @pl.when(z < n_line - 1)
    def _():
        pl.semaphore_signal(
            barrier, inc=1, device_id={"fsdp": z + 1}, device_id_type=pl.DeviceIdType.MESH
        )

    ends = jnp.where(z > 0, 1, 0) + jnp.where(z < n_line - 1, 1, 0)
    pl.semaphore_wait(barrier, len(others) + ends)


class Spread:
    def __init__(self, buf, send, recv, masks, me):
        self.buf, self.send, self.recv, self.me = buf, send, recv, me
        self.orders = (masks, masks[::-1])
        self.keys = tuple(walk(m) for m in self.orders)
        self.count = 1 << len(masks)

    def copy(self, chain, stage, i):
        to = (1 << stage) + i
        return remote(
            self.buf.at[chain, i], self.buf.at[chain, to],
            self.send.at[chain, to], self.recv.at[chain, to],
            ctx=self.me ^ self.orders[chain][stage],
        )

    def stages(self, i):
        return range(i.bit_length(), len(self.orders[0]))

    def start(self, chain, i, stages=None):
        for stage in self.stages(i) if stages is None else stages:
            self.copy(chain, stage, i).start()

    def arrive(self, chain, i):
        stage = i.bit_length() - 1
        self.copy(chain, stage, i - (1 << stage)).wait_recv()

    def finish(self):
        for chain in (0, 1):
            for i in range(self.count):
                for stage in self.stages(i):
                    self.copy(chain, stage, i).wait_send()


def gather_kernel(
    sizes, w, slots, pos, grad,
    proj, up12, up0, down0, down12, gext, wall, *rest
):
    n_ctx, n, far, pad = sizes
    turned, rest = rest[: n_ctx // 2], rest[n_ctx // 2 :]
    gather_body(n_ctx, n, far, pad, w, slots, pos, grad, proj, up12, up0, down0, down12, gext, wall, turned, *rest)


def gather_body(
    n_ctx, n, far, pad, w, slots, pos, grad,
    proj, up12, up0, down0, down12, gext, wall, turned,
    tbuf, wbuf, xbuf, sbuf, pbuf, part, ppart, acc,
    w_send, w_recv, s_send, s_recv, up_send, up_recv, dn_send, dn_recv,
    core_send, core_recv, misc_send, misc_recv, local_sem, out_sem, halo_send, halo_recv, turn_sem,
):
    me, z = lax.axis_index("ctx"), lax.axis_index("fsdp")
    core, chip = me % 2, me // 2
    chips = n_ctx // 2
    rows, dz = ppart.shape
    streams, feats, ch = wbuf.shape[2:]
    masks = chip_masks(n_ctx)
    greet(n_ctx, n)

    sib = me ^ 1
    own_pos = local(pos.at[0], pbuf.at[core], local_sem.at[0])
    own_pos.start()
    send_pos = remote(pos.at[0], pbuf.at[core], misc_send.at[0], misc_recv.at[0], ctx=sib)
    send_pos.start()
    own_slots = local(slots.at[pl.ds(2 * chip, 2)], sbuf.at[chip], local_sem.at[1])
    own_slots.start()
    deals = []
    for k in range(2, n_ctx, 2):
        to = me ^ k
        deals.append(remote(
            slots.at[pl.ds(to - core, 2)], sbuf.at[chip], s_send.at[k // 2], s_recv.at[k // 2], ctx=to
        ))
        deals[-1].start()
    own_w = local(w.at[:, :, at_cols(core * ch, ch)], wbuf.at[0, 0], local_sem.at[2])
    own_w.start()
    send_w = remote(
        w.at[:, :, at_cols((1 - core) * ch, ch)], wbuf.at[1, 0], misc_send.at[1], misc_recv.at[1], ctx=sib
    )
    send_w.start()
    own_rows = pl.ds(pl.multiple_of(core * rows, rows), rows)
    own_grad = local(grad.at[:, at_cols(core * ch, ch)], gext.at[own_rows], local_sem.at[3])
    own_grad.start()
    send_grad = remote(
        grad.at[:, at_cols((1 - core) * ch, ch)], gext.at[own_rows], misc_send.at[3], misc_recv.at[3], ctx=sib
    )
    send_grad.start()
    spread = Spread(wbuf, w_send, w_recv, masks, me)
    stages = len(masks)
    keep = []

    def stored(chain, i):
        keep.append(local(wbuf.at[chain, i], wall.at[chain, i], out_sem.at[chain, i]))
        keep[-1].start()

    own_w.wait()
    spread.start(0, 0, range(0, min(1, stages)))
    stored(0, 0)
    send_w.wait_recv()
    spread.start(1, 0, range(0, min(1, stages)))
    stored(1, 0)

    own_pos.wait()
    send_pos.wait_recv()
    own_slots.wait()
    for deal in deals:
        deal.wait_recv()
    spread.start(0, 0, range(1, stages))
    spread.start(1, 0, range(1, stages))

    seat = lax.broadcasted_iota(jnp.int32, (rows, pos.shape[2]), 0)

    def place(b):
        total = None
        for c in range(chips):
            row = pbuf[b, pl.ds(2 * c + core, 1), :]
            pick = jnp.where(row == seat, 1.0, 0.0).astype(BF16)
            term = jnp.dot(pick, sbuf[c, b], preferred_element_type=F32)
            total = term if total is None else total + term
        return total.astype(BF16)

    part[...] = place(1 - core)
    give = remote(part, ppart, misc_send.at[2], misc_recv.at[2], ctx=sib)
    give.start()
    mine = place(core)
    give.wait_recv()
    own_grad.wait()
    send_grad.wait_recv()
    edge_grad = remote(
        gext.at[pl.ds(0, far)], gext.at[pl.ds(2 * rows, far)], misc_send.at[4], misc_recv.at[4], ctx=me - 2
    )

    @pl.when(chip > 0)
    def _():
        edge_grad.start()

    xbuf[own_rows, at_cols(z * dz, dz)] = mine + ppart[...]

    def tile(t):
        return xbuf.at[own_rows, at_cols(t * dz, dz)]

    def to_core(t):
        return remote(tile(t), tile(t), core_send.at[t], core_recv.at[t], ctx=sib)

    def other_tile(t):
        there = xbuf.at[pl.ds(pl.multiple_of((1 - core) * rows, rows), rows), at_cols(t * dz, dz)]
        return remote(there, there, core_send.at[t], core_recv.at[t], ctx=sib)

    def up(h, t):
        return remote(tile(t), tile(t), up_send.at[h], up_recv.at[h], fsdp=z + 1)

    def down(h, t):
        return remote(tile(t), tile(t), dn_send.at[h], dn_recv.at[h], fsdp=z - 1)

    to_core(z).start()
    for h in range(1, n):
        @pl.when((z < n - 1) & (z - h + 1 >= 0))
        def _():
            up(h, z - h + 1).start()

        @pl.when((z > 0) & (z + h - 1 <= n - 1))
        def _():
            down(h, z + h - 1).start()

        @pl.when(z - h >= 0)
        def _():
            up(h, z - h).wait_recv()
            to_core(z - h).start()

        @pl.when(z + h <= n - 1)
        def _():
            down(h, z + h).wait_recv()
            to_core(z + h).start()

        if h == 1 and spread.count > 1:
            for chain in (0, 1):
                spread.arrive(chain, 1)
                spread.start(chain, 1)
                stored(chain, 1)
    for t in range(n):
        other_tile(t).wait_recv()
    for m in range(chips):
        tbuf[m] = xbuf[:, at_cols((me ^ (2 * m)) * feats, feats)].T
        keep.append(local(tbuf.at[m], turned[m], turn_sem.at[m]))
        keep[-1].start()

    def term(chain, i, s):
        cols = at_cols((me ^ chain ^ spread.keys[chain][i]) * feats, feats)
        return jnp.dot(xbuf[:, cols], wbuf[chain, i, s], preferred_element_type=F32)

    final = spread.count - 1
    for i in range(spread.count):
        for chain in (0, 1):
            if i > 1:
                spread.arrive(chain, i)
                spread.start(chain, i)
                stored(chain, i)
            if i == final:
                continue

            def one(s, _, chain=chain, i=i):
                total = term(chain, i, s)
                acc[s] = total if i == 0 and chain == 0 else total + acc[s]
                return 0

            lax.fori_loop(0, streams, one, 0)

    total = 2 * rows

    def halos(s, up_to, down_to):
        top, bottom = (up0, down0) if s == 0 else (up12.at[s - 1], down12.at[s - 1])
        high, low = (pad, far) if s == 0 else (far, pad)
        return (
            remote(proj.at[s, pl.ds(total - high, high)], top, halo_send.at[s], halo_recv.at[s], ctx=up_to),
            remote(proj.at[s, pl.ds(0, low)], bottom, halo_send.at[3 + s], halo_recv.at[3 + s], ctx=down_to),
        )

    edges = [halos(s, me + 2, me - 2) for s in range(streams)]
    for s in (1, 2, 0):
        proj[s] = (acc[s] + term(0, final, s) + term(1, final, s)).astype(BF16)

        @pl.when(chip < chips - 1)
        def _():
            edges[s][0].start()

        @pl.when(chip > 0)
        def _():
            edges[s][1].start()

    @pl.when(chip == 0)
    def _():
        up12[...] = jnp.zeros_like(up12)
        up0[...] = jnp.zeros_like(up0)

    @pl.when(chip == chips - 1)
    def _():
        gext[pl.ds(2 * rows, far), :] = jnp.zeros((far, ch), BF16)
        down0[...] = jnp.zeros_like(down0)
        down12[...] = jnp.zeros_like(down12)

    @pl.when(chip > 0)
    def _():
        for up_edge, down_edge in edges:
            up_edge.wait_recv()
            down_edge.wait_send()
        edge_grad.wait_send()

    @pl.when(chip < chips - 1)
    def _():
        for up_edge, down_edge in edges:
            down_edge.wait_recv()
            up_edge.wait_send()
        edge_grad.wait_recv()

    for h in range(1, n):
        @pl.when((z < n - 1) & (z - h + 1 >= 0))
        def _():
            up(h, z - h + 1).wait_send()

        @pl.when((z > 0) & (z + h - 1 <= n - 1))
        def _():
            down(h, z + h - 1).wait_send()
    for t in range(n):
        to_core(t).wait_send()
    for deal in deals + [send_pos, send_w, send_grad, give]:
        deal.wait_send()
    spread.finish()
    for copy in keep:
        copy.wait()


def gather(w, slots, pos, grad, far, pad):
    n_ctx, n = lax.axis_size("ctx"), lax.axis_size("fsdp")
    chips = n_ctx // 2
    streams, feats, two = w.shape
    ch, dz = two // 2, slots.shape[2]
    rows = grad.shape[0]
    total = 2 * rows
    any_space, vmem = pl.BlockSpec(memory_space=pl.ANY), pl.BlockSpec(memory_space=pltpu.VMEM)
    dma = pltpu.SemaphoreType.DMA

    def shape(*dims):
        return jax.ShapeDtypeStruct(dims, BF16)

    return pl.pallas_call(
        lambda *refs: gather_kernel((n_ctx, n, far, pad), *refs),
        in_specs=[any_space] * 4,
        out_specs=[vmem] * 6 + [any_space] * (1 + chips),
        out_shape=[
            shape(streams, total, ch), shape(2, far, ch), shape(pad, ch), shape(far, ch), shape(2, pad, ch),
            shape(total + far, ch),
            shape(2, chips, streams, feats, ch),
        ] + [shape(feats, total)] * chips,
        scratch_shapes=[
            pltpu.VMEM((chips, feats, total), BF16),
            pltpu.VMEM((2, chips, streams, feats, ch), BF16),
            pltpu.VMEM((total, n * dz), BF16),
            pltpu.VMEM((chips, 2, slots.shape[1], dz), BF16),
            pltpu.VMEM((2, *pos.shape[1:]), jnp.int32),
            pltpu.VMEM((rows, dz), BF16),
            pltpu.VMEM((rows, dz), BF16),
            pltpu.VMEM((streams, total, ch), F32),
            dma((2, chips)), dma((2, chips)), dma((chips,)), dma((chips,)),
            dma((n,)), dma((n,)), dma((n,)), dma((n,)),
            dma((n,)), dma((n,)), dma((5,)), dma((5,)), dma((4,)), dma((2, chips)), dma((6,)), dma((6,)), dma((chips,)),
        ],
        compiler_params=pltpu.CompilerParams(
            collective_id=0, has_side_effects=True, vmem_limit_bytes=56 << 20
        ),
        cost_estimate=pl.CostEstimate(
            flops=2 * total * n * dz * streams * ch, bytes_accessed=40 << 20, transcendentals=0
        ),
        name="gather_and_project",
    )(w, slots, pos, grad)


def reduce_kernel(
    sizes, grads, wall, gated, sums, *rest
):
    chips = sizes[0] // 2
    reduce_body(sizes, grads, wall, gated, sums, rest[:chips], *rest[chips:])


def reduce_body(
    sizes, grads, wall, gated, sums, turned,
    wg, tg, gout, filt,
    gbuf, lbuf, acc, wgb, wv, xp, xs, xr, up_tx, up_rx, dn_tx, dn_rx, fbuf, ftot,
    g_send, g_recv, f_send, f_recv, up_send, up_recv, dn_send, dn_recv,
    core_send, core_recv, misc_send, misc_recv, local_sem, wv_sem, t_sem, t_send, t_recv,
):
    n_ctx, n = sizes
    me, z = lax.axis_index("ctx"), lax.axis_index("fsdp")
    core, chip = me % 2, me // 2
    chips = n_ctx // 2
    streams, rows, ch = gbuf.shape[2:]
    feats = lbuf.shape[1]
    dz = xp.shape[1] // n
    masks = chip_masks(n_ctx)
    sib = me ^ 1
    own_g = [
        local(grads.at[:, pl.ds(b * rows, rows)], gbuf.at[b, 0], local_sem.at[b]) for b in (0, 1)
    ]
    for copy in own_g:
        copy.start()
    spread = Spread(gbuf, g_send, g_recv, masks, me)
    wkeys = (walk(masks), walk(masks[::-1]))
    order = [(chain, i) for i in range(chips) for chain in (0, 1)]

    def fetch(j):
        chain, i = order[j]
        return local(wall.at[chain, i], wv.at[j % 2], wv_sem.at[j % 2])

    fetch(0).start()
    lefts, trades = [], []
    for m in range(chips):
        cols = at_cols(((me - core) ^ (2 * m)) * rows, 2 * rows)
        lefts.append(local(turned[m], lbuf.at[0, :, cols], t_sem.at[m]))
        trades.append(remote(turned[m], lbuf.at[1, :, cols], t_send.at[m], t_recv.at[m], ctx=sib))
        lefts[-1].start()
    greet(n_ctx, n)
    for copy in own_g:
        copy.wait()
    for chain in (0, 1):
        spread.start(chain, 0)
    for trade in trades:
        trade.start()

    fbuf[chip] = sums[...]
    shares = []
    for k in range(2, n_ctx, 2):
        shares.append(remote(
            fbuf.at[chip], fbuf.at[chip], f_send.at[k // 2], f_recv.at[k // 2], ctx=me ^ k
        ))
    mine = at_cols(core * ch, ch)
    keep_gated = local(gated.at[pl.ds(core * rows, rows)], gout.at[:, mine], local_sem.at[3])
    give_gated = remote(
        gated.at[pl.ds((1 - core) * rows, rows)], gout.at[:, mine], misc_send.at[0], misc_recv.at[0], ctx=sib
    )
    keep_gated.start()
    give_gated.start()

    def to_core(block):
        cols = at_cols(block * feats, feats)
        return remote(xs.at[:, cols], xr.at[:, cols], core_send.at[block], core_recv.at[block], ctx=sib)

    for j, (chain, i) in enumerate(order):
        if j + 1 < len(order):
            fetch(j + 1).start()
        fetch(j).wait()
        block = me ^ chain ^ wkeys[chain][i]
        cols = at_cols(block * feats, feats)

        def back(b, j=j):
            total = None
            for s in range(streams):
                term = lax.dot_general(
                    gbuf[b, 0, s], wv[j % 2, s], (((1,), (1,)), ((), ())), preferred_element_type=F32
                )
                total = term if total is None else total + term
            return total

        xs[:, cols] = back(1 - core).astype(BF16)
        to_core(block).start()
        xp[:, cols] = back(core)

    step = 32

    def each(body):
        def one(r, _):
            body(pl.ds(pl.multiple_of(r * step, step), step))
            return 0

        lax.fori_loop(0, rows // step, one, 0)

    def weigh(chain, i, halves=(0, 1), end=False):
        where = ((me - core) ^ spread.keys[chain][i]) + chain
        cols = at_cols(where * rows, rows)
        first = i == 0 and chain == 0

        def one(r, _):
            h, s = r // streams, r % streams
            total = jnp.dot(lbuf[h, :, cols], gbuf[chain, i, s], preferred_element_type=F32)
            if not first:
                total = acc[r] + total
            if end:
                wgb[r] = total.astype(BF16)
            else:
                acc[r] = total
            return 0

        lax.fori_loop(halves[0] * streams, (halves[-1] + 1) * streams, one, 0)

    for block in range(n_ctx):
        to_core(block).wait_recv()
    for left, trade in zip(lefts, trades):
        left.wait()
        trade.wait_recv()

    def up(s):
        return remote(up_tx.at[s - 1], up_rx.at[s - 1], up_send.at[s], up_recv.at[s], fsdp=z + 1)

    def down(s):
        return remote(dn_tx.at[s - 1], dn_rx.at[s - 1], dn_send.at[s], dn_recv.at[s], fsdp=z - 1)

    zz = n - 1 - z

    def send_tile(s, a, far_end, tx, rx):
        cols = at_cols(a * dz, dz)

        @pl.when(far_end == 0)
        def _():
            def body(at):
                tx[s - 1, at] = (xp[at, cols] + xr[at, cols].astype(F32)).astype(BF16)
            each(body)

        if s >= 2:
            @pl.when(far_end > 0)
            def _():
                def body(at):
                    total = xp[at, cols] + xr[at, cols].astype(F32) + rx[s - 2, at].astype(F32)
                    tx[s - 1, at] = total.astype(BF16)
                each(body)

    def line_start(s):
        last = min(s - 1, n - 2)

        @pl.when(z <= last)
        def _():
            send_tile(s, n - s + z, z, up_tx, up_rx)
            up(s).start()

        @pl.when(zz <= last)
        def _():
            send_tile(s, z + s - n, zz, dn_tx, dn_rx)
            down(s).start()

    def line_wait(s):
        last = min(s - 1, n - 2)

        @pl.when((z >= 1) & (z - 1 <= last))
        def _():
            up(s).wait_recv()

        @pl.when((zz >= 1) & (zz - 1 <= last))
        def _():
            down(s).wait_recv()

    def finish_line():
        if n > 1:
            line_wait(n - 1)
        cols = at_cols(z * dz, dz)

        def final(at):
            acc_t = xp[at, cols] + xr[at, cols].astype(F32)
            if n > 1:
                acc_t = acc_t + jnp.where(z >= 1, up_rx[n - 2, at].astype(F32), 0.0)
                acc_t = acc_t + jnp.where(zz >= 1, dn_rx[n - 2, at].astype(F32), 0.0)
            tg[at] = acc_t.astype(BF16)

        each(final)

    if n > 1:
        line_start(1)
    sent = 1
    if spread.count == 1:
        finish_line()
    for i in range(spread.count):
        for chain in (0, 1):
            if i:
                spread.arrive(chain, i)
                spread.start(chain, i)
        if i == spread.count - 1:
            break
        for chain in (0, 1):
            weigh(chain, i)
        if i == spread.count - 2:
            while sent < n - 1:
                line_wait(sent)
                sent += 1
                line_start(sent)
            finish_line()
        elif sent < n - 1:
            line_wait(sent)
            sent += 1
            line_start(sent)
    for share in shares:
        share.start()
    give_w = remote(
        wgb.at[pl.ds(streams, streams)], wg.at[:, :, mine], misc_send.at[1], misc_recv.at[1], ctx=sib
    )
    keep_w = local(wgb.at[pl.ds(0, streams)], wg.at[:, :, mine], local_sem.at[4])
    for h, copy in ((1, give_w), (0, keep_w)):
        weigh(0, spread.count - 1, (h,))
        weigh(1, spread.count - 1, (h,), end=True)
        copy.start()
    for share in shares:
        share.wait_recv()
    total = fbuf[0].astype(F32)
    for c in range(1, chips):
        total = total + fbuf[c].astype(F32)
    ftot[...] = total
    give_f = remote(ftot, filt.at[:, mine], misc_send.at[2], misc_recv.at[2], ctx=sib)
    give_f.start()
    keep_f = local(ftot, filt.at[:, mine], local_sem.at[5])
    keep_f.start()

    for s in range(1, n):
        last = min(s - 1, n - 2)

        @pl.when(z <= last)
        def _():
            up(s).wait_send()

        @pl.when(zz <= last)
        def _():
            down(s).wait_send()
    for block in range(n_ctx):
        to_core(block).wait_send()
    spread.finish()
    for share in shares:
        share.wait_send()
    for trade in trades:
        trade.wait_send()
    for copy in (give_gated, give_w, give_f):
        copy.wait()
    for copy in (keep_gated, keep_w, keep_f):
        copy.wait()


def reduce(grads, wall, gated, sums, turned):
    n_ctx, n = lax.axis_size("ctx"), lax.axis_size("fsdp")
    chips = n_ctx // 2
    streams, total, ch = grads.shape
    rows = total // 2
    feats = turned[0].shape[0]
    dim = feats * n_ctx
    dz = dim // n
    any_space, vmem = pl.BlockSpec(memory_space=pl.ANY), pl.BlockSpec(memory_space=pltpu.VMEM)
    dma = pltpu.SemaphoreType.DMA
    hops = max(n - 1, 1)
    return pl.pallas_call(
        lambda *refs: reduce_kernel((n_ctx, n), *refs),
        in_specs=[any_space] * 3 + [vmem] + [any_space] * chips,
        out_specs=[any_space, vmem, any_space, any_space],
        out_shape=[
            jax.ShapeDtypeStruct((streams, feats, 2 * ch), BF16),
            jax.ShapeDtypeStruct((rows, dz), BF16),
            jax.ShapeDtypeStruct((rows, 2 * ch), BF16),
            jax.ShapeDtypeStruct((sums.shape[0], 2 * ch), F32),
        ],
        scratch_shapes=[
            pltpu.VMEM((2, chips, streams, rows, ch), BF16),
            pltpu.VMEM((2, feats, rows * n_ctx), BF16),
            pltpu.VMEM((2 * streams, feats, ch), F32),
            pltpu.VMEM((2 * streams, feats, ch), BF16),
            pltpu.VMEM((2, streams, feats, ch), BF16),
            pltpu.VMEM((rows, dim), F32),
            pltpu.VMEM((rows, dim), BF16),
            pltpu.VMEM((rows, dim), BF16),
            pltpu.VMEM((hops, rows, dz), BF16), pltpu.VMEM((hops, rows, dz), BF16),
            pltpu.VMEM((hops, rows, dz), BF16), pltpu.VMEM((hops, rows, dz), BF16),
            pltpu.VMEM((chips, *sums.shape), BF16),
            pltpu.VMEM(sums.shape, F32),
            dma((2, chips)), dma((2, chips)), dma((chips,)), dma((chips,)),
            dma((n,)), dma((n,)), dma((n,)), dma((n,)),
            dma((n_ctx,)), dma((n_ctx,)), dma((3,)), dma((3,)), dma((6,)), dma((2,)),
            dma((chips,)), dma((chips,)), dma((chips,)),
        ],
        compiler_params=pltpu.CompilerParams(
            collective_id=1, has_side_effects=True, vmem_limit_bytes=60 << 20
        ),
        cost_estimate=pl.CostEstimate(
            flops=4 * total * dim * streams * ch, bytes_accessed=40 << 20, transcendentals=0
        ),
        name="gather_and_reduce",
    )(grads, wall, gated, sums, *turned)


ROW = 8
LEAF = 2


def leaves(kind, size=ROW, buf=0, start=0, vec=(0, ROW), sign=1, rows=(0, ROW)):
    def split(size, buf, start, vec, adds):
        if size == LEAF:
            yield buf, start, vec, adds
            return
        h = size // 2
        step = {8: 1, 4: 2}[size]
        low, high, both = vec + (0,), vec + (1,), vec + (2,)
        yield from split(h, buf, start + h, both, adds + [(r + h, g) for r, g in adds])
        first = [(r, g) for r, g in adds]
        second = [(r + h, g) for r, g in adds]
        minus = lambda adds: [(r, -g) for r, g in adds]
        if kind == 0:
            yield from split(h, buf + step, start, high, first)
            yield from split(h, buf + step, start + h, low, minus(second))
        elif kind == 1:
            yield from split(h, buf + step, start + h, high, minus(first))
            yield from split(h, buf + step, start, low, second)
        else:
            yield from split(h, buf + step, start, low, first)
            yield from split(h, buf + step, start + h, high, minus(second))
    return list(split(ROW, 0, 0, (), [(0, 1)]))


def vector_parts(xs):
    parts = {(): xs}
    size = len(xs)
    while size > LEAF:
        size //= 2
        parts = {
            k + (m,): y
            for k, v in parts.items()
            for m, y in ((0, v[:size]), (1, v[size:]), (2, [a + b for a, b in zip(v[:size], v[size:])]))
        }
    return parts


KEYS = sorted(vector_parts([0] * ROW))
COUNT = len(KEYS)


def conv_kernel(
    dims, limits, near, proj, up12, up0, down0, down12, grads, all_short, all_long,
    gated, mixed, sums,
    s0, s1, s2, go, f0, f1, f2, prod, back, prod_less, back_less, leaves_l, seen, car, gf, acc, taps, taps_sums, few, out, short, long, tap_sem,
):
    rows, far, pad, short_w, long_w, spans, groups, seg, tail = dims

    def spread_rows(dst, at, pieces):
        size = dst.shape[0] // ROW
        for span in range(spans):
            base = span * seg + at
            for start, count, read in pieces:
                low, high = max(base, start), min(base + size, start + count)
                if low >= high:
                    continue
                for g in range(groups):
                    x = read(low - start, high - low, slice(g * LANES, (g + 1) * LANES)).astype(F32)
                    dst[pl.ds((low - base) * ROW + span * groups + g, high - low, stride=ROW), :] = x

    def piece(ref, start, *lead):
        return start, ref.shape[-2], lambda r, n, c: ref[(*lead, slice(r, r + n), c)]

    width = long.shape[1]
    mine = at_cols(lax.axis_index("ctx") % 2 * width, width)
    get_short = local(all_short.at[:, :, mine], short, tap_sem.at[0])
    get_long = local(all_long.at[:, mine], long, tap_sem.at[1])
    get_short.start()
    get_long.start()
    spread_rows(s0, -pad, [piece(up0, -pad), piece(proj, 0, 0), piece(down0, rows)])
    for k, dst in ((0, s1), (1, s2)):
        spread_rows(dst, -far, [piece(up12, -far, k), piece(proj, 0, 1 + k), piece(down12, rows, k)])
    spread_rows(go, 0, [piece(grads, 0)])
    get_short.wait()
    get_long.wait()
    for span in range(spans):
        for g in range(groups):
            c = slice(g * LANES, (g + 1) * LANES)
            taps[pl.ds(span * groups + g, long_w, stride=ROW), :] = long[:, c]
            for s in range(3):
                few[pl.ds(s * short_w * ROW + span * groups + g, short_w, stride=ROW), :] = short[s, :, c]

    def tile(ref, i):
        return ref[pl.ds(pl.multiple_of(i * ROW, ROW), ROW), :]

    def put(ref, i, x):
        ref[pl.ds(pl.multiple_of(i * ROW, ROW), ROW), :] = x

    def rounded(x):
        return x.astype(BF16).astype(F32)

    side = lax.broadcasted_iota(jnp.int32, (ROW, LANES), 0) // groups

    def bound(kind, i):
        x = jnp.full((ROW, LANES), near[kind, 0, i], jnp.int32)
        for span in range(1, spans):
            x = jnp.where(side == span, near[kind, span, i], x)
        return x

    def lead_short(ref, s, i0, off, r0, masked):
        xs = [tile(ref, i0 + off - short_w + 1 + k) for k in range(ROW + short_w - 1)]
        hs = [few[pl.ds((s * short_w + j) * ROW, ROW), :] for j in range(short_w)]
        res = []
        for b in range(ROW):
            total = hs[0] * xs[b + short_w - 1]
            if masked:
                far_b = bound(0, r0 + b)
                total = jnp.where(far_b >= 0, total, 0.0)
            for j in range(1, short_w):
                x = xs[b + short_w - 1 - j]
                if masked:
                    x = jnp.where(far_b >= j, x, 0.0)
                total = total + hs[j] * x
            res.append(total)
        return res

    lead = long_w

    def before(k, masked):
        i0 = k * ROW
        a = lead_short(s1, 1, i0, far - lead, i0, masked)
        for b in range(ROW):
            put(f1, i0 + b, a[b])
        d = lead_short(s2, 2, i0, far - lead, i0, masked)
        for b in range(ROW):
            put(f2, i0 + b, d[b])
            put(prod, i0 + b, rounded(a[b] * d[b]))

    def after(k, masked):
        i0 = k * ROW
        a = lead_short(s0, 0, i0, pad, i0 + lead, masked)
        for b in range(ROW):
            put(f0, i0 + b, a[b])
            put(back, i0 + b, rounded(tile(go, i0 + b) * a[b]))

    def pick(body, least, k):
        clear = limits[0, least] >= short_w - 1

        @pl.when(clear)
        def _():
            body(k, False)

        @pl.when(jnp.logical_not(clear))
        def _():
            body(k, True)

    count = (lead + seg + tail) // ROW
    lax.fori_loop(0, count, lambda k, _: (pick(before, k, k), 0)[1], 0)
    lax.fori_loop(0, count, lambda k, _: (pick(after, k + lead // ROW, k), 0)[1], 0)
    def differ(dst, ref):
        def step(k, _):
            for b in range(ROW):
                i = k * ROW + b
                x = [tile(ref, i + m) for m in (0, 4, 2, 6)]
                put(dst.at[0], i, x[0] - x[1])
                if LEAF < 4:
                    put(dst.at[1], i, x[0] - x[2])
                    put(dst.at[2], i, (x[0] - x[1]) - (x[2] - x[3]))
            return 0

        ref[pl.ds(count * ROW * ROW, ROW * ROW), :] = jnp.zeros((ROW * ROW, LANES), F32)
        lax.fori_loop(0, count, step, 0)

    differ(prod_less, prod)
    differ(back_less, back)

    def put_parts(ref, i, xs):
        parts = vector_parts(xs)
        for n, key in enumerate(KEYS):
            for m in range(LEAF):
                put(ref, (i * COUNT + n) * LEAF + m, parts[key][m])

    def tap_sums(k, _):
        put_parts(taps_sums, k, [tile(taps, k * ROW + j) for j in range(ROW)])
        return 0

    lax.fori_loop(0, long_w // ROW, tap_sums, 0)

    def products(kind, entry, vec, emit=None):
        res = []
        for buf, start, key, _ in leaves(kind):
            n = KEYS.index(key)
            es = [entry(buf, start + m) for m in range(2 * LEAF - 1)]
            vs = [vec(n * LEAF + m) for m in range(LEAF)]
            for r in range(LEAF):
                total = None
                for m in range(LEAF):
                    at = {0: LEAF - 1 + r - m, 1: LEAF - 1 + m - r, 2: r + m}[kind]
                    term = es[at] * vs[m]
                    total = term if total is None else total + term
                if emit:
                    emit(len(res), total)
                res.append(total)
        return res

    def joined(kind, parts):
        res = [None] * ROW
        for n, (_, _, _, adds) in enumerate(leaves(kind)):
            for r, g in adds:
                for m in range(LEAF):
                    x = parts[n * LEAF + m]
                    at = r + m
                    if res[at] is None:
                        res[at] = x if g > 0 else -x
                    else:
                        res[at] = res[at] + x if g > 0 else res[at] - x
        return res

    def cached(ref, less):
        got = {}

        def entry_at(base):
            def entry(buf, m):
                if (buf, m) not in got:
                    got[buf, m] = tile(ref if buf == 0 else less.at[{1: 0, 2: 1, 3: 2}[buf]], base + m)
                return got[buf, m]
            return entry
        return entry_at

    def derived(xs):
        got = {(0, m): x for m, x in enumerate(xs)}

        def entry(buf, m):
            if (buf, m) not in got:
                low, step = {1: (0, 4), 2: (0, 2), 3: (1, 2)}[buf]
                got[buf, m] = entry(low, m) - entry(low, m + step)
            return got[buf, m]
        return entry

    acc[...] = jnp.zeros_like(acc)
    leaves_l[...] = jnp.zeros_like(leaves_l)
    zero = jnp.zeros((ROW, LANES), F32)

    def long_block(k, own):
        i0 = k * ROW
        if own:
            put_parts(seen, 0, [tile(back, i0 + b) for b in range(ROW)])
        size = COUNT * LEAF

        def before_window(j0):
            xs = [tile(prod, i0 + lead - j0 - ROW + 1 + m) for m in range(2 * ROW - 1)]
            reach = bound(0, i0 + lead) - j0
            return [jnp.where(reach >= ROW - 1 - m, x, 0.0) for m, x in enumerate(xs)]

        def after_window(j0):
            ys = [tile(back, i0 + j0 + m) for m in range(2 * ROW - 1)]
            room = bound(1, i0 + ROW - 1) + (ROW - 1 - j0)
            return [jnp.where(room >= m, y, 0.0) for m, y in enumerate(ys)]

        def ahead(jb, carry, masked):
            j0 = jb * ROW
            entry = derived(before_window(j0)) if masked else cached(prod, prod_less)(i0 + lead - j0 - ROW + 1)
            parts = products(0, entry, lambda n: tile(taps_sums, jb * size + n))
            carry = tuple(c + x for c, x in zip(carry, parts))
            if own:
                def added(n, x):
                    put(leaves_l, jb * size + n, tile(leaves_l, jb * size + n) + x)

                products(1, entry, lambda n: tile(seen, n), added)
            return carry

        def ahead_rows(jb, carry, first):
            j0 = jb * ROW
            reach = [bound(0, i0 + lead + b) - j0 for b in range(ROW)]
            hs = [tile(taps, j0 + j) for j in range(ROW)]
            if first:
                xs = [tile(prod, i0 + lead - j0 - ROW + 1 + m) for m in range(2 * ROW - 1)]
            else:
                xs = before_window(j0)
            total = [zero] * ROW
            if own:
                zs = [tile(back, i0 + b) for b in range(ROW)]
                if not first:
                    zs = [jnp.where(reach[b] >= 0, z, 0.0) for b, z in enumerate(zs)]
                parts = [tile(acc, j0 + j) for j in range(ROW)]
            for j in range(ROW):
                for b in range(ROW):
                    x = xs[b - j + ROW - 1]
                    if first:
                        x = jnp.where(reach[b] >= j, x, 0.0)
                    total[b] = total[b] + hs[j] * x
                    if own:
                        parts[j] = parts[j] + zs[b] * x
            if own:
                for j in range(ROW):
                    put(acc, j0 + j, parts[j])
            if not first:
                total = [jnp.where(reach[b] >= 0, x, 0.0) for b, x in enumerate(total)]
            return tuple(c + x for c, x in zip(carry, total))

        def behind(jb, carry, masked):
            j0 = jb * ROW
            entry = derived(after_window(j0)) if masked else cached(back, back_less)(i0 + j0)
            parts = products(2, entry, lambda n: tile(taps_sums, jb * size + n))
            return tuple(c + x for c, x in zip(carry, parts))

        def behind_rows(jb, carry, first):
            j0 = jb * ROW
            room = [bound(1, i0 + b) - j0 for b in range(ROW)]
            hs = [tile(taps, j0 + j) for j in range(ROW)]
            ys = [tile(back, i0 + j0 + m) for m in range(2 * ROW - 1)] if first else after_window(j0)
            total = [zero] * ROW
            for j in range(ROW):
                for b in range(ROW):
                    y = ys[b + j]
                    if first:
                        y = jnp.where(room[b] >= j, y, 0.0)
                    total[b] = total[b] + hs[j] * y
            if not first:
                total = [jnp.where(room[b] >= 0, x, 0.0) for b, x in enumerate(total)]
            return tuple(c + x for c, x in zip(carry, total))

        even = limits[4, k + lead // ROW] == 1

        def all_of(kind, low, high, at, whole, by_row):
            some = jnp.minimum((limits[high, at] + ROW) // ROW, long_w // ROW)
            full = jnp.where(even, jnp.minimum((limits[low, at] + 1) // ROW, long_w // ROW), 0)
            middle = jnp.where(even, some, 0)
            pairs = jnp.where(even, some, jnp.minimum(some, 1))
            pairs_of = full // 2

            def two_steps(m, c):
                return whole(2 * m + 1, whole(2 * m, c, False), False)

            total = lax.fori_loop(0, pairs_of, two_steps, (zero,) * size)
            total = lax.fori_loop(2 * pairs_of, full, lambda j, c: whole(j, c, False), total)
            total = lax.fori_loop(full, middle, lambda j, c: whole(j, c, True), total)
            total = tuple(joined(kind, total))
            total = lax.fori_loop(middle, pairs, lambda j, c: by_row(j, c, True), total)
            return lax.fori_loop(pairs, some, lambda j, c: by_row(j, c, False), total)

        carry = all_of(0, 0, 1, k + lead // ROW, ahead, ahead_rows)
        grad = all_of(2, 2, 3, k, behind, behind_rows)
        for b in range(ROW):
            put(gf.at[0], i0 + b, rounded(tile(go, i0 + b) * carry[b]))
            put(gf.at[1], i0 + b, rounded(grad[b] * tile(f2, i0 + lead + b)))
            put(gf.at[2], i0 + b, rounded(grad[b] * tile(f1, i0 + lead + b)))
            if own:
                put(car, i0 + b, tile(f0, i0 + b) * carry[b])

    lax.fori_loop(0, seg // ROW, lambda k, _: (long_block(k, True), 0)[1], 0)
    for k in range(seg // ROW, (seg + tail) // ROW):
        long_block(k, False)

    def join_long(k, _):
        got = joined(1, [tile(leaves_l, k * COUNT * LEAF + n) for n in range(COUNT * LEAF)])
        for j in range(ROW):
            put(acc, k * ROW + j, tile(acc, k * ROW + j) + got[j])
        return 0

    lax.fori_loop(0, long_w // ROW, join_long, 0)

    def last(k, carry, s, src, off, masked):
        i0 = k * ROW
        ys = [tile(gf.at[s], i0 + m) for m in range(ROW + short_w - 1)]
        xs = [tile(src, i0 + off - short_w + 1 + m) for m in range(ROW + short_w - 1)]
        hs = [few[pl.ds((s * short_w + j) * ROW, ROW), :] for j in range(short_w)]
        parts = list(carry)
        for b in range(ROW):
            total = None
            if masked:
                room, reach = bound(1, i0 + b), bound(0, i0 + lead + b)
            for j in range(short_w):
                y, x = ys[b + j], xs[b + short_w - 1 - j]
                if masked:
                    y = jnp.where(room >= j, y, 0.0)
                    x = jnp.where(reach >= j, x, 0.0)
                total = hs[j] * y if total is None else total + hs[j] * y
                parts[j] = parts[j] + ys[b] * x
            put(out.at[s], i0 + b, total)
        return tuple(parts)

    for s, src, off in ((0, s0, pad), (1, s1, far), (2, s2, far)):
        def step(k, carry, s=s, src=src, off=off):
            least = jnp.minimum(limits[0, k + lead // ROW], limits[2, k])
            return lax.cond(
                least >= short_w - 1,
                lambda: last(k, carry, s, src, off, False),
                lambda: last(k, carry, s, src, off, True),
            )

        parts = lax.fori_loop(0, seg // ROW, step, (zero,) * short_w)
        for j in range(short_w):
            put(acc, long_w + s * ROW + j, parts[j])

    total_rows = acc.shape[0] // ROW
    for g in range(groups):
        c = slice(g * LANES, (g + 1) * LANES)
        total = None
        for span in range(spans):
            r = span * groups + g
            own = pl.ds(span * seg, seg)
            gated[own, c] = car[pl.ds(r, seg, stride=ROW), :].astype(BF16)
            for s in range(3):
                mixed[s, own, c] = out[s, pl.ds(r, seg, stride=ROW), :].astype(BF16)
            x = acc[pl.ds(r, total_rows, stride=ROW), :]
            total = x if total is None else total + x
        sums[:, c] = total.astype(BF16)


def conv_block(proj, up12, up0, down0, down12, grad_out, short_taps, long_taps, contig_lengths):
    _, rows, chans = proj.shape
    short_w, long_w = short_taps.shape[1], long_taps.shape[0]
    far, pad = up12.shape[1], up0.shape[0]
    groups = chans // LANES
    spans = ROW // groups
    seg, tail = rows // spans, ROW
    lead = long_w

    offset = lax.axis_index("ctx") // 2 * rows
    order = jnp.arange(contig_lengths.shape[0], dtype=jnp.int32)
    ends = jnp.sum(jnp.where(order[None, :] <= order[:, None], contig_lengths[None, :], 0), axis=1)
    begins = ends - contig_lengths
    span = jnp.arange(spans, dtype=jnp.int32) * seg
    count = lead + seg + tail + lead
    at = offset - lead + jnp.arange(count, dtype=jnp.int32)[:, None] + span[None, :]
    first = jnp.max(jnp.where(begins[None, None, :] <= at[:, :, None], begins[None, None, :], 0), axis=2)
    reach = at - first
    here = at[lead : lead + seg + tail]
    end = jnp.min(jnp.where(ends[None, None, :] > here[:, :, None], ends[None, None, :], jnp.int32(2**30)), axis=2)
    room = end - 1 - here

    near = jnp.stack([reach.T, jnp.pad(room.T, ((0, 0), (0, count - room.shape[0])))])

    def blocks(x, how):
        return jnp.pad(how(x.reshape(-1, ROW * spans), axis=1), (0, (count - x.shape[0]) // ROW))

    limits = jnp.stack([
        blocks(reach, jnp.min), blocks(reach, jnp.max), blocks(room, jnp.min), blocks(room, jnp.max),
        jnp.all(reach[ROW - 1 :: ROW] - reach[::ROW] == ROW - 1, axis=1).astype(jnp.int32),
    ])

    def vmem(n):
        return pltpu.VMEM((n * ROW, LANES), F32)

    dims = (rows, far, pad, short_w, long_w, spans, groups, seg, tail)
    size = lead + seg + tail
    in_vmem = pl.BlockSpec(memory_space=pltpu.VMEM)
    return pl.pallas_call(
        lambda *refs: conv_kernel(dims, *refs),
        in_specs=[pl.BlockSpec(memory_space=pltpu.SMEM)] * 2 + [in_vmem] * 6 + [pl.BlockSpec(memory_space=pl.ANY)] * 2,
        out_specs=[in_vmem] * 3,
        out_shape=[
            jax.ShapeDtypeStruct((rows, chans), BF16),
            jax.ShapeDtypeStruct((3, rows, chans), BF16),
            jax.ShapeDtypeStruct((long_w + 4 * ROW, chans), BF16),
        ],
        scratch_shapes=[
            vmem(pad + seg + far), vmem(far + seg + pad), vmem(far + seg + pad), vmem(seg + far),
            vmem(size), vmem(size), vmem(size), vmem(size + ROW), vmem(size + ROW),
            pltpu.VMEM((3, size * ROW, LANES), F32), pltpu.VMEM((3, size * ROW, LANES), F32),
            vmem(long_w // ROW * COUNT * LEAF), vmem(COUNT * LEAF), vmem(seg + tail),
            pltpu.VMEM((3, (seg + 2 * tail) * ROW, LANES), F32),
            vmem(long_w + 4 * ROW), vmem(long_w), vmem(long_w // ROW * COUNT * LEAF), vmem(3 * short_w),
            pltpu.VMEM((3, seg * ROW, LANES), F32),
            pltpu.VMEM((3, short_w, chans), F32), pltpu.VMEM((long_w, chans), F32), pltpu.SemaphoreType.DMA((2,)),
        ],
        compiler_params=pltpu.CompilerParams(vmem_limit_bytes=56 << 20),
        cost_estimate=pl.CostEstimate(
            flops=rows * chans * long_w * 1000, bytes_accessed=rows * chans * 24, transcendentals=0
        ),
        name="hyena_filters",
    )(limits, near, proj, up12, up0, down0, down12, grad_out, short_taps, long_taps)


def deliver(weights, tokens, gated, filters, long_w, short_w):
    streams, feats, chans = weights.shape

    steps = 4
    extra = filters.shape[0] - long_w

    def kernel(w, t, g, f, few, w_out, t_out, g_out, short_out, long_out):
        w_out[...] = w[...]
        t_out[...] = t[...]
        g_out[...] = g[...]
        long_out[...] = f[...]

        @pl.when(pl.program_id(0) == 0)
        def _():
            for s in range(streams):
                short_out[s] = few[pl.ds(ROW * s, short_w), :]

    def rows_of(count, width):
        return pl.BlockSpec((count // steps, width), lambda i: (i, 0))

    part = pl.BlockSpec((streams, feats // steps, chans), lambda i: (0, i, 0))
    short_shape = (streams, short_w, chans)
    parts = [part, rows_of(*tokens.shape), rows_of(*gated.shape)]
    return pl.pallas_call(
        kernel,
        grid=(steps,),
        in_specs=parts + [
            rows_of(long_w, chans), pl.BlockSpec((extra, chans), lambda i: (long_w // extra, 0)),
        ],
        out_specs=parts + [pl.BlockSpec(short_shape, lambda i: (0, 0, 0)), rows_of(long_w, chans)],
        out_shape=[
            jax.ShapeDtypeStruct(weights.shape, BF16),
            jax.ShapeDtypeStruct(tokens.shape, BF16),
            jax.ShapeDtypeStruct(gated.shape, BF16),
            jax.ShapeDtypeStruct(short_shape, F32),
            jax.ShapeDtypeStruct((long_w, chans), F32),
        ],
        compiler_params=pltpu.CompilerParams(vmem_limit_bytes=56 << 20),
        cost_estimate=pl.CostEstimate(flops=0, bytes_accessed=4 * weights.size, transcendentals=0),
        name="deliver",
    )(weights, tokens, gated, filters, filters)


def on_device(loaded, slot_pos, contig_lengths, w_in, short_taps, long_taps, grad_out):
    me = lax.axis_index("ctx")
    core = me % 2
    chans = grad_out.shape[1]
    short_w, long_w = short_taps.shape[1], long_taps.shape[0]
    far, pad = round_up(long_w, 16) + 16, 16
    n_ctx = lax.axis_size("ctx")

    proj, up12, up0, down0, down12, grad_c, wall, *turned = gather(
        jnp.transpose(w_in, (1, 0, 2)), loaded[0], slot_pos, grad_out, far, pad
    )
    turned = [swapped(x, 2 * m) if m else x for m, x in enumerate(turned)]
    gated, grads, sums = conv_block(
        proj, up12, up0, down0, down12, grad_c, short_taps, long_taps, contig_lengths
    )
    results = reduce(grads, wall, gated, sums, turned)
    weight_grads, token_grads, gated_out, short_total, long_total = deliver(*results, long_w, short_w)
    return gated_out, token_grads, jnp.transpose(weight_grads, (1, 0, 2)), short_total, long_total


def solution(mesh):
    in_specs = (
        P("ctx", None, None, "fsdp"),
        P("ctx", None, None),
        P(),
        P("ctx", None, "fsdp"),
        P(None, None, "fsdp"),
        P(None, "fsdp"),
        P("ctx", "fsdp"),
    )
    out_specs = (
        P("ctx", "fsdp"),
        P("ctx", "fsdp"),
        P("ctx", None, "fsdp"),
        P(None, None, "fsdp"),
        P(None, "fsdp"),
    )
    return jax.shard_map(
        on_device, mesh=mesh, in_specs=in_specs, out_specs=out_specs, check_vma=False
    )
```

```python
import jax
import jax.numpy as jnp
from jax import lax
from jax.experimental import pallas as pl
from jax.experimental.pallas import tpu as pltpu
from jax.sharding import PartitionSpec as P

LANES = 128
F32, BF16 = jnp.float32, jnp.bfloat16


def round_up(x, to):
    return -(-x // to) * to


def swapped(x, mask):
    size = lax.axis_size("ctx")
    return lax.ppermute(x, "ctx", [(i, i ^ mask) for i in range(size)])


def chip_masks(size):
    masks, step = [], 2
    while step < size:
        masks.append(step)
        step *= 2
    return masks


def walk(masks):
    held = [0]
    for mask in masks:
        held = held + [k ^ mask for k in held]
    return held


def half(x, dim, which):
    width = x.shape[dim] // 2
    return lax.dynamic_slice_in_dim(x, which * width, width, dim)


def remote(src, dst, send, recv, **place):
    return pltpu.make_async_remote_copy(
        src_ref=src, dst_ref=dst, send_sem=send, recv_sem=recv,
        device_id=place, device_id_type=pl.DeviceIdType.MESH,
    )


def local(src, dst, sem):
    return pltpu.make_async_copy(src, dst, sem)


def at_cols(start, size):
    return pl.ds(pl.multiple_of(start, LANES), size)


def greet(n_ctx, n_line):
    me, z = lax.axis_index("ctx"), lax.axis_index("fsdp")
    barrier = pltpu.get_barrier_semaphore()
    others = [1] + [k for k in range(2, n_ctx, 2)]
    for k in others:
        pl.semaphore_signal(
            barrier, inc=1, device_id={"ctx": me ^ k}, device_id_type=pl.DeviceIdType.MESH
        )

    @pl.when(z > 0)
    def _():
        pl.semaphore_signal(
            barrier, inc=1, device_id={"fsdp": z - 1}, device_id_type=pl.DeviceIdType.MESH
        )

    @pl.when(z < n_line - 1)
    def _():
        pl.semaphore_signal(
            barrier, inc=1, device_id={"fsdp": z + 1}, device_id_type=pl.DeviceIdType.MESH
        )

    ends = jnp.where(z > 0, 1, 0) + jnp.where(z < n_line - 1, 1, 0)
    pl.semaphore_wait(barrier, len(others) + ends)


class Spread:
    def __init__(self, buf, send, recv, masks, me):
        self.buf, self.send, self.recv, self.me = buf, send, recv, me
        self.orders = (masks, masks[::-1])
        self.keys = tuple(walk(m) for m in self.orders)
        self.count = 1 << len(masks)

    def copy(self, chain, stage, i):
        to = (1 << stage) + i
        return remote(
            self.buf.at[chain, i], self.buf.at[chain, to],
            self.send.at[chain, to], self.recv.at[chain, to],
            ctx=self.me ^ self.orders[chain][stage],
        )

    def stages(self, i):
        return range(i.bit_length(), len(self.orders[0]))

    def start(self, chain, i, stages=None):
        for stage in self.stages(i) if stages is None else stages:
            self.copy(chain, stage, i).start()

    def arrive(self, chain, i):
        stage = i.bit_length() - 1
        self.copy(chain, stage, i - (1 << stage)).wait_recv()

    def finish(self):
        for chain in (0, 1):
            for i in range(self.count):
                for stage in self.stages(i):
                    self.copy(chain, stage, i).wait_send()


def gather_kernel(
    sizes, w, slots, pos, grad,
    proj, up12, up0, down0, down12, gext, wall, *rest
):
    n_ctx, n, far, pad = sizes
    turned, rest = rest[: n_ctx // 2], rest[n_ctx // 2 :]
    gather_body(n_ctx, n, far, pad, w, slots, pos, grad, proj, up12, up0, down0, down12, gext, wall, turned, *rest)


def gather_body(
    n_ctx, n, far, pad, w, slots, pos, grad,
    proj, up12, up0, down0, down12, gext, wall, turned,
    tbuf, wbuf, xbuf, sbuf, pbuf, part, ppart, acc,
    w_send, w_recv, s_send, s_recv, up_send, up_recv, dn_send, dn_recv,
    core_send, core_recv, misc_send, misc_recv, local_sem, out_sem, halo_send, halo_recv, turn_sem,
):
    me, z = lax.axis_index("ctx"), lax.axis_index("fsdp")
    core, chip = me % 2, me // 2
    chips = n_ctx // 2
    rows, dz = ppart.shape
    streams, feats, ch = wbuf.shape[2:]
    masks = chip_masks(n_ctx)
    greet(n_ctx, n)

    sib = me ^ 1
    own_pos = local(pos.at[0], pbuf.at[core], local_sem.at[0])
    own_pos.start()
    send_pos = remote(pos.at[0], pbuf.at[core], misc_send.at[0], misc_recv.at[0], ctx=sib)
    send_pos.start()
    own_slots = local(slots.at[pl.ds(2 * chip, 2)], sbuf.at[chip], local_sem.at[1])
    own_slots.start()
    deals = []
    for k in range(2, n_ctx, 2):
        to = me ^ k
        deals.append(remote(
            slots.at[pl.ds(to - core, 2)], sbuf.at[chip], s_send.at[k // 2], s_recv.at[k // 2], ctx=to
        ))
        deals[-1].start()
    own_w = local(w.at[:, :, at_cols(core * ch, ch)], wbuf.at[0, 0], local_sem.at[2])
    own_w.start()
    send_w = remote(
        w.at[:, :, at_cols((1 - core) * ch, ch)], wbuf.at[1, 0], misc_send.at[1], misc_recv.at[1], ctx=sib
    )
    send_w.start()
    own_rows = pl.ds(pl.multiple_of(core * rows, rows), rows)
    own_grad = local(grad.at[:, at_cols(core * ch, ch)], gext.at[own_rows], local_sem.at[3])
    own_grad.start()
    send_grad = remote(
        grad.at[:, at_cols((1 - core) * ch, ch)], gext.at[own_rows], misc_send.at[3], misc_recv.at[3], ctx=sib
    )
    send_grad.start()
    spread = Spread(wbuf, w_send, w_recv, masks, me)
    stages = len(masks)
    keep = []

    def stored(chain, i):
        keep.append(local(wbuf.at[chain, i], wall.at[chain, i], out_sem.at[chain, i]))
        keep[-1].start()

    own_w.wait()
    spread.start(0, 0, range(0, min(1, stages)))
    stored(0, 0)
    send_w.wait_recv()
    spread.start(1, 0, range(0, min(1, stages)))
    stored(1, 0)

    own_pos.wait()
    send_pos.wait_recv()
    own_slots.wait()
    for deal in deals:
        deal.wait_recv()
    spread.start(0, 0, range(1, stages))
    spread.start(1, 0, range(1, stages))

    seat = lax.broadcasted_iota(jnp.int32, (rows, pos.shape[2]), 0)

    def place(b):
        total = None
        for c in range(chips):
            row = pbuf[b, pl.ds(2 * c + core, 1), :]
            pick = jnp.where(row == seat, 1.0, 0.0).astype(BF16)
            term = jnp.dot(pick, sbuf[c, b], preferred_element_type=F32)
            total = term if total is None else total + term
        return total.astype(BF16)

    part[...] = place(1 - core)
    give = remote(part, ppart, misc_send.at[2], misc_recv.at[2], ctx=sib)
    give.start()
    mine = place(core)
    give.wait_recv()
    own_grad.wait()
    send_grad.wait_recv()
    edge_grad = remote(
        gext.at[pl.ds(0, far)], gext.at[pl.ds(2 * rows, far)], misc_send.at[4], misc_recv.at[4], ctx=me - 2
    )

    @pl.when(chip > 0)
    def _():
        edge_grad.start()

    xbuf[own_rows, at_cols(z * dz, dz)] = mine + ppart[...]

    def tile(t):
        return xbuf.at[own_rows, at_cols(t * dz, dz)]

    def to_core(t):
        return remote(tile(t), tile(t), core_send.at[t], core_recv.at[t], ctx=sib)

    def other_tile(t):
        there = xbuf.at[pl.ds(pl.multiple_of((1 - core) * rows, rows), rows), at_cols(t * dz, dz)]
        return remote(there, there, core_send.at[t], core_recv.at[t], ctx=sib)

    def up(h, t):
        return remote(tile(t), tile(t), up_send.at[h], up_recv.at[h], fsdp=z + 1)

    def down(h, t):
        return remote(tile(t), tile(t), dn_send.at[h], dn_recv.at[h], fsdp=z - 1)

    to_core(z).start()
    for h in range(1, n):
        @pl.when((z < n - 1) & (z - h + 1 >= 0))
        def _():
            up(h, z - h + 1).start()

        @pl.when((z > 0) & (z + h - 1 <= n - 1))
        def _():
            down(h, z + h - 1).start()

        @pl.when(z - h >= 0)
        def _():
            up(h, z - h).wait_recv()
            to_core(z - h).start()

        @pl.when(z + h <= n - 1)
        def _():
            down(h, z + h).wait_recv()
            to_core(z + h).start()

        if h == 1 and spread.count > 1:
            for chain in (0, 1):
                spread.arrive(chain, 1)
                spread.start(chain, 1)
                stored(chain, 1)
    for t in range(n):
        other_tile(t).wait_recv()
    for m in range(chips):
        tbuf[m] = xbuf[:, at_cols((me ^ (2 * m)) * feats, feats)].T
        keep.append(local(tbuf.at[m], turned[m], turn_sem.at[m]))
        keep[-1].start()

    def term(chain, i, s):
        cols = at_cols((me ^ chain ^ spread.keys[chain][i]) * feats, feats)
        return jnp.dot(xbuf[:, cols], wbuf[chain, i, s], preferred_element_type=F32)

    final = spread.count - 1
    for i in range(spread.count):
        for chain in (0, 1):
            if i > 1:
                spread.arrive(chain, i)
                spread.start(chain, i)
                stored(chain, i)
            if i == final:
                continue

            def one(s, _, chain=chain, i=i):
                total = term(chain, i, s)
                acc[s] = total if i == 0 and chain == 0 else total + acc[s]
                return 0

            lax.fori_loop(0, streams, one, 0)

    total = 2 * rows

    def halos(s, up_to, down_to):
        top, bottom = (up0, down0) if s == 0 else (up12.at[s - 1], down12.at[s - 1])
        high, low = (pad, far) if s == 0 else (far, pad)
        return (
            remote(proj.at[s, pl.ds(total - high, high)], top, halo_send.at[s], halo_recv.at[s], ctx=up_to),
            remote(proj.at[s, pl.ds(0, low)], bottom, halo_send.at[3 + s], halo_recv.at[3 + s], ctx=down_to),
        )

    edges = [halos(s, me + 2, me - 2) for s in range(streams)]
    for s in (1, 2, 0):
        proj[s] = (acc[s] + term(0, final, s) + term(1, final, s)).astype(BF16)

        @pl.when(chip < chips - 1)
        def _():
            edges[s][0].start()

        @pl.when(chip > 0)
        def _():
            edges[s][1].start()

    @pl.when(chip == 0)
    def _():
        up12[...] = jnp.zeros_like(up12)
        up0[...] = jnp.zeros_like(up0)

    @pl.when(chip == chips - 1)
    def _():
        gext[pl.ds(2 * rows, far), :] = jnp.zeros((far, ch), BF16)
        down0[...] = jnp.zeros_like(down0)
        down12[...] = jnp.zeros_like(down12)

    @pl.when(chip > 0)
    def _():
        for up_edge, down_edge in edges:
            up_edge.wait_recv()
            down_edge.wait_send()
        edge_grad.wait_send()

    @pl.when(chip < chips - 1)
    def _():
        for up_edge, down_edge in edges:
            down_edge.wait_recv()
            up_edge.wait_send()
        edge_grad.wait_recv()

    for h in range(1, n):
        @pl.when((z < n - 1) & (z - h + 1 >= 0))
        def _():
            up(h, z - h + 1).wait_send()

        @pl.when((z > 0) & (z + h - 1 <= n - 1))
        def _():
            down(h, z + h - 1).wait_send()
    for t in range(n):
        to_core(t).wait_send()
    for deal in deals + [send_pos, send_w, send_grad, give]:
        deal.wait_send()
    spread.finish()
    for copy in keep:
        copy.wait()


def gather(w, slots, pos, grad, far, pad):
    n_ctx, n = lax.axis_size("ctx"), lax.axis_size("fsdp")
    chips = n_ctx // 2
    streams, feats, two = w.shape
    ch, dz = two // 2, slots.shape[2]
    rows = grad.shape[0]
    total = 2 * rows
    any_space, vmem = pl.BlockSpec(memory_space=pl.ANY), pl.BlockSpec(memory_space=pltpu.VMEM)
    dma = pltpu.SemaphoreType.DMA

    def shape(*dims):
        return jax.ShapeDtypeStruct(dims, BF16)

    return pl.pallas_call(
        lambda *refs: gather_kernel((n_ctx, n, far, pad), *refs),
        in_specs=[any_space] * 4,
        out_specs=[vmem] * 6 + [any_space] * (1 + chips),
        out_shape=[
            shape(streams, total, ch), shape(2, far, ch), shape(pad, ch), shape(far, ch), shape(2, pad, ch),
            shape(total + far, ch),
            shape(2, chips, streams, feats, ch),
        ] + [shape(feats, total)] * chips,
        scratch_shapes=[
            pltpu.VMEM((chips, feats, total), BF16),
            pltpu.VMEM((2, chips, streams, feats, ch), BF16),
            pltpu.VMEM((total, n * dz), BF16),
            pltpu.VMEM((chips, 2, slots.shape[1], dz), BF16),
            pltpu.VMEM((2, *pos.shape[1:]), jnp.int32),
            pltpu.VMEM((rows, dz), BF16),
            pltpu.VMEM((rows, dz), BF16),
            pltpu.VMEM((streams, total, ch), F32),
            dma((2, chips)), dma((2, chips)), dma((chips,)), dma((chips,)),
            dma((n,)), dma((n,)), dma((n,)), dma((n,)),
            dma((n,)), dma((n,)), dma((5,)), dma((5,)), dma((4,)), dma((2, chips)), dma((6,)), dma((6,)), dma((chips,)),
        ],
        compiler_params=pltpu.CompilerParams(
            collective_id=0, has_side_effects=True, vmem_limit_bytes=56 << 20
        ),
        cost_estimate=pl.CostEstimate(
            flops=2 * total * n * dz * streams * ch, bytes_accessed=40 << 20, transcendentals=0
        ),
        name="gather_and_project",
    )(w, slots, pos, grad)


def reduce_kernel(
    sizes, grads, wall, gated, sums, *rest
):
    chips = sizes[0] // 2
    reduce_body(sizes, grads, wall, gated, sums, rest[:chips], *rest[chips:])


def reduce_body(
    sizes, grads, wall, gated, sums, turned,
    wg, tg, gout, filt,
    gbuf, lbuf, acc, wgb, wv, xp, xs, xr, up_tx, up_rx, dn_tx, dn_rx, fbuf, ftot,
    g_send, g_recv, f_send, f_recv, up_send, up_recv, dn_send, dn_recv,
    core_send, core_recv, misc_send, misc_recv, local_sem, wv_sem, t_sem, t_send, t_recv,
):
    n_ctx, n = sizes
    me, z = lax.axis_index("ctx"), lax.axis_index("fsdp")
    core, chip = me % 2, me // 2
    chips = n_ctx // 2
    streams, rows, ch = gbuf.shape[2:]
    feats = lbuf.shape[1]
    dz = xp.shape[1] // n
    masks = chip_masks(n_ctx)
    sib = me ^ 1
    own_g = [
        local(grads.at[:, pl.ds(b * rows, rows)], gbuf.at[b, 0], local_sem.at[b]) for b in (0, 1)
    ]
    for copy in own_g:
        copy.start()
    spread = Spread(gbuf, g_send, g_recv, masks, me)
    wkeys = (walk(masks), walk(masks[::-1]))
    order = [(chain, i) for i in range(chips) for chain in (0, 1)]

    def fetch(j):
        chain, i = order[j]
        return local(wall.at[chain, i], wv.at[j % 2], wv_sem.at[j % 2])

    fetch(0).start()
    lefts, trades = [], []
    for m in range(chips):
        cols = at_cols(((me - core) ^ (2 * m)) * rows, 2 * rows)
        lefts.append(local(turned[m], lbuf.at[0, :, cols], t_sem.at[m]))
        trades.append(remote(turned[m], lbuf.at[1, :, cols], t_send.at[m], t_recv.at[m], ctx=sib))
        lefts[-1].start()
    greet(n_ctx, n)
    for copy in own_g:
        copy.wait()
    for chain in (0, 1):
        spread.start(chain, 0)
    for trade in trades:
        trade.start()

    fbuf[chip] = sums[...]
    shares = []
    for k in range(2, n_ctx, 2):
        shares.append(remote(
            fbuf.at[chip], fbuf.at[chip], f_send.at[k // 2], f_recv.at[k // 2], ctx=me ^ k
        ))
    mine = at_cols(core * ch, ch)
    keep_gated = local(gated.at[pl.ds(core * rows, rows)], gout.at[:, mine], local_sem.at[3])
    give_gated = remote(
        gated.at[pl.ds((1 - core) * rows, rows)], gout.at[:, mine], misc_send.at[0], misc_recv.at[0], ctx=sib
    )
    keep_gated.start()
    give_gated.start()

    def to_core(block):
        cols = at_cols(block * feats, feats)
        return remote(xs.at[:, cols], xr.at[:, cols], core_send.at[block], core_recv.at[block], ctx=sib)

    for j, (chain, i) in enumerate(order):
        if j + 1 < len(order):
            fetch(j + 1).start()
        fetch(j).wait()
        block = me ^ chain ^ wkeys[chain][i]
        cols = at_cols(block * feats, feats)

        def back(b, j=j):
            total = None
            for s in range(streams):
                term = lax.dot_general(
                    gbuf[b, 0, s], wv[j % 2, s], (((1,), (1,)), ((), ())), preferred_element_type=F32
                )
                total = term if total is None else total + term
            return total

        xs[:, cols] = back(1 - core).astype(BF16)
        to_core(block).start()
        xp[:, cols] = back(core)

    step = 32

    def each(body):
        def one(r, _):
            body(pl.ds(pl.multiple_of(r * step, step), step))
            return 0

        lax.fori_loop(0, rows // step, one, 0)

    def weigh(chain, i, halves=(0, 1), end=False):
        where = ((me - core) ^ spread.keys[chain][i]) + chain
        cols = at_cols(where * rows, rows)
        first = i == 0 and chain == 0

        def one(r, _):
            h, s = r // streams, r % streams
            total = jnp.dot(lbuf[h, :, cols], gbuf[chain, i, s], preferred_element_type=F32)
            if not first:
                total = acc[r] + total
            if end:
                wgb[r] = total.astype(BF16)
            else:
                acc[r] = total
            return 0

        lax.fori_loop(halves[0] * streams, (halves[-1] + 1) * streams, one, 0)

    for block in range(n_ctx):
        to_core(block).wait_recv()
    for left, trade in zip(lefts, trades):
        left.wait()
        trade.wait_recv()

    def up(s):
        return remote(up_tx.at[s - 1], up_rx.at[s - 1], up_send.at[s], up_recv.at[s], fsdp=z + 1)

    def down(s):
        return remote(dn_tx.at[s - 1], dn_rx.at[s - 1], dn_send.at[s], dn_recv.at[s], fsdp=z - 1)

    zz = n - 1 - z

    def send_tile(s, a, far_end, tx, rx):
        cols = at_cols(a * dz, dz)

        @pl.when(far_end == 0)
        def _():
            def body(at):
                tx[s - 1, at] = (xp[at, cols] + xr[at, cols].astype(F32)).astype(BF16)
            each(body)

        if s >= 2:
            @pl.when(far_end > 0)
            def _():
                def body(at):
                    total = xp[at, cols] + xr[at, cols].astype(F32) + rx[s - 2, at].astype(F32)
                    tx[s - 1, at] = total.astype(BF16)
                each(body)

    def line_start(s):
        last = min(s - 1, n - 2)

        @pl.when(z <= last)
        def _():
            send_tile(s, n - s + z, z, up_tx, up_rx)
            up(s).start()

        @pl.when(zz <= last)
        def _():
            send_tile(s, z + s - n, zz, dn_tx, dn_rx)
            down(s).start()

    def line_wait(s):
        last = min(s - 1, n - 2)

        @pl.when((z >= 1) & (z - 1 <= last))
        def _():
            up(s).wait_recv()

        @pl.when((zz >= 1) & (zz - 1 <= last))
        def _():
            down(s).wait_recv()

    def finish_line():
        if n > 1:
            line_wait(n - 1)
        cols = at_cols(z * dz, dz)

        def final(at):
            acc_t = xp[at, cols] + xr[at, cols].astype(F32)
            if n > 1:
                acc_t = acc_t + jnp.where(z >= 1, up_rx[n - 2, at].astype(F32), 0.0)
                acc_t = acc_t + jnp.where(zz >= 1, dn_rx[n - 2, at].astype(F32), 0.0)
            tg[at] = acc_t.astype(BF16)

        each(final)

    if n > 1:
        line_start(1)
    sent = 1
    if spread.count == 1:
        finish_line()
    for i in range(spread.count):
        for chain in (0, 1):
            if i:
                spread.arrive(chain, i)
                spread.start(chain, i)
        if i == spread.count - 1:
            break
        for chain in (0, 1):
            weigh(chain, i)
        if i == spread.count - 2:
            while sent < n - 1:
                line_wait(sent)
                sent += 1
                line_start(sent)
            finish_line()
        elif sent < n - 1:
            line_wait(sent)
            sent += 1
            line_start(sent)
    for share in shares:
        share.start()
    give_w = remote(
        wgb.at[pl.ds(streams, streams)], wg.at[:, :, mine], misc_send.at[1], misc_recv.at[1], ctx=sib
    )
    keep_w = local(wgb.at[pl.ds(0, streams)], wg.at[:, :, mine], local_sem.at[4])
    for h, copy in ((1, give_w), (0, keep_w)):
        weigh(0, spread.count - 1, (h,))
        weigh(1, spread.count - 1, (h,), end=True)
        copy.start()
    for share in shares:
        share.wait_recv()
    total = fbuf[0].astype(F32)
    for c in range(1, chips):
        total = total + fbuf[c].astype(F32)
    ftot[...] = total
    give_f = remote(ftot, filt.at[:, mine], misc_send.at[2], misc_recv.at[2], ctx=sib)
    give_f.start()
    keep_f = local(ftot, filt.at[:, mine], local_sem.at[5])
    keep_f.start()

    for s in range(1, n):
        last = min(s - 1, n - 2)

        @pl.when(z <= last)
        def _():
            up(s).wait_send()

        @pl.when(zz <= last)
        def _():
            down(s).wait_send()
    for block in range(n_ctx):
        to_core(block).wait_send()
    spread.finish()
    for share in shares:
        share.wait_send()
    for trade in trades:
        trade.wait_send()
    for copy in (give_gated, give_w, give_f):
        copy.wait()
    for copy in (keep_gated, keep_w, keep_f):
        copy.wait()


def reduce(grads, wall, gated, sums, turned):
    n_ctx, n = lax.axis_size("ctx"), lax.axis_size("fsdp")
    chips = n_ctx // 2
    streams, total, ch = grads.shape
    rows = total // 2
    feats = turned[0].shape[0]
    dim = feats * n_ctx
    dz = dim // n
    any_space, vmem = pl.BlockSpec(memory_space=pl.ANY), pl.BlockSpec(memory_space=pltpu.VMEM)
    dma = pltpu.SemaphoreType.DMA
    hops = max(n - 1, 1)
    return pl.pallas_call(
        lambda *refs: reduce_kernel((n_ctx, n), *refs),
        in_specs=[any_space] * 3 + [vmem] + [any_space] * chips,
        out_specs=[any_space, vmem, any_space, any_space],
        out_shape=[
            jax.ShapeDtypeStruct((streams, feats, 2 * ch), BF16),
            jax.ShapeDtypeStruct((rows, dz), BF16),
            jax.ShapeDtypeStruct((rows, 2 * ch), BF16),
            jax.ShapeDtypeStruct((sums.shape[0], 2 * ch), F32),
        ],
        scratch_shapes=[
            pltpu.VMEM((2, chips, streams, rows, ch), BF16),
            pltpu.VMEM((2, feats, rows * n_ctx), BF16),
            pltpu.VMEM((2 * streams, feats, ch), F32),
            pltpu.VMEM((2 * streams, feats, ch), BF16),
            pltpu.VMEM((2, streams, feats, ch), BF16),
            pltpu.VMEM((rows, dim), F32),
            pltpu.VMEM((rows, dim), BF16),
            pltpu.VMEM((rows, dim), BF16),
            pltpu.VMEM((hops, rows, dz), BF16), pltpu.VMEM((hops, rows, dz), BF16),
            pltpu.VMEM((hops, rows, dz), BF16), pltpu.VMEM((hops, rows, dz), BF16),
            pltpu.VMEM((chips, *sums.shape), BF16),
            pltpu.VMEM(sums.shape, F32),
            dma((2, chips)), dma((2, chips)), dma((chips,)), dma((chips,)),
            dma((n,)), dma((n,)), dma((n,)), dma((n,)),
            dma((n_ctx,)), dma((n_ctx,)), dma((3,)), dma((3,)), dma((6,)), dma((2,)),
            dma((chips,)), dma((chips,)), dma((chips,)),
        ],
        compiler_params=pltpu.CompilerParams(
            collective_id=1, has_side_effects=True, vmem_limit_bytes=60 << 20
        ),
        cost_estimate=pl.CostEstimate(
            flops=4 * total * dim * streams * ch, bytes_accessed=40 << 20, transcendentals=0
        ),
        name="gather_and_reduce",
    )(grads, wall, gated, sums, *turned)


ROW = 8
LEAF = 2


def leaves(kind, size=ROW, buf=0, start=0, vec=(0, ROW), sign=1, rows=(0, ROW)):
    def split(size, buf, start, vec, adds):
        if size == LEAF:
            yield buf, start, vec, adds
            return
        h = size // 2
        step = {8: 1, 4: 2}[size]
        low, high, both = vec + (0,), vec + (1,), vec + (2,)
        yield from split(h, buf, start + h, both, adds + [(r + h, g) for r, g in adds])
        first = [(r, g) for r, g in adds]
        second = [(r + h, g) for r, g in adds]
        minus = lambda adds: [(r, -g) for r, g in adds]
        if kind == 0:
            yield from split(h, buf + step, start, high, first)
            yield from split(h, buf + step, start + h, low, minus(second))
        elif kind == 1:
            yield from split(h, buf + step, start + h, high, minus(first))
            yield from split(h, buf + step, start, low, second)
        else:
            yield from split(h, buf + step, start, low, first)
            yield from split(h, buf + step, start + h, high, minus(second))
    return list(split(ROW, 0, 0, (), [(0, 1)]))


def vector_parts(xs):
    parts = {(): xs}
    size = len(xs)
    while size > LEAF:
        size //= 2
        parts = {
            k + (m,): y
            for k, v in parts.items()
            for m, y in ((0, v[:size]), (1, v[size:]), (2, [a + b for a, b in zip(v[:size], v[size:])]))
        }
    return parts


KEYS = sorted(vector_parts([0] * ROW))
COUNT = len(KEYS)


def conv_kernel(
    dims, limits, near, proj, up12, up0, down0, down12, grads, all_short, all_long,
    gated, mixed, sums,
    s0, s1, s2, go, f0, f1, f2, prod, back, prod_less, back_less, leaves_l, seen, car, gf, acc, taps, taps_sums, few, out, short, long, tap_sem,
):
    rows, far, pad, short_w, long_w, spans, groups, seg, tail = dims

    def spread_rows(dst, at, pieces):
        size = dst.shape[0] // ROW
        for span in range(spans):
            base = span * seg + at
            for start, count, read in pieces:
                low, high = max(base, start), min(base + size, start + count)
                if low >= high:
                    continue
                for g in range(groups):
                    x = read(low - start, high - low, slice(g * LANES, (g + 1) * LANES)).astype(F32)
                    dst[pl.ds((low - base) * ROW + span * groups + g, high - low, stride=ROW), :] = x

    def piece(ref, start, *lead):
        return start, ref.shape[-2], lambda r, n, c: ref[(*lead, slice(r, r + n), c)]

    width = long.shape[1]
    mine = at_cols(lax.axis_index("ctx") % 2 * width, width)
    get_short = local(all_short.at[:, :, mine], short, tap_sem.at[0])
    get_long = local(all_long.at[:, mine], long, tap_sem.at[1])
    get_short.start()
    get_long.start()
    spread_rows(s0, -pad, [piece(up0, -pad), piece(proj, 0, 0), piece(down0, rows)])
    for k, dst in ((0, s1), (1, s2)):
        spread_rows(dst, -far, [piece(up12, -far, k), piece(proj, 0, 1 + k), piece(down12, rows, k)])
    spread_rows(go, 0, [piece(grads, 0)])
    get_short.wait()
    get_long.wait()
    for span in range(spans):
        for g in range(groups):
            c = slice(g * LANES, (g + 1) * LANES)
            taps[pl.ds(span * groups + g, long_w, stride=ROW), :] = long[:, c]
            for s in range(3):
                few[pl.ds(s * short_w * ROW + span * groups + g, short_w, stride=ROW), :] = short[s, :, c]

    def tile(ref, i):
        return ref[pl.ds(pl.multiple_of(i * ROW, ROW), ROW), :]

    def put(ref, i, x):
        ref[pl.ds(pl.multiple_of(i * ROW, ROW), ROW), :] = x

    def rounded(x):
        return x.astype(BF16).astype(F32)

    side = lax.broadcasted_iota(jnp.int32, (ROW, LANES), 0) // groups

    def bound(kind, i):
        x = jnp.full((ROW, LANES), near[kind, 0, i], jnp.int32)
        for span in range(1, spans):
            x = jnp.where(side == span, near[kind, span, i], x)
        return x

    def lead_short(ref, s, i0, off, r0, masked):
        xs = [tile(ref, i0 + off - short_w + 1 + k) for k in range(ROW + short_w - 1)]
        hs = [few[pl.ds((s * short_w + j) * ROW, ROW), :] for j in range(short_w)]
        res = []
        for b in range(ROW):
            total = hs[0] * xs[b + short_w - 1]
            if masked:
                far_b = bound(0, r0 + b)
                total = jnp.where(far_b >= 0, total, 0.0)
            for j in range(1, short_w):
                x = xs[b + short_w - 1 - j]
                if masked:
                    x = jnp.where(far_b >= j, x, 0.0)
                total = total + hs[j] * x
            res.append(total)
        return res

    lead = long_w

    def before(k, masked):
        i0 = k * ROW
        a = lead_short(s1, 1, i0, far - lead, i0, masked)
        for b in range(ROW):
            put(f1, i0 + b, a[b])
        d = lead_short(s2, 2, i0, far - lead, i0, masked)
        for b in range(ROW):
            put(f2, i0 + b, d[b])
            put(prod, i0 + b, rounded(a[b] * d[b]))

    def after(k, masked):
        i0 = k * ROW
        a = lead_short(s0, 0, i0, pad, i0 + lead, masked)
        for b in range(ROW):
            put(f0, i0 + b, a[b])
            put(back, i0 + b, rounded(tile(go, i0 + b) * a[b]))

    def pick(body, least, k):
        clear = limits[0, least] >= short_w - 1

        @pl.when(clear)
        def _():
            body(k, False)

        @pl.when(jnp.logical_not(clear))
        def _():
            body(k, True)

    count = (lead + seg + tail) // ROW
    lax.fori_loop(0, count, lambda k, _: (pick(before, k, k), 0)[1], 0)
    lax.fori_loop(0, count, lambda k, _: (pick(after, k + lead // ROW, k), 0)[1], 0)
    def differ(dst, ref):
        def step(k, _):
            for b in range(ROW):
                i = k * ROW + b
                x = [tile(ref, i + m) for m in (0, 4, 2, 6)]
                put(dst.at[0], i, x[0] - x[1])
                if LEAF < 4:
                    put(dst.at[1], i, x[0] - x[2])
                    put(dst.at[2], i, (x[0] - x[1]) - (x[2] - x[3]))
            return 0

        ref[pl.ds(count * ROW * ROW, ROW * ROW), :] = jnp.zeros((ROW * ROW, LANES), F32)
        lax.fori_loop(0, count, step, 0)

    differ(prod_less, prod)
    differ(back_less, back)

    def put_parts(ref, i, xs):
        parts = vector_parts(xs)
        for n, key in enumerate(KEYS):
            for m in range(LEAF):
                put(ref, (i * COUNT + n) * LEAF + m, parts[key][m])

    def tap_sums(k, _):
        put_parts(taps_sums, k, [tile(taps, k * ROW + j) for j in range(ROW)])
        return 0

    lax.fori_loop(0, long_w // ROW, tap_sums, 0)

    def products(kind, entry, vec, emit=None):
        res = []
        for buf, start, key, _ in leaves(kind):
            n = KEYS.index(key)
            es = [entry(buf, start + m) for m in range(2 * LEAF - 1)]
            vs = [vec(n * LEAF + m) for m in range(LEAF)]
            for r in range(LEAF):
                total = None
                for m in range(LEAF):
                    at = {0: LEAF - 1 + r - m, 1: LEAF - 1 + m - r, 2: r + m}[kind]
                    term = es[at] * vs[m]
                    total = term if total is None else total + term
                if emit:
                    emit(len(res), total)
                res.append(total)
        return res

    def joined(kind, parts):
        res = [None] * ROW
        for n, (_, _, _, adds) in enumerate(leaves(kind)):
            for r, g in adds:
                for m in range(LEAF):
                    x = parts[n * LEAF + m]
                    at = r + m
                    if res[at] is None:
                        res[at] = x if g > 0 else -x
                    else:
                        res[at] = res[at] + x if g > 0 else res[at] - x
        return res

    def cached(ref, less):
        got = {}

        def entry_at(base):
            def entry(buf, m):
                if (buf, m) not in got:
                    got[buf, m] = tile(ref if buf == 0 else less.at[{1: 0, 2: 1, 3: 2}[buf]], base + m)
                return got[buf, m]
            return entry
        return entry_at

    def derived(xs):
        got = {(0, m): x for m, x in enumerate(xs)}

        def entry(buf, m):
            if (buf, m) not in got:
                low, step = {1: (0, 4), 2: (0, 2), 3: (1, 2)}[buf]
                got[buf, m] = entry(low, m) - entry(low, m + step)
            return got[buf, m]
        return entry

    acc[...] = jnp.zeros_like(acc)
    leaves_l[...] = jnp.zeros_like(leaves_l)
    zero = jnp.zeros((ROW, LANES), F32)

    def long_block(k, own):
        i0 = k * ROW
        if own:
            put_parts(seen, 0, [tile(back, i0 + b) for b in range(ROW)])
        size = COUNT * LEAF

        def before_window(j0):
            xs = [tile(prod, i0 + lead - j0 - ROW + 1 + m) for m in range(2 * ROW - 1)]
            reach = bound(0, i0 + lead) - j0
            return [jnp.where(reach >= ROW - 1 - m, x, 0.0) for m, x in enumerate(xs)]

        def after_window(j0):
            ys = [tile(back, i0 + j0 + m) for m in range(2 * ROW - 1)]
            room = bound(1, i0 + ROW - 1) + (ROW - 1 - j0)
            return [jnp.where(room >= m, y, 0.0) for m, y in enumerate(ys)]

        def ahead(jb, carry, masked):
            j0 = jb * ROW
            entry = derived(before_window(j0)) if masked else cached(prod, prod_less)(i0 + lead - j0 - ROW + 1)
            parts = products(0, entry, lambda n: tile(taps_sums, jb * size + n))
            carry = tuple(c + x for c, x in zip(carry, parts))
            if own:
                def added(n, x):
                    put(leaves_l, jb * size + n, tile(leaves_l, jb * size + n) + x)

                products(1, entry, lambda n: tile(seen, n), added)
            return carry

        def ahead_rows(jb, carry, first):
            j0 = jb * ROW
            reach = [bound(0, i0 + lead + b) - j0 for b in range(ROW)]
            hs = [tile(taps, j0 + j) for j in range(ROW)]
            if first:
                xs = [tile(prod, i0 + lead - j0 - ROW + 1 + m) for m in range(2 * ROW - 1)]
            else:
                xs = before_window(j0)
            total = [zero] * ROW
            if own:
                zs = [tile(back, i0 + b) for b in range(ROW)]
                if not first:
                    zs = [jnp.where(reach[b] >= 0, z, 0.0) for b, z in enumerate(zs)]
                parts = [tile(acc, j0 + j) for j in range(ROW)]
            for j in range(ROW):
                for b in range(ROW):
                    x = xs[b - j + ROW - 1]
                    if first:
                        x = jnp.where(reach[b] >= j, x, 0.0)
                    total[b] = total[b] + hs[j] * x
                    if own:
                        parts[j] = parts[j] + zs[b] * x
            if own:
                for j in range(ROW):
                    put(acc, j0 + j, parts[j])
            if not first:
                total = [jnp.where(reach[b] >= 0, x, 0.0) for b, x in enumerate(total)]
            return tuple(c + x for c, x in zip(carry, total))

        def behind(jb, carry, masked):
            j0 = jb * ROW
            entry = derived(after_window(j0)) if masked else cached(back, back_less)(i0 + j0)
            parts = products(2, entry, lambda n: tile(taps_sums, jb * size + n))
            return tuple(c + x for c, x in zip(carry, parts))

        def behind_rows(jb, carry, first):
            j0 = jb * ROW
            room = [bound(1, i0 + b) - j0 for b in range(ROW)]
            hs = [tile(taps, j0 + j) for j in range(ROW)]
            ys = [tile(back, i0 + j0 + m) for m in range(2 * ROW - 1)] if first else after_window(j0)
            total = [zero] * ROW
            for j in range(ROW):
                for b in range(ROW):
                    y = ys[b + j]
                    if first:
                        y = jnp.where(room[b] >= j, y, 0.0)
                    total[b] = total[b] + hs[j] * y
            if not first:
                total = [jnp.where(room[b] >= 0, x, 0.0) for b, x in enumerate(total)]
            return tuple(c + x for c, x in zip(carry, total))

        even = limits[4, k + lead // ROW] == 1

        def all_of(kind, low, high, at, whole, by_row):
            some = jnp.minimum((limits[high, at] + ROW) // ROW, long_w // ROW)
            full = jnp.where(even, jnp.minimum((limits[low, at] + 1) // ROW, long_w // ROW), 0)
            middle = jnp.where(even, some, 0)
            pairs = jnp.where(even, some, jnp.minimum(some, 1))
            pairs_of = full // 2

            def two_steps(m, c):
                return whole(2 * m + 1, whole(2 * m, c, False), False)

            total = lax.fori_loop(0, pairs_of, two_steps, (zero,) * size)
            total = lax.fori_loop(2 * pairs_of, full, lambda j, c: whole(j, c, False), total)
            total = lax.fori_loop(full, middle, lambda j, c: whole(j, c, True), total)
            total = tuple(joined(kind, total))
            total = lax.fori_loop(middle, pairs, lambda j, c: by_row(j, c, True), total)
            return lax.fori_loop(pairs, some, lambda j, c: by_row(j, c, False), total)

        carry = all_of(0, 0, 1, k + lead // ROW, ahead, ahead_rows)
        grad = all_of(2, 2, 3, k, behind, behind_rows)
        for b in range(ROW):
            put(gf.at[0], i0 + b, rounded(tile(go, i0 + b) * carry[b]))
            put(gf.at[1], i0 + b, rounded(grad[b] * tile(f2, i0 + lead + b)))
            put(gf.at[2], i0 + b, rounded(grad[b] * tile(f1, i0 + lead + b)))
            if own:
                put(car, i0 + b, tile(f0, i0 + b) * carry[b])

    lax.fori_loop(0, seg // ROW, lambda k, _: (long_block(k, True), 0)[1], 0)
    for k in range(seg // ROW, (seg + tail) // ROW):
        long_block(k, False)

    def join_long(k, _):
        got = joined(1, [tile(leaves_l, k * COUNT * LEAF + n) for n in range(COUNT * LEAF)])
        for j in range(ROW):
            put(acc, k * ROW + j, tile(acc, k * ROW + j) + got[j])
        return 0

    lax.fori_loop(0, long_w // ROW, join_long, 0)

    def last(k, carry, s, src, off, masked):
        i0 = k * ROW
        ys = [tile(gf.at[s], i0 + m) for m in range(ROW + short_w - 1)]
        xs = [tile(src, i0 + off - short_w + 1 + m) for m in range(ROW + short_w - 1)]
        hs = [few[pl.ds((s * short_w + j) * ROW, ROW), :] for j in range(short_w)]
        parts = list(carry)
        for b in range(ROW):
            total = None
            if masked:
                room, reach = bound(1, i0 + b), bound(0, i0 + lead + b)
            for j in range(short_w):
                y, x = ys[b + j], xs[b + short_w - 1 - j]
                if masked:
                    y = jnp.where(room >= j, y, 0.0)
                    x = jnp.where(reach >= j, x, 0.0)
                total = hs[j] * y if total is None else total + hs[j] * y
                parts[j] = parts[j] + ys[b] * x
            put(out.at[s], i0 + b, total)
        return tuple(parts)

    for s, src, off in ((0, s0, pad), (1, s1, far), (2, s2, far)):
        def step(k, carry, s=s, src=src, off=off):
            least = jnp.minimum(limits[0, k + lead // ROW], limits[2, k])
            return lax.cond(
                least >= short_w - 1,
                lambda: last(k, carry, s, src, off, False),
                lambda: last(k, carry, s, src, off, True),
            )

        parts = lax.fori_loop(0, seg // ROW, step, (zero,) * short_w)
        for j in range(short_w):
            put(acc, long_w + s * ROW + j, parts[j])

    total_rows = acc.shape[0] // ROW
    for g in range(groups):
        c = slice(g * LANES, (g + 1) * LANES)
        total = None
        for span in range(spans):
            r = span * groups + g
            own = pl.ds(span * seg, seg)
            gated[own, c] = car[pl.ds(r, seg, stride=ROW), :].astype(BF16)
            for s in range(3):
                mixed[s, own, c] = out[s, pl.ds(r, seg, stride=ROW), :].astype(BF16)
            x = acc[pl.ds(r, total_rows, stride=ROW), :]
            total = x if total is None else total + x
        sums[:, c] = total.astype(BF16)


def conv_block(proj, up12, up0, down0, down12, grad_out, short_taps, long_taps, contig_lengths):
    _, rows, chans = proj.shape
    short_w, long_w = short_taps.shape[1], long_taps.shape[0]
    far, pad = up12.shape[1], up0.shape[0]
    groups = chans // LANES
    spans = ROW // groups
    seg, tail = rows // spans, ROW
    lead = long_w

    offset = lax.axis_index("ctx") // 2 * rows
    order = jnp.arange(contig_lengths.shape[0], dtype=jnp.int32)
    ends = jnp.sum(jnp.where(order[None, :] <= order[:, None], contig_lengths[None, :], 0), axis=1)
    begins = ends - contig_lengths
    span = jnp.arange(spans, dtype=jnp.int32) * seg
    count = lead + seg + tail + lead
    at = offset - lead + jnp.arange(count, dtype=jnp.int32)[:, None] + span[None, :]
    first = jnp.max(jnp.where(begins[None, None, :] <= at[:, :, None], begins[None, None, :], 0), axis=2)
    reach = at - first
    here = at[lead : lead + seg + tail]
    end = jnp.min(jnp.where(ends[None, None, :] > here[:, :, None], ends[None, None, :], jnp.int32(2**30)), axis=2)
    room = end - 1 - here

    near = jnp.stack([reach.T, jnp.pad(room.T, ((0, 0), (0, count - room.shape[0])))])

    def blocks(x, how):
        return jnp.pad(how(x.reshape(-1, ROW * spans), axis=1), (0, (count - x.shape[0]) // ROW))

    limits = jnp.stack([
        blocks(reach, jnp.min), blocks(reach, jnp.max), blocks(room, jnp.min), blocks(room, jnp.max),
        jnp.all(reach[ROW - 1 :: ROW] - reach[::ROW] == ROW - 1, axis=1).astype(jnp.int32),
    ])

    def vmem(n):
        return pltpu.VMEM((n * ROW, LANES), F32)

    dims = (rows, far, pad, short_w, long_w, spans, groups, seg, tail)
    size = lead + seg + tail
    in_vmem = pl.BlockSpec(memory_space=pltpu.VMEM)
    return pl.pallas_call(
        lambda *refs: conv_kernel(dims, *refs),
        in_specs=[pl.BlockSpec(memory_space=pltpu.SMEM)] * 2 + [in_vmem] * 6 + [pl.BlockSpec(memory_space=pl.ANY)] * 2,
        out_specs=[in_vmem] * 3,
        out_shape=[
            jax.ShapeDtypeStruct((rows, chans), BF16),
            jax.ShapeDtypeStruct((3, rows, chans), BF16),
            jax.ShapeDtypeStruct((long_w + 4 * ROW, chans), BF16),
        ],
        scratch_shapes=[
            vmem(pad + seg + far), vmem(far + seg + pad), vmem(far + seg + pad), vmem(seg + far),
            vmem(size), vmem(size), vmem(size), vmem(size + ROW), vmem(size + ROW),
            pltpu.VMEM((3, size * ROW, LANES), F32), pltpu.VMEM((3, size * ROW, LANES), F32),
            vmem(long_w // ROW * COUNT * LEAF), vmem(COUNT * LEAF), vmem(seg + tail),
            pltpu.VMEM((3, (seg + 2 * tail) * ROW, LANES), F32),
            vmem(long_w + 4 * ROW), vmem(long_w), vmem(long_w // ROW * COUNT * LEAF), vmem(3 * short_w),
            pltpu.VMEM((3, seg * ROW, LANES), F32),
            pltpu.VMEM((3, short_w, chans), F32), pltpu.VMEM((long_w, chans), F32), pltpu.SemaphoreType.DMA((2,)),
        ],
        compiler_params=pltpu.CompilerParams(vmem_limit_bytes=56 << 20),
        cost_estimate=pl.CostEstimate(
            flops=rows * chans * long_w * 1000, bytes_accessed=rows * chans * 24, transcendentals=0
        ),
        name="hyena_filters",
    )(limits, near, proj, up12, up0, down0, down12, grad_out, short_taps, long_taps)


def deliver(weights, tokens, gated, filters, long_w, short_w):
    streams, feats, chans = weights.shape

    steps = 2
    extra = filters.shape[0] - long_w

    def kernel(w, t, g, f, few, w_out, t_out, g_out, short_out, long_out):
        w_out[...] = w[...]
        t_out[...] = t[...]
        g_out[...] = g[...]
        long_out[...] = f[...]

        @pl.when(pl.program_id(0) == 0)
        def _():
            for s in range(streams):
                short_out[s] = few[pl.ds(ROW * s, short_w), :]

    def rows_of(count, width):
        return pl.BlockSpec((count // steps, width), lambda i: (i, 0))

    part = pl.BlockSpec((streams, feats // steps, chans), lambda i: (0, i, 0))
    short_shape = (streams, short_w, chans)
    parts = [part, rows_of(*tokens.shape), rows_of(*gated.shape)]
    return pl.pallas_call(
        kernel,
        grid=(steps,),
        in_specs=parts + [
            rows_of(long_w, chans), pl.BlockSpec((extra, chans), lambda i: (long_w // extra, 0)),
        ],
        out_specs=parts + [pl.BlockSpec(short_shape, lambda i: (0, 0, 0)), rows_of(long_w, chans)],
        out_shape=[
            jax.ShapeDtypeStruct(weights.shape, BF16),
            jax.ShapeDtypeStruct(tokens.shape, BF16),
            jax.ShapeDtypeStruct(gated.shape, BF16),
            jax.ShapeDtypeStruct(short_shape, F32),
            jax.ShapeDtypeStruct((long_w, chans), F32),
        ],
        compiler_params=pltpu.CompilerParams(vmem_limit_bytes=56 << 20),
        cost_estimate=pl.CostEstimate(flops=0, bytes_accessed=4 * weights.size, transcendentals=0),
        name="deliver",
    )(weights, tokens, gated, filters, filters)


def on_device(loaded, slot_pos, contig_lengths, w_in, short_taps, long_taps, grad_out):
    me = lax.axis_index("ctx")
    core = me % 2
    chans = grad_out.shape[1]
    short_w, long_w = short_taps.shape[1], long_taps.shape[0]
    far, pad = round_up(long_w, 16) + 16, 16
    n_ctx = lax.axis_size("ctx")

    proj, up12, up0, down0, down12, grad_c, wall, *turned = gather(
        jnp.transpose(w_in, (1, 0, 2)), loaded[0], slot_pos, grad_out, far, pad
    )
    turned = [swapped(x, 2 * m) if m else x for m, x in enumerate(turned)]
    gated, grads, sums = conv_block(
        proj, up12, up0, down0, down12, grad_c, short_taps, long_taps, contig_lengths
    )
    results = reduce(grads, wall, gated, sums, turned)
    weight_grads, token_grads, gated_out, short_total, long_total = deliver(*results, long_w, short_w)
    return gated_out, token_grads, jnp.transpose(weight_grads, (1, 0, 2)), short_total, long_total


def solution(mesh):
    in_specs = (
        P("ctx", None, None, "fsdp"),
        P("ctx", None, None),
        P(),
        P("ctx", None, "fsdp"),
        P(None, None, "fsdp"),
        P(None, "fsdp"),
        P("ctx", "fsdp"),
    )
    out_specs = (
        P("ctx", "fsdp"),
        P("ctx", "fsdp"),
        P("ctx", None, "fsdp"),
        P(None, None, "fsdp"),
        P(None, "fsdp"),
    )
    return jax.shard_map(
        on_device, mesh=mesh, in_specs=in_specs, out_specs=out_specs, check_vma=False
    )
```
